32 devices in a mesh: pts: 4 (over y, core), grid: 8 (over z, x).
Axes of the slice: x: 2, y: 2, z: 4, core: 2. Of those that a mesh axis runs over, the one named last changes fastest.
Arguments:
- features: bfloat16 [32, 524288], P(None, ('pts', 'grid')), may hold values from -6 to 6
- w_in: bfloat16 [32, 64], replicated, may hold values from -1 to 1
- w_mid: bfloat16 [64, 64], replicated, may hold values from -0.75 to 0.75
- w_conv: bfloat16 [2, 3, 3, 3, 64, 64], replicated, may hold values from -0.15625 to 0.15625
- point_frac: float32 [3, 524288], P(None, ('pts', 'grid')), may hold values from 0 to 1
- point_base: int32 [3, 524288], P(None, ('pts', 'grid')), may hold values from 0 to 6, as said below
- slot_dest: int32 [2048], P(('pts', 'grid')), may hold values from 0 to 7, as said below
- slot_tile_block: int32 [2048], P(('pts', 'grid')), may hold values from 0 to 63
- slot_count: int32 [2048], P(('pts', 'grid')), may hold values from 1 to 256, as said below
Outputs:
- point_out: bfloat16 [64, 524288], P(None, ('pts', 'grid'))
The draws below stay inside these ranges and needn't reach their ends.
Inputs may be any that keep to these rules, and one draw needn't show every extreme that they name: `point_base`: the three rows give base cells along the first, second and third dimension; the first two rows lie in 0 .. 2 and the third in 0 .. 6, so all eight corners of a point lie in its block. `slot_dest`: among the 64 slots of one device at most 16 name the same value; on every device one value is named by exactly 16 slots, the same value on all devices of one index along pts. `slot_count`: every device has a slot with exactly 256 live points.
All inputs are finite; a program needn't handle non-finite values.
Results may differ from the reference program's by a relative error of at most 0.0035.
The reference program's roundings to bfloat16 on the way count: a program that leaves them out, or rounds other values in their place, can miss the bound.
Values may be sent and summed in bfloat16 or wider, within the bound.
A program may use at most 128 MiB of HBM per device.

```python
import jax
import jax.numpy as jnp
from jax import lax

CIN = 32
HID = 64
GZ = 8
BLOCK_EDGE_CELLS = 4
LAYERS = 2
TX = 32
TY = 32
DEVICE_SLOTS = 64
CAP = 256
CAPB = 16
NXG = 256
NYG = 128
SLOT_COUNT_ALL = 2048
NPT = 524288
TILE_BLOCK_COUNT = 64
N_PTS = 4
N_GRID = 8


def draw_point_base(key, part):
    first_two = jax.random.randint(jax.random.fold_in(key, 1), (2, NPT), 0, BLOCK_EDGE_CELLS - 1)
    third_row = jax.random.randint(jax.random.fold_in(key, 2), (1, NPT), 0, GZ - 1)
    return jnp.concatenate([first_two, third_row], axis=0).astype(jnp.int32)


def draw_slot_dest(key, part):
    devices = N_PTS * N_GRID
    hot_row = jax.random.randint(jax.random.fold_in(key, 3), (N_PTS,), 0, N_GRID)
    hot_owner = jnp.repeat(hot_row, N_GRID)
    spare_total = (N_GRID - 1) * CAPB

    def one_device(device_key, owner):
        pool_values = jnp.arange(spare_total, dtype=jnp.int32) // CAPB
        pool_values = pool_values + (pool_values >= owner).astype(jnp.int32)
        picked = jax.random.permutation(jax.random.fold_in(device_key, 1), pool_values)[:DEVICE_SLOTS - CAPB]
        whole_list = jnp.concatenate([jnp.full((CAPB,), owner, jnp.int32), picked.astype(jnp.int32)])
        return jax.random.permutation(jax.random.fold_in(device_key, 2), whole_list)
    device_keys = jax.random.split(jax.random.fold_in(key, 4), devices)
    return jax.vmap(one_device)(device_keys, hot_owner).reshape(-1).astype(jnp.int32)


def draw_slot_count(key, part):
    devices = N_PTS * N_GRID
    counts = jax.random.randint(jax.random.fold_in(key, 5), (devices, DEVICE_SLOTS), 1, CAP + 1)
    full_at = jax.random.randint(jax.random.fold_in(key, 6), (devices, 1), 0, DEVICE_SLOTS)
    counts = jnp.where(jnp.arange(DEVICE_SLOTS, dtype=jnp.int32)[None, :] == full_at, CAP, counts)
    return counts.reshape(-1).astype(jnp.int32)


def set_ends(result, own_key, low, high):
    longest = result.shape.index(max(result.shape))
    spots = []
    for shift in (0, 1):
        where = [jax.random.randint(jax.random.fold_in(own_key, axis), (), 0, length) for axis, length in enumerate(result.shape)]
        where[longest] = (where[longest] + shift) % result.shape[longest]
        spots.append(tuple(where))
    return result.at[spots[0]].set(low).at[spots[1]].set(high)


def block_levels(stream_key, dims, cuts, smallest, top_value):
    level, own = 1.0, jax.random.fold_in(stream_key, 6)
    for position, shards_of in cuts:
        steps = jnp.exp(jax.random.uniform(jax.random.fold_in(own, position), (shards_of,), jnp.float32, smallest / len(cuts), top_value / len(cuts)))
        level = level * jnp.repeat(steps, dims[position] // shards_of).reshape([-1 if axis == position else 1 for axis in range(len(dims))])
    return level


def gaussian(key, extent, scale, limit, cuts=(), kind=jnp.bfloat16):
    entries = jax.random.normal(key, extent, jnp.float32) * scale
    if len(cuts) > 0:
        entries = block_levels(key, extent, cuts, -0.22, 0.18) * entries
    return jnp.clip(entries, min=-limit, max=limit).astype(kind)


def setup_inputs(seed: int = 0) -> dict:
    arg_keys = jax.random.split(jax.random.key(seed), 10)
    features = gaussian(arg_keys[0], (CIN, NPT), 1.0, 6.0, ((1, 32),))
    w_in = gaussian(arg_keys[1], (CIN, HID), CIN ** -0.5, 1.0)
    w_mid = gaussian(arg_keys[2], (HID, HID), HID ** -0.5, 0.75)
    w_conv = gaussian(arg_keys[3], (LAYERS, 3, 3, 3, HID, HID), (27 * HID) ** -0.5, 0.15625)
    point_frac = jnp.clip(1.0 * jax.random.uniform(arg_keys[4], (3, NPT), jnp.float32) ** block_levels(arg_keys[4], (3, NPT), ((1, 32),), -0.2, 0.2), 0.0, 1.0)
    point_base = draw_point_base(jax.random.fold_in(arg_keys[9], 71), 0)
    slot_dest = draw_slot_dest(jax.random.fold_in(arg_keys[9], 71), 0)
    slot_tile_block = set_ends(jax.random.randint(arg_keys[7], (SLOT_COUNT_ALL,), 0, TILE_BLOCK_COUNT), jax.random.fold_in(arg_keys[7], 1), 0, TILE_BLOCK_COUNT - 1).astype(jnp.int32)
    slot_count = draw_slot_count(jax.random.fold_in(arg_keys[9], 71), 0)
    return {"features": features, "w_in": w_in, "w_mid": w_mid, "w_conv": w_conv, "point_frac": point_frac, "point_base": point_base, "slot_dest": slot_dest, "slot_tile_block": slot_tile_block, "slot_count": slot_count}


def axis_weights(offset, corner, length):
    positions = jnp.arange(length, dtype=jnp.int32)[:, None, None]
    below_part = jnp.where(positions == corner[None], 1.0 - offset[None], 0.0)
    above_part = jnp.where(positions == corner[None] + 1, offset[None], 0.0)
    return below_part + above_part


def trilinear(offsets, corners, counts, block_edge, grid_depth):
    slot_width = offsets.shape[2]
    live_mask = (jnp.arange(slot_width, dtype=jnp.int32)[None, :] < counts[:, None]).astype(jnp.float32)
    along_x = axis_weights(offsets[0], corners[0], block_edge)
    along_y = axis_weights(offsets[1], corners[1], block_edge)
    along_z = axis_weights(offsets[2], corners[2], grid_depth)
    corner_weights = along_x[:, None, None] * along_y[None, :, None] * along_z[None, None, :] * live_mask
    return corner_weights.reshape(block_edge * block_edge, grid_depth, offsets.shape[1], slot_width).astype(jnp.bfloat16)


def point_layer(weight, inputs):
    mixed_sum = jnp.dot(weight.T, inputs, preferred_element_type=jnp.float32)
    return jax.nn.silu(mixed_sum).astype(jnp.bfloat16)


def banded_weights(kernel, grid_depth):
    depth_range = jnp.arange(grid_depth, dtype=jnp.int32)
    shifts = (depth_range[None, :, None] == depth_range[None, None, :] + jnp.arange(3, dtype=jnp.int32)[:, None, None] - 1).astype(jnp.float32)
    banded = jnp.einsum("kab,xykij->xyaibj", shifts, kernel.astype(jnp.float32))
    return banded.astype(jnp.bfloat16).reshape(3, 3, grid_depth * kernel.shape[3], grid_depth * kernel.shape[4])


def reference(features, w_in, w_mid, w_conv, point_frac, point_base, slot_dest, slot_tile_block, slot_count):
    devices = N_PTS * N_GRID
    per_device = DEVICE_SLOTS * CAP
    every_channel = GZ * HID
    feats_dev = features.reshape(CIN, devices, per_device).transpose(1, 0, 2)
    frac_dev = point_frac.reshape(3, devices, DEVICE_SLOTS, CAP).transpose(1, 0, 2, 3)
    base_dev = point_base.reshape(3, devices, DEVICE_SLOTS, CAP).transpose(1, 0, 2, 3)
    count_dev = slot_count.reshape(devices, DEVICE_SLOTS)

    def local_part(feats, offsets, corners, counts):
        hidden_two = point_layer(w_mid, point_layer(w_in, feats)).reshape(HID, DEVICE_SLOTS, CAP)
        weights = trilinear(offsets, corners, counts, BLOCK_EDGE_CELLS, GZ)
        return hidden_two, weights

    def splat_part(packed):
        hidden_two, weights = local_part(*packed)
        sums = jnp.einsum("czsp,hsp->sczh", weights.astype(jnp.float32), hidden_two.astype(jnp.float32))
        return sums.astype(jnp.bfloat16).reshape(DEVICE_SLOTS, BLOCK_EDGE_CELLS * BLOCK_EDGE_CELLS * every_channel)

    partial_sums = lax.map(splat_part, (feats_dev, frac_dev, base_dev, count_dev))
    nbx_local = TX // BLOCK_EDGE_CELLS
    nby_local = TY // BLOCK_EDGE_CELLS
    blocks_along_first = nbx_local * N_GRID
    blocks_along_second = nby_local * N_PTS
    slot_owner_device = jnp.arange(SLOT_COUNT_ALL, dtype=jnp.int32) // DEVICE_SLOTS
    row_pts = slot_owner_device // N_GRID
    block_x = slot_dest * nbx_local + slot_tile_block // nby_local
    block_y = row_pts * nby_local + slot_tile_block % nby_local
    block_number = (block_x * blocks_along_second + block_y).astype(jnp.int32)
    summed_blocks = jax.ops.segment_sum(partial_sums.reshape(SLOT_COUNT_ALL, BLOCK_EDGE_CELLS * BLOCK_EDGE_CELLS * every_channel).astype(jnp.float32), block_number, num_segments=blocks_along_first * blocks_along_second)
    grid = summed_blocks.astype(jnp.bfloat16).reshape(blocks_along_first, blocks_along_second, BLOCK_EDGE_CELLS, BLOCK_EDGE_CELLS, every_channel)
    grid = grid.transpose(0, 2, 1, 3, 4).reshape(NXG, NYG, every_channel)
    for layer_index in range(LAYERS):
        banded = banded_weights(w_conv[layer_index], GZ).astype(jnp.float32)
        padded = jnp.pad(grid, ((1, 1), (1, 1), (0, 0))).astype(jnp.float32)
        total_sum = jnp.zeros((NXG, NYG, every_channel), jnp.float32)
        for shift_x in range(3):
            for shift_y in range(3):
                window = padded[shift_x:shift_x + NXG, shift_y:shift_y + NYG]
                total_sum = total_sum + jnp.einsum("xyi,ij->xyj", window, banded[shift_x, shift_y])
        grid = jax.nn.silu(total_sum).astype(jnp.bfloat16)
    blocks = grid.reshape(blocks_along_first, BLOCK_EDGE_CELLS, blocks_along_second, BLOCK_EDGE_CELLS, every_channel).transpose(0, 2, 1, 3, 4)
    blocks = blocks.reshape(blocks_along_first * blocks_along_second, BLOCK_EDGE_CELLS * BLOCK_EDGE_CELLS, every_channel)
    slot_cells = blocks[block_number].reshape(devices, DEVICE_SLOTS, BLOCK_EDGE_CELLS * BLOCK_EDGE_CELLS, GZ, HID)

    def finish_part(packed):
        feats, offsets, corners, counts, cells = packed
        hidden_two, weights = local_part(feats, offsets, corners, counts)
        interp = jnp.einsum("czsp,sczh->hsp", weights.astype(jnp.float32), cells.astype(jnp.float32)).astype(jnp.bfloat16)
        point_out = (hidden_two.astype(jnp.float32) + interp.astype(jnp.float32)).astype(jnp.bfloat16)
        return point_out.reshape(HID, per_device)

    results = lax.map(finish_part, (feats_dev, frac_dev, base_dev, count_dev, slot_cells))
    return results.transpose(1, 0, 2).reshape(HID, NPT)
```

```python
import functools

import jax
import jax.numpy as jnp
from jax import lax
from jax.experimental import pallas as pl
from jax.experimental.pallas import tpu as pltpu
from jax.sharding import PartitionSpec as P

GZ = 8
EDGE = 4
TX = 32
TY = 32
LANES = 128
PAIR = 2
Z = GZ // PAIR
MESH = pl.DeviceIdType.MESH
DIRECTIONS = ((0, 1), (0, -1), (1, 0), (-1, 0), (1, 1), (1, -1), (-1, 1), (-1, -1))
ORDER = (3, 0, 1, 2)
OUT_ORDER = (0, 3, 1, 2)


def point_layer(weight, inputs):
    mixed_sum = lax.dot_general(
        weight, inputs, (((0,), (0,)), ((), ())), preferred_element_type=jnp.float32
    )
    return jax.nn.silu(mixed_sum).astype(jnp.bfloat16)


def axis_weights(offset, corner, positions):
    positions = positions[:, None, None]
    below_part = jnp.where(positions == corner[None], 1.0 - offset[None], 0.0)
    above_part = jnp.where(positions == corner[None] + 1, offset[None], 0.0)
    return below_part + above_part


def trilinear(offsets, corners, counts, block_edge, grid_depth):
    slot_width = offsets.shape[2]
    live_mask = (jnp.arange(slot_width, dtype=jnp.int32)[None, :] < counts[:, None]).astype(
        jnp.float32
    )
    cells = jnp.arange(block_edge * block_edge, dtype=jnp.int32)
    along_x = axis_weights(offsets[0], corners[0], cells // block_edge)
    along_y = axis_weights(offsets[1], corners[1], cells % block_edge)
    along_z = axis_weights(offsets[2], corners[2], jnp.arange(grid_depth, dtype=jnp.int32))
    corner_weights = (along_x * along_y)[:, None] * along_z[None] * live_mask
    return corner_weights.astype(jnp.bfloat16)


def splat(weights, hidden):
    sums = jnp.einsum("czsp,hsp->sczh", weights, hidden, preferred_element_type=jnp.float32)
    slots, channels = sums.shape[0], sums.shape[3]
    sums = sums.astype(jnp.bfloat16)
    sums = sums.reshape(slots, EDGE, EDGE // PAIR, PAIR, Z, PAIR, channels)
    sums = sums.transpose(4, 1, 0, 2, 5, 3, 6)
    return sums.reshape(Z, EDGE, slots, EDGE * PAIR * channels)


def interpolate(weights, blocks):
    slots, channels = blocks.shape[2], blocks.shape[3] // (EDGE * PAIR)
    cells = blocks.reshape(Z, EDGE, slots, EDGE // PAIR, PAIR, PAIR, channels)
    cells = cells.transpose(2, 1, 3, 5, 0, 4, 6).reshape(slots, EDGE * EDGE, GZ, channels)
    return jnp.einsum("czsp,sczh->hsp", weights, cells, preferred_element_type=jnp.float32).astype(
        jnp.bfloat16
    )


def build_band(w_ref, band_ref):
    channels = w_ref.shape[1]
    width = PAIR * channels

    def one(n, carry):
        layer, a = lax.div(n, 3), lax.rem(n, 3)
        band_ref[layer, :, a] = jnp.zeros(band_ref.shape[1:2] + band_ref.shape[3:], band_ref.dtype)
        for zl in range(2 + PAIR):
            part, slot = (0, zl - 1) if 1 <= zl <= PAIR else (1, 0 if zl == 0 else 1)
            for zz in range(PAIR):
                e = zl - zz
                if not 0 <= e <= 2:
                    continue
                for source, row in ((0, 0), (1, 1), (2, 2), (-1, 3)):
                    for target in range(PAIR):
                        b = source - target + 1
                        if not 0 <= b <= 2:
                            continue
                        rows = slice(row * channels, (row + 1) * channels)
                        lanes = zz * width + target * channels
                        band_ref[layer, part, a, slot, rows, lanes : lanes + channels] = w_ref[
                            n * 9 + b * 3 + e
                        ]
        return carry

    lax.fori_loop(0, band_ref.shape[0] * 3, one, 0)


def conv_kernel(
    sizes,
    ids_ref,
    sums_ref,
    w_ref,
    out_ref,
    ids,
    arrived,
    field,
    band_ref,
    totals,
    sum_picks,
    out_picks,
    dense,
    values,
    id_send,
    id_recv,
    z_send,
    z_recv,
    x_send,
    x_recv,
    halo_send,
    halo_recv,
    rx_send,
    rx_recv,
    rz_send,
    rz_recv,
):
    rows, columns = sizes
    strips = rows // Z
    blocks = dense.shape[2]
    slots = ids.shape[1]
    span = (field.shape[4] - blocks) // 2
    layers = field.shape[0]
    me_row, me_column = lax.axis_index("grid"), lax.axis_index("pts")
    me_z, me_x = lax.div(me_row, strips), lax.rem(me_row, strips)
    inner = pl.ds(span, blocks)

    def place(dz, ds):
        strip = me_column * strips + me_x + ds
        z = me_z + dz
        present = (strip >= 0) & (strip < columns * strips) & (z >= 0) & (z < Z)
        column = lax.div(strip + strips, strips) - 1
        return present, column, z * strips + lax.rem(strip + strips, strips)

    def tell(t):
        return pltpu.make_async_remote_copy(
            src_ref=ids_ref,
            dst_ref=ids.at[me_row],
            send_sem=id_send.at[t],
            recv_sem=id_recv.at[t],
            device_id=(me_column, lax.rem(me_row + t, rows)),
            device_id_type=MESH,
        )

    def along_z(i, t):
        z = lax.rem(me_z + t, Z)
        return pltpu.make_async_remote_copy(
            src_ref=sums_ref.at[z, i],
            dst_ref=arrived.at[i, me_row],
            send_sem=z_send.at[i, t],
            recv_sem=z_recv.at[i, t],
            device_id=(me_column, z * strips + me_x),
            device_id_type=MESH,
        )

    def along_x(i, t, u):
        origin = lax.rem(me_z - t + Z, Z) * strips + me_x
        return pltpu.make_async_remote_copy(
            src_ref=sums_ref.at[me_z, i] if t == 0 else arrived.at[i, origin],
            dst_ref=arrived.at[i, origin],
            send_sem=x_send.at[i, t, u],
            recv_sem=x_recv.at[i, t, u],
            device_id=(me_column, me_z * strips + lax.rem(me_x + u, strips)),
            device_id_type=MESH,
        )

    def halo(layer, i, k):
        dz, ds = DIRECTIONS[k]
        _, column, row = place(dz, ds)
        pairs = slice(0, PAIR) if ds == 0 else slice(1, 2) if ds > 0 else slice(0, 1)
        source_z = slice(1, 3) if dz == 0 else slice(2, 3) if dz > 0 else slice(1, 2)
        target_z = slice(1, 3) if dz == 0 else slice(0, 1) if dz > 0 else slice(3, 4)
        if ds == 0:
            source_rows = target_rows = slice(span, span + blocks)
        elif ds > 0:
            source_rows, target_rows = slice(blocks, blocks + span), slice(0, span)
        else:
            source_rows = slice(span, 2 * span)
            target_rows = slice(span + blocks, 2 * span + blocks)
        return pltpu.make_async_remote_copy(
            src_ref=field.at[layer, i + 1, pairs, source_z, source_rows],
            dst_ref=field.at[layer, i + 1, pairs, target_z, target_rows],
            send_sem=halo_send.at[layer, i, k],
            recv_sem=halo_recv.at[layer, i, k],
            device_id=(column, row),
            device_id_type=MESH,
        )

    def back_x(i, u):
        return pltpu.make_async_remote_copy(
            src_ref=dense.at[i, me_x],
            dst_ref=dense.at[i, me_x],
            send_sem=rx_send.at[i, u],
            recv_sem=rx_recv.at[i, u],
            device_id=(me_column, me_z * strips + lax.rem(me_x + u, strips)),
            device_id_type=MESH,
        )

    def back_z(i, t):
        z = lax.rem(me_z + t, Z)
        return pltpu.make_async_remote_copy(
            src_ref=values.at[i, z],
            dst_ref=out_ref.at[me_z, i],
            send_sem=rz_send.at[i, t],
            recv_sem=rz_recv.at[i, t],
            device_id=(me_column, z * strips + me_x),
            device_id_type=MESH,
        )

    def send_halos(layer, i):
        for k, (dz, ds) in enumerate(DIRECTIONS):
            present, _, _ = place(dz, ds)

            @pl.when(present)
            def _():
                halo(layer, i, k).start()

    def wait_halos(layer, i, ks):
        for k in ks:
            dz, ds = DIRECTIONS[k]
            present, _, _ = place(-dz, -ds)

            @pl.when(present)
            def _():
                halo(layer, i, k).wait_recv()

    barrier = pltpu.get_barrier_semaphore()
    for t in range(1, rows):
        pl.semaphore_signal(
            barrier,
            inc=1,
            device_id=(me_column, lax.rem(me_row + t, rows)),
            device_id_type=MESH,
        )
    expected = rows - 1
    for dz in (-1, 0, 1):
        for ds in (-1, 1):
            present, column, row = place(dz, ds)
            other = present & (column != me_column)
            expected = expected + other.astype(jnp.int32)

            @pl.when(other)
            def _():
                pl.semaphore_signal(barrier, inc=1, device_id=(column, row), device_id_type=MESH)

    pl.semaphore_wait(barrier, expected)

    for t in range(1, rows):
        tell(t).start()
    for i in ORDER:
        for t in (2, 1, 3):
            along_z(i, t).start()
        for u in range(1, strips):
            along_x(i, 0, u).start()
    for i in ORDER:
        arrived[i, me_row] = sums_ref[me_z, i]
    ids[me_row] = ids_ref[...]
    for k, (dz, ds) in enumerate(DIRECTIONS):
        present, _, _ = place(-dz, -ds)

        @pl.when(jnp.logical_not(present))
        def _():
            target_z = slice(1, 3) if dz == 0 else slice(0, 1) if dz > 0 else slice(3, 4)
            pairs = slice(0, PAIR) if ds == 0 else slice(1, 2) if ds > 0 else slice(0, 1)
            low, high = (
                (span, span + blocks)
                if ds == 0
                else (0, span)
                if ds > 0
                else (span + blocks, 2 * span + blocks)
            )
            for layer in range(layers):
                view = field.at[layer, 1 : EDGE + 1, pairs, target_z, low:high]
                view[...] = jnp.zeros(view.shape, field.dtype)

    build_band(w_ref, band_ref)
    for t in range(1, rows):
        tell(t).wait_recv()

    def picks(named, first, width):
        parts = []
        for low in range(0, width, LANES):
            place_of = lax.broadcasted_iota(jnp.int32, named.shape, 1) + (low + first)
            parts.append(jnp.where(named == place_of, 1.0, 0.0))
        return jnp.concatenate(parts, axis=1)

    for r in range(rows):
        one_hot = picks(ids[r], me_x * blocks, blocks)
        sum_picks[:, r * slots : (r + 1) * slots] = one_hot.T.astype(jnp.bfloat16)
    for z in range(Z):
        out_picks[z * slots : (z + 1) * slots] = picks(
            ids[z * strips + me_x], 0, strips * blocks
        ).astype(jnp.bfloat16)

    def forward(i):
        for t in (1, 2, 3):
            along_z(i, t).wait_recv()
            for u in range(1, strips):
                along_x(i, t, u).start()

    def spread(layer, i, tiles):
        for jp in range(PAIR):
            for zz in range(PAIR):
                field[layer, i + 1, jp, 1 + zz, inner] = tiles(jp, zz)
        send_halos(layer, i)

    def gather(i):
        for t in range(Z):
            for u in range(1, strips):
                along_x(i, t, u).wait_recv()
        summed = jnp.dot(
            sum_picks[...],
            arrived[i].reshape(rows * slots, arrived.shape[3]),
            preferred_element_type=jnp.float32,
        ).astype(jnp.bfloat16)

        def tiles(jp, zz):
            low = (jp * PAIR + zz) * LANES
            return summed[:, low : low + LANES]

        spread(0, i, tiles)

    for n, i in enumerate(ORDER):
        forward(i)
        if n > 0:
            gather(ORDER[n - 1])
    gather(ORDER[-1])

    low_half = lax.broadcasted_iota(jnp.int32, (blocks, LANES), 1) < LANES // PAIR

    def shift(layer, down, levels):
        source, target = (EDGE, 0) if down else (1, EDGE + 1)
        for jp in range(PAIR):
            low = 0 if jp == 1 else span
            size = blocks + span
            ranks = lax.broadcasted_iota(jnp.int32, (size, LANES), 0)
            edge_rank = 0 if down else span - 1
            keep = lax.rem(ranks, span) != edge_rank
            for zl in levels:
                moved = pltpu.roll(
                    field[layer, source, jp, zl, low : low + size].astype(jnp.float32),
                    1 if down else size - 1,
                    0,
                )
                field[layer, target, jp, zl, low : low + size] = jnp.where(
                    keep, moved, 0.0
                ).astype(jnp.bfloat16)

    def windows(layer, i, jp, levels):
        parts = []
        for a in range(3):
            for zl in levels:
                here = field.at[layer, i + a, :, zl]
                parts.append(here[jp, inner])
                if jp == 0:
                    up, down = here[1, inner], here[1, 0:blocks]
                else:
                    up, down = here[0, 2 * span : 2 * span + blocks], here[0, inner]
                parts.append(jnp.where(low_half, up, down))
        return jnp.concatenate(parts, axis=1)

    def conv_terms(layer, i, part):
        levels = (1, 2) if part == 0 else (0, 3)
        weight = band_ref[layer, part].reshape(-1, band_ref.shape[5])
        lhs = jnp.concatenate([windows(layer, i, jp, levels) for jp in range(PAIR)], axis=0)
        return jnp.dot(lhs, weight, preferred_element_type=jnp.float32)

    beside = [k for k, (dz, _) in enumerate(DIRECTIONS) if dz == 0]
    across = [k for k, (dz, _) in enumerate(DIRECTIONS) if dz != 0]
    for layer in range(layers):
        before = ORDER if layer == 0 else OUT_ORDER
        for i in before:
            wait_halos(layer, i, beside)
        shift(layer, True, (1, 2))
        shift(layer, False, (1, 2))
        for i in OUT_ORDER:
            totals[i] = conv_terms(layer, i, 0)
        waited = set()
        for i in OUT_ORDER:
            needed = {(i - 1) % EDGE, i, (i + 1) % EDGE}
            for phase in before:
                if phase in needed and phase not in waited:
                    wait_halos(layer, phase, across)
                    waited.add(phase)
                    if phase == EDGE - 1:
                        shift(layer, True, (0, 3))
                    if phase == 0:
                        shift(layer, False, (0, 3))
            total = totals[i] + conv_terms(layer, i, 1)
            activated = (total / (1.0 + jnp.exp(-total))).astype(jnp.bfloat16)

            def tiles(jp, zz):
                return activated[
                    jp * blocks : (jp + 1) * blocks, zz * LANES : (zz + 1) * LANES
                ]

            if layer < layers - 1:
                spread(layer + 1, i, tiles)
            else:
                for jp in range(PAIR):
                    for zz in range(PAIR):
                        low = (jp * PAIR + zz) * LANES
                        dense[i, me_x, :, low : low + LANES] = tiles(jp, zz)
                for u in range(1, strips):
                    back_x(i, u).start()

    for i in OUT_ORDER:
        for u in range(1, strips):
            back_x(i, u).wait_recv()
        picked = jnp.dot(
            out_picks[...],
            dense[i].reshape(strips * blocks, dense.shape[3]),
            preferred_element_type=jnp.float32,
        ).astype(jnp.bfloat16)
        values[i] = picked.reshape(values.shape[1:])
        for t in (2, 1, 3):
            back_z(i, t).start()
        out_ref[me_z, i] = values[i, me_z]

    for t in range(1, rows):
        tell(t).wait_send()
    for i in range(EDGE):
        for t in (1, 2, 3):
            back_z(i, t).wait_recv()
            back_z(i, t).wait_send()
            along_z(i, t).wait_send()
        for u in range(1, strips):
            back_x(i, u).wait_send()
            for t in range(Z):
                along_x(i, t, u).wait_send()
        for layer in range(layers):
            for k, (dz, ds) in enumerate(DIRECTIONS):
                present, _, _ = place(dz, ds)

                @pl.when(present)
                def _():
                    halo(layer, i, k).wait_send()


def exchange_and_convolve(ids, sums, w_conv):
    rows, columns = lax.axis_size("grid"), lax.axis_size("pts")
    strips = rows // Z
    slots, width = sums.shape[2:]
    layers, channels = w_conv.shape[0], w_conv.shape[4]
    span = rows * (TX // EDGE)
    blocks = span * (TY // EDGE) // strips
    halos = (layers, EDGE, len(DIRECTIONS))
    dma = pltpu.SemaphoreType.DMA
    return pl.pallas_call(
        functools.partial(conv_kernel, (rows, columns)),
        out_shape=jax.ShapeDtypeStruct(sums.shape, jnp.bfloat16),
        in_specs=[pl.BlockSpec(memory_space=pltpu.VMEM)] * 3,
        out_specs=pl.BlockSpec(memory_space=pltpu.VMEM),
        scratch_shapes=[
            pltpu.VMEM((rows, slots, LANES), jnp.int32),
            pltpu.VMEM((EDGE, rows, slots, width), jnp.bfloat16),
            pltpu.VMEM((layers, EDGE + 2, PAIR, PAIR + 2, blocks + 2 * span, LANES), jnp.bfloat16),
            pltpu.VMEM((layers, 2, 3, 2, 2 * LANES, 2 * LANES), jnp.bfloat16),
            pltpu.VMEM((EDGE, PAIR * blocks, 2 * LANES), jnp.float32),
            pltpu.VMEM((blocks, rows * slots), jnp.bfloat16),
            pltpu.VMEM((Z * slots, strips * blocks), jnp.bfloat16),
            pltpu.VMEM((EDGE, strips, blocks, width), jnp.bfloat16),
            pltpu.VMEM((EDGE, Z, slots, width), jnp.bfloat16),
            dma((rows,)),
            dma((rows,)),
            dma((EDGE, Z)),
            dma((EDGE, Z)),
            dma((EDGE, Z, strips)),
            dma((EDGE, Z, strips)),
            dma(halos),
            dma(halos),
            dma((EDGE, strips)),
            dma((EDGE, strips)),
            dma((EDGE, Z)),
            dma((EDGE, Z)),
        ],
        compiler_params=pltpu.CompilerParams(collective_id=0, has_side_effects=True),
    )(ids, sums, w_conv.reshape(layers * 27, channels, channels))


def per_device(
    features, w_in, w_mid, w_conv, point_frac, point_base, slot_dest, slot_tile_block, slot_count
):
    slot_total = slot_dest.shape[0]
    slot_width = features.shape[1] // slot_total
    span = lax.axis_size("grid") * (TX // EDGE)
    along, across = TX // EDGE, TY // EDGE
    hidden_one = point_layer(w_in, features)
    hidden_two = point_layer(w_mid, hidden_one)
    channels = hidden_two.shape[0]
    hidden_two = hidden_two.reshape(channels, slot_total, slot_width)
    offsets, corners = lax.optimization_barrier(
        (
            point_frac.reshape(3, slot_total, slot_width),
            point_base.reshape(3, slot_total, slot_width),
        )
    )
    block_x = slot_dest * along + slot_tile_block // across
    block_y = slot_tile_block % across
    ids = jnp.broadcast_to((block_y * span + block_x)[:, None], (slot_total, LANES))
    weights = trilinear(offsets, corners, slot_count, EDGE, GZ)
    local_sums = splat(weights, hidden_two)
    blocks = exchange_and_convolve(ids, local_sums, w_conv)
    interp = interpolate(weights, blocks)
    point_out = (hidden_two.astype(jnp.float32) + interp.astype(jnp.float32)).astype(jnp.bfloat16)
    return point_out.reshape(channels, slot_total * slot_width)


def solution(mesh):
    return jax.shard_map(
        per_device,
        mesh=mesh,
        in_specs=(
            P(None, ("pts", "grid")),
            P(),
            P(),
            P(),
            P(None, ("pts", "grid")),
            P(None, ("pts", "grid")),
            P(("pts", "grid")),
            P(("pts", "grid")),
            P(("pts", "grid")),
        ),
        out_specs=P(None, ("pts", "grid")),
        check_vma=False,
    )
```

```python
import functools

import jax
import jax.numpy as jnp
from jax import lax
from jax.experimental import pallas as pl
from jax.experimental.pallas import tpu as pltpu
from jax.sharding import PartitionSpec as P

GZ = 8
EDGE = 4
TX = 32
TY = 32
LANES = 128
PAIR = 2
Z = GZ // PAIR
MESH = pl.DeviceIdType.MESH
LEVELS = ((1, 2), (0, 3))
ORDER = (3, 0, 1, 2)
OUT_ORDER = (0, 3, 1, 2)


def point_layer(weight, inputs):
    mixed_sum = lax.dot_general(
        weight, inputs, (((0,), (0,)), ((), ())), preferred_element_type=jnp.float32
    )
    return jax.nn.silu(mixed_sum).astype(jnp.bfloat16)


def axis_weights(offset, corner, positions):
    positions = positions[:, None, None]
    below_part = jnp.where(positions == corner[None], 1.0 - offset[None], 0.0)
    above_part = jnp.where(positions == corner[None] + 1, offset[None], 0.0)
    return below_part + above_part


def trilinear(offsets, corners, counts, block_edge, grid_depth):
    slot_width = offsets.shape[2]
    live_mask = (jnp.arange(slot_width, dtype=jnp.int32)[None, :] < counts[:, None]).astype(
        jnp.float32
    )
    cells = jnp.arange(block_edge * block_edge, dtype=jnp.int32)
    along_x = axis_weights(offsets[0], corners[0], cells // block_edge)
    along_y = axis_weights(offsets[1], corners[1], cells % block_edge)
    along_z = axis_weights(offsets[2], corners[2], jnp.arange(grid_depth, dtype=jnp.int32))
    corner_weights = (along_x * along_y)[:, None] * along_z[None] * live_mask
    return corner_weights.astype(jnp.bfloat16)


def splat(weights, hidden):
    sums = jnp.einsum("czsp,hsp->sczh", weights, hidden, preferred_element_type=jnp.float32)
    slots, channels = sums.shape[0], sums.shape[3]
    sums = sums.astype(jnp.bfloat16)
    sums = sums.reshape(slots, EDGE, EDGE // PAIR, PAIR, Z, PAIR, channels)
    sums = sums.transpose(4, 1, 0, 2, 5, 3, 6)
    return sums.reshape(Z, EDGE, slots, EDGE * PAIR * channels)


def interpolate(weights, blocks):
    slots, channels = blocks.shape[2], blocks.shape[3] // (EDGE * PAIR)
    cells = blocks.reshape(Z, EDGE, slots, EDGE // PAIR, PAIR, PAIR, channels)
    cells = cells.transpose(2, 1, 3, 5, 0, 4, 6).reshape(slots, EDGE * EDGE, GZ, channels)
    return jnp.einsum("czsp,sczh->hsp", weights, cells, preferred_element_type=jnp.float32).astype(
        jnp.bfloat16
    )


def build_band(w_ref, band_ref, side_ref):
    channels = w_ref.shape[1]
    width = PAIR * channels

    def one(n, carry):
        layer, a = lax.div(n, 3), lax.rem(n, 3)
        band_ref[layer, :, a] = jnp.zeros(band_ref.shape[1:2] + band_ref.shape[3:], band_ref.dtype)
        side_ref[layer, :, a] = jnp.zeros(side_ref.shape[1:2] + side_ref.shape[3:], side_ref.dtype)
        for part, levels in enumerate(LEVELS):
            for slot, zl in enumerate(levels):
                for zz in range(PAIR):
                    e = zl - zz
                    if not 0 <= e <= 2:
                        continue
                    for source, row in ((0, 0), (1, 1), (2, 2), (-1, 3)):
                        for target in range(PAIR):
                            b = source - target + 1
                            if not 0 <= b <= 2:
                                continue
                            rows = slice(row * channels, (row + 1) * channels)
                            lanes = zz * width + target * channels
                            lanes = slice(lanes, lanes + channels)
                            block = w_ref[n * 9 + b * 3 + e]
                            band_ref[layer, part, a, slot, rows, lanes] = block
                            if source in (-1, 2):
                                rows = slice(slot * channels, (slot + 1) * channels)
                                side_ref[layer, max(source, 0) // 2, a, part, rows, lanes] = block
        return carry

    lax.fori_loop(0, band_ref.shape[0] * 3, one, 0)


def conv_kernel(
    sizes,
    ids_ref,
    sums_ref,
    w_ref,
    out_ref,
    ids,
    arrived,
    field,
    edge_out,
    edge_in,
    band_ref,
    side_ref,
    totals,
    sum_picks,
    out_picks,
    dense,
    values,
    id_send,
    id_recv,
    z_send,
    z_recv,
    x_send,
    x_recv,
    halo_send,
    halo_recv,
    edge_send,
    edge_recv,
    rx_send,
    rx_recv,
    rz_send,
    rz_recv,
):
    rows, columns = sizes
    strips = rows // Z
    blocks = dense.shape[2]
    slots = ids.shape[1]
    span = (field.shape[4] - blocks) // 2
    layers = field.shape[0]
    me_row, me_column = lax.axis_index("grid"), lax.axis_index("pts")
    me_z, me_x = lax.div(me_row, strips), lax.rem(me_row, strips)
    inner = pl.ds(span, blocks)

    def snake(column, x):
        return x + lax.rem(column, 2) * (strips - 1 - 2 * x)

    me_strip = snake(me_column, me_x)

    def beside(ds):
        strip = me_column * strips + me_strip + ds
        present = (strip >= 0) & (strip < columns * strips)
        column = lax.div(strip + strips, strips) - 1
        x = snake(column + 2, lax.rem(strip + strips, strips))
        return present, column, me_z * strips + x

    def above(dz):
        return (me_z + dz >= 0) & (me_z + dz < Z)

    def tell(t):
        return pltpu.make_async_remote_copy(
            src_ref=ids_ref,
            dst_ref=ids.at[me_row],
            send_sem=id_send.at[t],
            recv_sem=id_recv.at[t],
            device_id=(me_column, lax.rem(me_row + t, rows)),
            device_id_type=MESH,
        )

    def along_z(i, t):
        z = lax.rem(me_z + t, Z)
        return pltpu.make_async_remote_copy(
            src_ref=sums_ref.at[z, i],
            dst_ref=arrived.at[i, me_row],
            send_sem=z_send.at[i, t],
            recv_sem=z_recv.at[i, t],
            device_id=(me_column, z * strips + me_x),
            device_id_type=MESH,
        )

    def along_x(i, t, u):
        origin = lax.rem(me_z - t + Z, Z) * strips + me_x
        return pltpu.make_async_remote_copy(
            src_ref=sums_ref.at[me_z, i] if t == 0 else arrived.at[i, origin],
            dst_ref=arrived.at[i, origin],
            send_sem=x_send.at[i, t, u],
            recv_sem=x_recv.at[i, t, u],
            device_id=(me_column, me_z * strips + lax.rem(me_x + u, strips)),
            device_id_type=MESH,
        )

    def halo(layer, i, k):
        dz = (1, -1)[k]
        return pltpu.make_async_remote_copy(
            src_ref=field.at[layer, i + 1, :, 2 - k, inner],
            dst_ref=field.at[layer, i + 1, :, 3 * k, inner],
            send_sem=halo_send.at[layer, i, k],
            recv_sem=halo_recv.at[layer, i, k],
            device_id=(me_column, (me_z + dz) * strips + me_x),
            device_id_type=MESH,
        )

    def border(layer, i, part, side):
        _, column, row = beside((1, -1)[side])
        return pltpu.make_async_remote_copy(
            src_ref=edge_out.at[layer, i, side, part],
            dst_ref=edge_in.at[layer, i + 1, side, part],
            send_sem=edge_send.at[layer, i, part, side],
            recv_sem=edge_recv.at[layer, i, part, side],
            device_id=(column, row),
            device_id_type=MESH,
        )

    def back_x(i, u):
        return pltpu.make_async_remote_copy(
            src_ref=dense.at[i, me_strip],
            dst_ref=dense.at[i, me_strip],
            send_sem=rx_send.at[i, u],
            recv_sem=rx_recv.at[i, u],
            device_id=(me_column, me_z * strips + lax.rem(me_x + u, strips)),
            device_id_type=MESH,
        )

    def back_z(i, t):
        z = lax.rem(me_z + t, Z)
        return pltpu.make_async_remote_copy(
            src_ref=values.at[i, z],
            dst_ref=out_ref.at[me_z, i],
            send_sem=rz_send.at[i, t],
            recv_sem=rz_recv.at[i, t],
            device_id=(me_column, z * strips + me_x),
            device_id_type=MESH,
        )

    low_half = lax.broadcasted_iota(jnp.int32, (blocks, LANES), 1) < LANES // PAIR

    def send_border(layer, i, part):
        first, second = LEVELS[part]
        for side in range(2):
            rows = slice(blocks, blocks + span) if side == 0 else slice(span, 2 * span)
            view = field.at[layer, i + 1, 1 - side]
            tiles = [view[first, rows], view[second, rows]]
            tiles[side] = pltpu.roll(tiles[side].astype(jnp.float32), LANES // PAIR, 1).astype(
                jnp.bfloat16
            )
            edge_out[layer, i, side, part] = jnp.where(low_half[:span], tiles[0], tiles[1])

            @pl.when(beside((1, -1)[side])[0])
            def _():
                border(layer, i, part, side).start()

    def wait_border(layer, i):
        for side in range(2):

            @pl.when(beside((-1, 1)[side])[0])
            def _():
                for part in range(2):
                    border(layer, i, part, side).wait_recv()

    barrier = pltpu.get_barrier_semaphore()
    for t in range(1, rows):
        pl.semaphore_signal(
            barrier,
            inc=1,
            device_id=(me_column, lax.rem(me_row + t, rows)),
            device_id_type=MESH,
        )
    expected = rows - 1
    for ds in (-1, 1):
        present, column, row = beside(ds)
        other = present & (column != me_column)
        expected = expected + other.astype(jnp.int32)

        @pl.when(other)
        def _():
            pl.semaphore_signal(barrier, inc=1, device_id=(column, row), device_id_type=MESH)

    pl.semaphore_wait(barrier, expected)

    for t in range(1, rows):
        tell(t).start()
    for i in ORDER:
        for t in (2, 1, 3):
            along_z(i, t).start()
        for u in range(1, strips):
            along_x(i, 0, u).start()
    for i in ORDER:
        arrived[i, me_row] = sums_ref[me_z, i]
    ids[me_row] = ids_ref[...]
    for k in range(2):

        @pl.when(jnp.logical_not(above((-1, 1)[k])))
        def _():
            view = field.at[:, 1 : EDGE + 1, :, 3 * k, inner]
            view[...] = jnp.zeros(view.shape, field.dtype)

        @pl.when(jnp.logical_not(beside((-1, 1)[k])[0]))
        def _():
            view = edge_in.at[:, 1 : EDGE + 1, k]
            view[...] = jnp.zeros(view.shape, edge_in.dtype)

    for jp, rows_out in ((0, slice(span + blocks, 2 * span + blocks)), (1, slice(0, span))):
        view = field.at[:, :, jp, :, rows_out]
        view[...] = jnp.zeros(view.shape, field.dtype)
    build_band(w_ref, band_ref, side_ref)
    for t in range(1, rows):
        tell(t).wait_recv()

    def picks(named, first, width):
        parts = []
        for low in range(0, width, LANES):
            place_of = lax.broadcasted_iota(jnp.int32, named.shape, 1) + (low + first)
            parts.append(jnp.where(named == place_of, 1.0, 0.0))
        return jnp.concatenate(parts, axis=1)

    for r in range(rows):
        one_hot = picks(ids[r], me_strip * blocks, blocks)
        sum_picks[:, r * slots : (r + 1) * slots] = one_hot.T.astype(jnp.bfloat16)
    for z in range(Z):
        out_picks[z * slots : (z + 1) * slots] = picks(
            ids[z * strips + me_x], 0, strips * blocks
        ).astype(jnp.bfloat16)

    def forward(i):
        for t in (1, 2, 3):
            along_z(i, t).wait_recv()
            for u in range(1, strips):
                along_x(i, t, u).start()

    def spread(layer, i, tiles):
        for jp in range(PAIR):
            for zz in range(PAIR):
                field[layer, i + 1, jp, 1 + zz, inner] = tiles(jp, zz)
        for k in range(2):

            @pl.when(above((1, -1)[k]))
            def _():
                halo(layer, i, k).start()

        send_border(layer, i, 0)

    def gather(i):
        for t in range(Z):
            for u in range(1, strips):
                along_x(i, t, u).wait_recv()
        summed = jnp.dot(
            sum_picks[...],
            arrived[i].reshape(rows * slots, arrived.shape[3]),
            preferred_element_type=jnp.float32,
        ).astype(jnp.bfloat16)

        def tiles(jp, zz):
            low = (jp * PAIR + zz) * LANES
            return summed[:, low : low + LANES]

        spread(0, i, tiles)

    def shifted(tile, down):
        size = tile.shape[0]
        ranks = lax.broadcasted_iota(jnp.int32, tile.shape, 0)
        keep = lax.rem(ranks, span) != (0 if down else span - 1)
        moved = pltpu.roll(tile.astype(jnp.float32), 1 if down else size - 1, 0)
        return jnp.where(keep, moved, 0.0).astype(jnp.bfloat16)

    def shift(layer, i, levels):
        for down, phase, target in ((True, EDGE - 1, 0), (False, 0, EDGE + 1)):
            if phase == i:
                for jp in range(PAIR):
                    for zl in levels:
                        view = field.at[layer, :, jp, zl]
                        view[target, inner] = shifted(view[i + 1, inner], down)

    def shift_edges(layer, i):
        for down, phase, target in ((True, EDGE - 1, 0), (False, 0, EDGE + 1)):
            if phase == i:
                for side in range(2):
                    for part in range(2):
                        view = edge_in.at[layer, :, side, part]
                        view[target] = shifted(view[i + 1], down)

    def windows(layer, i, jp, levels):
        parts = []
        for a in range(3):
            for zl in levels:
                here = field.at[layer, i + a, :, zl]
                parts.append(here[jp, inner])
                if jp == 0:
                    up, down = here[1, inner], here[1, 0:blocks]
                else:
                    up, down = here[0, 2 * span : 2 * span + blocks], here[0, inner]
                parts.append(jnp.where(low_half, up, down))
        return jnp.concatenate(parts, axis=1)

    def conv_terms(layer, i, part):
        weight = band_ref[layer, part].reshape(-1, band_ref.shape[5])
        lhs = jnp.concatenate(
            [windows(layer, i, jp, LEVELS[part]) for jp in range(PAIR)], axis=0
        )
        return jnp.dot(lhs, weight, preferred_element_type=jnp.float32)

    def own_terms(layer, i):
        totals[i] = conv_terms(layer, i, 0)

    def edge_terms(layer, i):
        for side in range(2):
            lhs = jnp.concatenate(
                [edge_in[layer, i + a, side, part] for a in range(3) for part in range(2)], axis=1
            )
            weight = side_ref[layer, side].reshape(-1, side_ref.shape[5])
            rows_in = slice(0, span) if side == 0 else slice(2 * blocks - span, 2 * blocks)
            totals[i, rows_in] += jnp.dot(lhs, weight, preferred_element_type=jnp.float32)

    def finish(layer, i):
        total = totals[i]
        activated = (total / (1.0 + jnp.exp(-total))).astype(jnp.bfloat16)

        def tiles(jp, zz):
            return activated[jp * blocks : (jp + 1) * blocks, zz * LANES : (zz + 1) * LANES]

        if layer < layers - 1:
            spread(layer + 1, i, tiles)
            shift(layer + 1, i, LEVELS[0])
        else:
            for jp in range(PAIR):
                for zz in range(PAIR):
                    low = (jp * PAIR + zz) * LANES
                    dense[i, me_strip, :, low : low + LANES] = tiles(jp, zz)
            for u in range(1, strips):
                back_x(i, u).start()

    def ready(i, done):
        return {(i - 1) % EDGE, i, (i + 1) % EDGE} <= set(done)

    for n, i in enumerate(ORDER):
        forward(i)
        if n > 0:
            gather(ORDER[n - 1])
            shift(0, ORDER[n - 1], LEVELS[0])
    for i in OUT_ORDER:
        if ready(i, ORDER[:-1]):
            own_terms(0, i)
    gather(ORDER[-1])
    shift(0, ORDER[-1], LEVELS[0])
    for i in OUT_ORDER:
        if not ready(i, ORDER[:-1]):
            own_terms(0, i)

    for layer in range(layers):
        before = ORDER if layer == 0 else OUT_ORDER
        if layer > 0:
            for i in OUT_ORDER:
                own_terms(layer, i)
        reached, bordered = [], []

        def reach(i):
            for phase in before:
                if phase in {(i - 1) % EDGE, i, (i + 1) % EDGE} and phase not in reached:
                    for k in range(2):

                        @pl.when(above((-1, 1)[k]))
                        def _():
                            halo(layer, phase, k).wait_recv()

                    send_border(layer, phase, 1)
                    shift(layer, phase, LEVELS[1])
                    reached.append(phase)

        def close(i):
            for phase in before:
                if phase in {(i - 1) % EDGE, i, (i + 1) % EDGE} and phase not in bordered:
                    wait_border(layer, phase)
                    shift_edges(layer, phase)
                    bordered.append(phase)
            edge_terms(layer, i)
            finish(layer, i)

        for n, i in enumerate(OUT_ORDER):
            reach(i)
            totals[i] += conv_terms(layer, i, 1)
            if n > 0:
                close(OUT_ORDER[n - 1])
        close(OUT_ORDER[-1])

    for i in OUT_ORDER:
        for u in range(1, strips):
            back_x(i, u).wait_recv()
        picked = jnp.dot(
            out_picks[...],
            dense[i].reshape(strips * blocks, dense.shape[3]),
            preferred_element_type=jnp.float32,
        ).astype(jnp.bfloat16)
        values[i] = picked.reshape(values.shape[1:])
        for t in (2, 1, 3):
            back_z(i, t).start()
        out_ref[me_z, i] = values[i, me_z]

    for t in range(1, rows):
        tell(t).wait_send()
    for i in range(EDGE):
        for t in (1, 2, 3):
            back_z(i, t).wait_recv()
            back_z(i, t).wait_send()
            along_z(i, t).wait_send()
        for u in range(1, strips):
            back_x(i, u).wait_send()
            for t in range(Z):
                along_x(i, t, u).wait_send()
        for layer in range(layers):
            for k in range(2):

                @pl.when(above((1, -1)[k]))
                def _():
                    halo(layer, i, k).wait_send()

                @pl.when(beside((1, -1)[k])[0])
                def _():
                    for part in range(2):
                        border(layer, i, part, k).wait_send()


def exchange_and_convolve(ids, sums, w_conv):
    rows, columns = lax.axis_size("grid"), lax.axis_size("pts")
    strips = rows // Z
    slots, width = sums.shape[2:]
    layers, channels = w_conv.shape[0], w_conv.shape[4]
    span = rows * (TX // EDGE)
    blocks = span * (TY // EDGE) // strips
    halos = (layers, EDGE, 2)
    borders = halos + (2,)
    dma = pltpu.SemaphoreType.DMA
    return pl.pallas_call(
        functools.partial(conv_kernel, (rows, columns)),
        out_shape=jax.ShapeDtypeStruct(sums.shape, jnp.bfloat16),
        in_specs=[pl.BlockSpec(memory_space=pltpu.VMEM)] * 3,
        out_specs=pl.BlockSpec(memory_space=pltpu.VMEM),
        scratch_shapes=[
            pltpu.VMEM((rows, slots, LANES), jnp.int32),
            pltpu.VMEM((EDGE, rows, slots, width), jnp.bfloat16),
            pltpu.VMEM((layers, EDGE + 2, PAIR, PAIR + 2, blocks + 2 * span, LANES), jnp.bfloat16),
            pltpu.VMEM(borders + (span, LANES), jnp.bfloat16),
            pltpu.VMEM((layers, EDGE + 2, 2, 2, span, LANES), jnp.bfloat16),
            pltpu.VMEM((layers, 2, 3, 2, 2 * LANES, 2 * LANES), jnp.bfloat16),
            pltpu.VMEM((layers, 2, 3, 2, LANES, 2 * LANES), jnp.bfloat16),
            pltpu.VMEM((EDGE, PAIR * blocks, 2 * LANES), jnp.float32),
            pltpu.VMEM((blocks, rows * slots), jnp.bfloat16),
            pltpu.VMEM((Z * slots, strips * blocks), jnp.bfloat16),
            pltpu.VMEM((EDGE, strips, blocks, width), jnp.bfloat16),
            pltpu.VMEM((EDGE, Z, slots, width), jnp.bfloat16),
            dma((rows,)),
            dma((rows,)),
            dma((EDGE, Z)),
            dma((EDGE, Z)),
            dma((EDGE, Z, strips)),
            dma((EDGE, Z, strips)),
            dma(halos),
            dma(halos),
            dma(borders),
            dma(borders),
            dma((EDGE, strips)),
            dma((EDGE, strips)),
            dma((EDGE, Z)),
            dma((EDGE, Z)),
        ],
        compiler_params=pltpu.CompilerParams(collective_id=0, has_side_effects=True),
    )(ids, sums, w_conv.reshape(layers * 27, channels, channels))


def per_device(
    features, w_in, w_mid, w_conv, point_frac, point_base, slot_dest, slot_tile_block, slot_count
):
    slot_total = slot_dest.shape[0]
    slot_width = features.shape[1] // slot_total
    span = lax.axis_size("grid") * (TX // EDGE)
    along, across = TX // EDGE, TY // EDGE
    hidden_one = point_layer(w_in, features)
    hidden_two = point_layer(w_mid, hidden_one)
    channels = hidden_two.shape[0]
    hidden_two = hidden_two.reshape(channels, slot_total, slot_width)
    offsets, corners = lax.optimization_barrier(
        (
            point_frac.reshape(3, slot_total, slot_width),
            point_base.reshape(3, slot_total, slot_width),
        )
    )
    block_x = slot_dest * along + slot_tile_block // across
    block_y = slot_tile_block % across
    ids = jnp.broadcast_to((block_y * span + block_x)[:, None], (slot_total, LANES))
    weights = trilinear(offsets, corners, slot_count, EDGE, GZ)
    local_sums = splat(weights, hidden_two)
    blocks = exchange_and_convolve(ids, local_sums, w_conv)
    interp = interpolate(weights, blocks)
    point_out = (hidden_two.astype(jnp.float32) + interp.astype(jnp.float32)).astype(jnp.bfloat16)
    return point_out.reshape(channels, slot_total * slot_width)


def solution(mesh):
    return jax.shard_map(
        per_device,
        mesh=mesh,
        in_specs=(
            P(None, ("pts", "grid")),
            P(),
            P(),
            P(),
            P(None, ("pts", "grid")),
            P(None, ("pts", "grid")),
            P(("pts", "grid")),
            P(("pts", "grid")),
            P(("pts", "grid")),
        ),
        out_specs=P(None, ("pts", "grid")),
        check_vma=False,
    )
```

```python
import functools

import jax
import jax.numpy as jnp
from jax import lax
from jax.experimental import pallas as pl
from jax.experimental.pallas import tpu as pltpu
from jax.sharding import PartitionSpec as P

GZ = 8
EDGE = 4
TX = 32
TY = 32
LANES = 128
PAIR = 2
Z = GZ // PAIR
GROUP = 16
MESH = pl.DeviceIdType.MESH
LEVELS = ((1, 2), (0, 3))
ORDER = (3, 0, 1, 2)
OUT_ORDER = (0, 3, 1, 2)


def silu(total):
    return (total / (1.0 + jnp.exp(-total))).astype(jnp.bfloat16)


def point_layer(weight, inputs):
    return silu(
        lax.dot_general(
            weight, inputs, (((0,), (0,)), ((), ())), preferred_element_type=jnp.float32
        )
    )


def slot_weights(offsets, corners, count):
    width = offsets.shape[1]
    ranks = lax.broadcasted_iota(jnp.int32, (GZ, width), 0)
    live = lax.broadcasted_iota(jnp.int32, (GZ, width), 1) < count

    def axis(position, offset, corner):
        below_part = jnp.where(position == corner, 1.0 - offset, 0.0)
        above_part = jnp.where(position == corner + 1, offset, 0.0)
        return below_part + above_part

    first = ranks < EDGE
    along_xy = axis(
        lax.rem(ranks, EDGE),
        jnp.where(first, offsets[0:1], offsets[1:2]),
        jnp.where(first, corners[0:1], corners[1:2]),
    )
    along_z = jnp.where(live, axis(ranks, offsets[2:3], corners[2:3]), 0.0)
    rows = []
    for parity in range(PAIR):
        for i in range(EDGE):
            for jp in range(EDGE // PAIR):
                j = EDGE + jp * PAIR + parity
                rows.append(along_xy[i : i + 1] * along_xy[j : j + 1] * along_z)
    return jnp.concatenate(rows, axis=0).astype(jnp.bfloat16)


def splat_kernel(
    span,
    dest_ref,
    block_ref,
    count_ref,
    features_ref,
    w_in_ref,
    w_mid_ref,
    frac_ref,
    base_ref,
    sums_ref,
    hidden_ref,
    ids_ref,
    swap_ref,
):
    group = sums_ref.shape[2]
    width = hidden_ref.shape[1] // group
    half = EDGE * EDGE // PAIR * GZ
    along, across = TX // EDGE, TY // EDGE
    start = pl.program_id(0) * group
    hidden_one = point_layer(w_in_ref[...], features_ref[...])
    hidden_two = point_layer(w_mid_ref[...], hidden_one)
    hidden_ref[...] = hidden_two
    for s in range(group):
        points = slice(s * width, (s + 1) * width)
        weights = slot_weights(frac_ref[:, points], base_ref[:, points], count_ref[start + s])
        sums = lax.dot_general(
            weights,
            hidden_two[:, points],
            (((1,), (1,)), ((), ())),
            preferred_element_type=jnp.float32,
        )
        swap_ref[s * half : (s + 1) * half] = jnp.concatenate([sums[:half], sums[half:]], axis=1)
        dest, block = dest_ref[start + s], block_ref[start + s]
        number = lax.rem(block, across) * span + dest * along + lax.div(block, across)
        ids_ref[s : s + 1] = jnp.full((1, ids_ref.shape[1]), number, jnp.int32)
    for i in range(EDGE):
        for jp in range(EDGE // PAIR):
            for z in range(GZ):
                row = (i * (EDGE // PAIR) + jp) * GZ + z
                low = (jp * PAIR + z % PAIR) * LANES
                sums_ref[z // PAIR, i, :, low : low + LANES] = swap_ref[
                    pl.ds(row, group, stride=half)
                ].astype(jnp.bfloat16)


def interpolate_kernel(count_ref, cells_ref, hidden_ref, frac_ref, base_ref, out_ref, swap_ref):
    group = cells_ref.shape[2]
    width = hidden_ref.shape[1] // group
    channels = hidden_ref.shape[0]
    half = EDGE * EDGE // PAIR * GZ
    start = pl.program_id(0) * group
    for i in range(EDGE):
        for jp in range(EDGE // PAIR):
            for z in range(GZ):
                row = (i * (EDGE // PAIR) + jp) * GZ + z
                low = (jp * PAIR + z % PAIR) * LANES
                swap_ref[row * group : (row + 1) * group] = cells_ref[
                    z // PAIR, i, :, low : low + LANES
                ].astype(jnp.float32)
    for s in range(group):
        points = slice(s * width, (s + 1) * width)
        weights = slot_weights(frac_ref[:, points], base_ref[:, points], count_ref[start + s])
        cells = swap_ref[pl.ds(s, half, stride=group)].T
        cells = jnp.concatenate([cells[:channels], cells[channels:]], axis=1).astype(jnp.bfloat16)
        interp = jnp.dot(cells, weights, preferred_element_type=jnp.float32).astype(jnp.bfloat16)
        out_ref[:, points] = (
            hidden_ref[:, points].astype(jnp.float32) + interp.astype(jnp.float32)
        ).astype(jnp.bfloat16)


def grouped(extent, dimension, groups):
    block = tuple(n // groups if d == dimension else n for d, n in enumerate(extent))
    return pl.BlockSpec(block, lambda g: tuple(g if d == dimension else 0 for d in range(len(extent))))


def whole(extent):
    return pl.BlockSpec(extent, lambda g: (0,) * len(extent))


def splat(features, w_in, w_mid, frac, base, dest, block, count, span):
    slots, channels = dest.shape[0], w_mid.shape[1]
    groups = max(1, slots // GROUP)
    sums = (Z, EDGE, slots, EDGE * PAIR * channels)
    hidden = (channels, features.shape[1])
    half = EDGE * EDGE // PAIR * GZ
    smem = pl.BlockSpec(memory_space=pltpu.SMEM)
    return pl.pallas_call(
        functools.partial(splat_kernel, span),
        grid=(groups,),
        out_shape=(
            jax.ShapeDtypeStruct(sums, jnp.bfloat16),
            jax.ShapeDtypeStruct(hidden, jnp.bfloat16),
            jax.ShapeDtypeStruct((slots, LANES), jnp.int32),
        ),
        in_specs=[
            smem,
            smem,
            smem,
            grouped(features.shape, 1, groups),
            whole(w_in.shape),
            whole(w_mid.shape),
            grouped(frac.shape, 1, groups),
            grouped(base.shape, 1, groups),
        ],
        out_specs=(
            grouped(sums, 2, groups),
            grouped(hidden, 1, groups),
            grouped((slots, LANES), 0, groups),
        ),
        scratch_shapes=[pltpu.VMEM((slots // groups * half, PAIR * channels), jnp.float32)],
    )(dest, block, count, features, w_in, w_mid, frac, base)


def interpolate(cells, hidden, frac, base, count):
    slots, channels = count.shape[0], hidden.shape[0]
    groups = max(1, slots // GROUP)
    half = EDGE * EDGE // PAIR * GZ
    return pl.pallas_call(
        interpolate_kernel,
        grid=(groups,),
        out_shape=jax.ShapeDtypeStruct(hidden.shape, jnp.bfloat16),
        in_specs=[
            pl.BlockSpec(memory_space=pltpu.SMEM),
            grouped(cells.shape, 2, groups),
            grouped(hidden.shape, 1, groups),
            grouped(frac.shape, 1, groups),
            grouped(base.shape, 1, groups),
        ],
        out_specs=grouped(hidden.shape, 1, groups),
        scratch_shapes=[pltpu.VMEM((slots // groups * half, PAIR * channels), jnp.float32)],
    )(count, cells, hidden, frac, base)


def build_band(w_ref, band_ref, side_ref):
    channels = w_ref.shape[1]
    width = PAIR * channels

    def one(n, carry):
        layer, a = lax.div(n, 3), lax.rem(n, 3)
        band_ref[layer, :, a] = jnp.zeros(band_ref.shape[1:2] + band_ref.shape[3:], band_ref.dtype)
        side_ref[layer, :, a] = jnp.zeros(side_ref.shape[1:2] + side_ref.shape[3:], side_ref.dtype)
        for part, levels in enumerate(LEVELS):
            for slot, zl in enumerate(levels):
                for zz in range(PAIR):
                    e = zl - zz
                    if not 0 <= e <= 2:
                        continue
                    for source, row in ((0, 0), (1, 1), (2, 2), (-1, 3)):
                        for target in range(PAIR):
                            b = source - target + 1
                            if not 0 <= b <= 2:
                                continue
                            rows = slice(row * channels, (row + 1) * channels)
                            lanes = zz * width + target * channels
                            lanes = slice(lanes, lanes + channels)
                            block = w_ref[n * 9 + b * 3 + e]
                            band_ref[layer, part, a, slot, rows, lanes] = block
                            if source in (-1, 2):
                                rows = slice(slot * channels, (slot + 1) * channels)
                                side_ref[layer, max(source, 0) // 2, a, part, rows, lanes] = block
        return carry

    lax.fori_loop(0, band_ref.shape[0] * 3, one, 0)


def conv_kernel(
    sizes,
    ids_ref,
    sums_ref,
    w_ref,
    out_ref,
    ids,
    arrived,
    field,
    edge_out,
    edge_in,
    band_ref,
    side_ref,
    totals,
    sum_picks,
    out_picks,
    dense,
    values,
    id_send,
    id_recv,
    z_send,
    z_recv,
    x_send,
    x_recv,
    halo_send,
    halo_recv,
    edge_send,
    edge_recv,
    rx_send,
    rx_recv,
    rz_send,
    rz_recv,
):
    rows, columns = sizes
    strips = rows // Z
    blocks = dense.shape[2]
    slots = ids.shape[1]
    span = (field.shape[4] - blocks) // 2
    layers = field.shape[0]
    me_row, me_column = lax.axis_index("grid"), lax.axis_index("pts")
    me_z, me_x = lax.div(me_row, strips), lax.rem(me_row, strips)
    inner = pl.ds(span, blocks)

    def snake(column, x):
        return x + lax.rem(column, 2) * (strips - 1 - 2 * x)

    me_strip = snake(me_column, me_x)

    def beside(ds):
        strip = me_column * strips + me_strip + ds
        present = (strip >= 0) & (strip < columns * strips)
        column = lax.div(strip + strips, strips) - 1
        x = snake(column + 2, lax.rem(strip + strips, strips))
        return present, column, me_z * strips + x

    def above(dz):
        return (me_z + dz >= 0) & (me_z + dz < Z)

    def tell(t):
        return pltpu.make_async_remote_copy(
            src_ref=ids_ref,
            dst_ref=ids.at[me_row],
            send_sem=id_send.at[t],
            recv_sem=id_recv.at[t],
            device_id=(me_column, lax.rem(me_row + t, rows)),
            device_id_type=MESH,
        )

    def along_z(i, t):
        z = lax.rem(me_z + t, Z)
        return pltpu.make_async_remote_copy(
            src_ref=sums_ref.at[z, i],
            dst_ref=arrived.at[i, me_row],
            send_sem=z_send.at[i, t],
            recv_sem=z_recv.at[i, t],
            device_id=(me_column, z * strips + me_x),
            device_id_type=MESH,
        )

    def along_x(i, t, u):
        origin = lax.rem(me_z - t + Z, Z) * strips + me_x
        return pltpu.make_async_remote_copy(
            src_ref=sums_ref.at[me_z, i] if t == 0 else arrived.at[i, origin],
            dst_ref=arrived.at[i, origin],
            send_sem=x_send.at[i, t, u],
            recv_sem=x_recv.at[i, t, u],
            device_id=(me_column, me_z * strips + lax.rem(me_x + u, strips)),
            device_id_type=MESH,
        )

    def halo(layer, i, k):
        dz = (1, -1)[k]
        return pltpu.make_async_remote_copy(
            src_ref=field.at[layer, i + 1, :, 2 - k, inner],
            dst_ref=field.at[layer, i + 1, :, 3 * k, inner],
            send_sem=halo_send.at[layer, i, k],
            recv_sem=halo_recv.at[layer, i, k],
            device_id=(me_column, (me_z + dz) * strips + me_x),
            device_id_type=MESH,
        )

    def border(layer, i, part, side):
        _, column, row = beside((1, -1)[side])
        return pltpu.make_async_remote_copy(
            src_ref=edge_out.at[layer, i, side, part],
            dst_ref=edge_in.at[layer, i + 1, side, part],
            send_sem=edge_send.at[layer, i, part, side],
            recv_sem=edge_recv.at[layer, i, part, side],
            device_id=(column, row),
            device_id_type=MESH,
        )

    def back_x(i, u):
        return pltpu.make_async_remote_copy(
            src_ref=dense.at[i, me_strip],
            dst_ref=dense.at[i, me_strip],
            send_sem=rx_send.at[i, u],
            recv_sem=rx_recv.at[i, u],
            device_id=(me_column, me_z * strips + lax.rem(me_x + u, strips)),
            device_id_type=MESH,
        )

    def back_z(i, t):
        z = lax.rem(me_z + t, Z)
        return pltpu.make_async_remote_copy(
            src_ref=values.at[i, z],
            dst_ref=out_ref.at[me_z, i],
            send_sem=rz_send.at[i, t],
            recv_sem=rz_recv.at[i, t],
            device_id=(me_column, z * strips + me_x),
            device_id_type=MESH,
        )

    low_half = lax.broadcasted_iota(jnp.int32, (blocks, LANES), 1) < LANES // PAIR

    def send_border(layer, i, part):
        first, second = LEVELS[part]
        for side in range(2):
            rows = slice(blocks, blocks + span) if side == 0 else slice(span, 2 * span)
            view = field.at[layer, i + 1, 1 - side]
            tiles = [view[first, rows], view[second, rows]]
            tiles[side] = pltpu.roll(tiles[side].astype(jnp.float32), LANES // PAIR, 1).astype(
                jnp.bfloat16
            )
            edge_out[layer, i, side, part] = jnp.where(low_half[:span], tiles[0], tiles[1])

            @pl.when(beside((1, -1)[side])[0])
            def _():
                border(layer, i, part, side).start()

    def wait_border(layer, i):
        for side in range(2):

            @pl.when(beside((-1, 1)[side])[0])
            def _():
                for part in range(2):
                    border(layer, i, part, side).wait_recv()

    barrier = pltpu.get_barrier_semaphore()
    for t in range(1, rows):
        pl.semaphore_signal(
            barrier,
            inc=1,
            device_id=(me_column, lax.rem(me_row + t, rows)),
            device_id_type=MESH,
        )
    expected = rows - 1
    for ds in (-1, 1):
        present, column, row = beside(ds)
        other = present & (column != me_column)
        expected = expected + other.astype(jnp.int32)

        @pl.when(other)
        def _():
            pl.semaphore_signal(barrier, inc=1, device_id=(column, row), device_id_type=MESH)

    pl.semaphore_wait(barrier, expected)

    for t in range(1, rows):
        tell(t).start()
    for i in ORDER:
        for t in (2, 1, 3):
            along_z(i, t).start()
        for u in range(1, strips):
            along_x(i, 0, u).start()
    for i in ORDER:
        arrived[i, me_row] = sums_ref[me_z, i]
    ids[me_row] = ids_ref[...]
    for k in range(2):

        @pl.when(jnp.logical_not(above((-1, 1)[k])))
        def _():
            view = field.at[:, 1 : EDGE + 1, :, 3 * k, inner]
            view[...] = jnp.zeros(view.shape, field.dtype)

        @pl.when(jnp.logical_not(beside((-1, 1)[k])[0]))
        def _():
            view = edge_in.at[:, 1 : EDGE + 1, k]
            view[...] = jnp.zeros(view.shape, edge_in.dtype)

    for jp, rows_out in ((0, slice(span + blocks, 2 * span + blocks)), (1, slice(0, span))):
        view = field.at[:, :, jp, :, rows_out]
        view[...] = jnp.zeros(view.shape, field.dtype)
    build_band(w_ref, band_ref, side_ref)
    for t in range(1, rows):
        tell(t).wait_recv()

    def picks(named, first, width):
        parts = []
        for low in range(0, width, LANES):
            place_of = lax.broadcasted_iota(jnp.int32, named.shape, 1) + (low + first)
            parts.append(jnp.where(named == place_of, 1.0, 0.0))
        return jnp.concatenate(parts, axis=1)

    for r in range(rows):
        one_hot = picks(ids[r], me_strip * blocks, blocks)
        sum_picks[:, r * slots : (r + 1) * slots] = one_hot.T.astype(jnp.bfloat16)
    for z in range(Z):
        out_picks[z * slots : (z + 1) * slots] = picks(
            ids[z * strips + me_x], 0, strips * blocks
        ).astype(jnp.bfloat16)

    def forward(i):
        for t in (1, 2, 3):
            along_z(i, t).wait_recv()
            for u in range(1, strips):
                along_x(i, t, u).start()

    def spread(layer, i, tiles):
        for jp in range(PAIR):
            for zz in range(PAIR):
                field[layer, i + 1, jp, 1 + zz, inner] = tiles(jp, zz)
        for k in range(2):

            @pl.when(above((1, -1)[k]))
            def _():
                halo(layer, i, k).start()

        send_border(layer, i, 0)

    def gather(i):
        for t in range(Z):
            for u in range(1, strips):
                along_x(i, t, u).wait_recv()
        summed = jnp.dot(
            sum_picks[...],
            arrived[i].reshape(rows * slots, arrived.shape[3]),
            preferred_element_type=jnp.float32,
        ).astype(jnp.bfloat16)

        def tiles(jp, zz):
            low = (jp * PAIR + zz) * LANES
            return summed[:, low : low + LANES]

        spread(0, i, tiles)

    def shifted(tile, down):
        size = tile.shape[0]
        ranks = lax.broadcasted_iota(jnp.int32, tile.shape, 0)
        keep = lax.rem(ranks, span) != (0 if down else span - 1)
        moved = pltpu.roll(tile.astype(jnp.float32), 1 if down else size - 1, 0)
        return jnp.where(keep, moved, 0.0).astype(jnp.bfloat16)

    def shift(layer, i, levels):
        for down, phase, target in ((True, EDGE - 1, 0), (False, 0, EDGE + 1)):
            if phase == i:
                for jp in range(PAIR):
                    for zl in levels:
                        view = field.at[layer, :, jp, zl]
                        view[target, inner] = shifted(view[i + 1, inner], down)

    def shift_edges(layer, i):
        for down, phase, target in ((True, EDGE - 1, 0), (False, 0, EDGE + 1)):
            if phase == i:
                for side in range(2):
                    for part in range(2):
                        view = edge_in.at[layer, :, side, part]
                        view[target] = shifted(view[i + 1], down)

    def windows(layer, i, jp, levels):
        parts = []
        for a in range(3):
            for zl in levels:
                here = field.at[layer, i + a, :, zl]
                parts.append(here[jp, inner])
                if jp == 0:
                    up, down = here[1, inner], here[1, 0:blocks]
                else:
                    up, down = here[0, 2 * span : 2 * span + blocks], here[0, inner]
                parts.append(jnp.where(low_half, up, down))
        return jnp.concatenate(parts, axis=1)

    def conv_terms(layer, i, part):
        weight = band_ref[layer, part].reshape(-1, band_ref.shape[5])
        lhs = jnp.concatenate(
            [windows(layer, i, jp, LEVELS[part]) for jp in range(PAIR)], axis=0
        )
        return jnp.dot(lhs, weight, preferred_element_type=jnp.float32)

    def own_terms(layer, i):
        totals[i] = conv_terms(layer, i, 0)

    def edge_terms(layer, i):
        for side in range(2):
            lhs = jnp.concatenate(
                [edge_in[layer, i + a, side, part] for a in range(3) for part in range(2)], axis=1
            )
            weight = side_ref[layer, side].reshape(-1, side_ref.shape[5])
            rows_in = slice(0, span) if side == 0 else slice(2 * blocks - span, 2 * blocks)
            totals[i, rows_in] += jnp.dot(lhs, weight, preferred_element_type=jnp.float32)

    def finish(layer, i):
        total = totals[i]
        activated = silu(total)

        def tiles(jp, zz):
            return activated[jp * blocks : (jp + 1) * blocks, zz * LANES : (zz + 1) * LANES]

        if layer < layers - 1:
            spread(layer + 1, i, tiles)
            shift(layer + 1, i, LEVELS[0])
        else:
            for jp in range(PAIR):
                for zz in range(PAIR):
                    low = (jp * PAIR + zz) * LANES
                    dense[i, me_strip, :, low : low + LANES] = tiles(jp, zz)
            for u in range(1, strips):
                back_x(i, u).start()

    def ready(i, done):
        return {(i - 1) % EDGE, i, (i + 1) % EDGE} <= set(done)

    for n, i in enumerate(ORDER):
        forward(i)
        if n > 0:
            gather(ORDER[n - 1])
            shift(0, ORDER[n - 1], LEVELS[0])
    for i in OUT_ORDER:
        if ready(i, ORDER[:-1]):
            own_terms(0, i)
    gather(ORDER[-1])
    shift(0, ORDER[-1], LEVELS[0])
    for i in OUT_ORDER:
        if not ready(i, ORDER[:-1]):
            own_terms(0, i)

    for layer in range(layers):
        before = ORDER if layer == 0 else OUT_ORDER
        if layer > 0:
            for i in OUT_ORDER:
                own_terms(layer, i)
        reached, bordered = [], []

        def reach(i):
            for phase in before:
                if phase in {(i - 1) % EDGE, i, (i + 1) % EDGE} and phase not in reached:
                    for k in range(2):

                        @pl.when(above((-1, 1)[k]))
                        def _():
                            halo(layer, phase, k).wait_recv()

                    send_border(layer, phase, 1)
                    shift(layer, phase, LEVELS[1])
                    reached.append(phase)

        def close(i):
            for phase in before:
                if phase in {(i - 1) % EDGE, i, (i + 1) % EDGE} and phase not in bordered:
                    wait_border(layer, phase)
                    shift_edges(layer, phase)
                    bordered.append(phase)
            edge_terms(layer, i)
            finish(layer, i)

        for n, i in enumerate(OUT_ORDER):
            reach(i)
            totals[i] += conv_terms(layer, i, 1)
            if n > 0:
                close(OUT_ORDER[n - 1])
        close(OUT_ORDER[-1])

    for i in OUT_ORDER:
        for u in range(1, strips):
            back_x(i, u).wait_recv()
        picked = jnp.dot(
            out_picks[...],
            dense[i].reshape(strips * blocks, dense.shape[3]),
            preferred_element_type=jnp.float32,
        ).astype(jnp.bfloat16)
        values[i] = picked.reshape(values.shape[1:])
        for t in (2, 1, 3):
            back_z(i, t).start()
        out_ref[me_z, i] = values[i, me_z]

    for t in range(1, rows):
        tell(t).wait_send()
    for i in range(EDGE):
        for t in (1, 2, 3):
            back_z(i, t).wait_recv()
            back_z(i, t).wait_send()
            along_z(i, t).wait_send()
        for u in range(1, strips):
            back_x(i, u).wait_send()
            for t in range(Z):
                along_x(i, t, u).wait_send()
        for layer in range(layers):
            for k in range(2):

                @pl.when(above((1, -1)[k]))
                def _():
                    halo(layer, i, k).wait_send()

                @pl.when(beside((1, -1)[k])[0])
                def _():
                    for part in range(2):
                        border(layer, i, part, k).wait_send()


def exchange_and_convolve(ids, sums, w_conv):
    rows, columns = lax.axis_size("grid"), lax.axis_size("pts")
    strips = rows // Z
    slots, width = sums.shape[2:]
    layers, channels = w_conv.shape[0], w_conv.shape[4]
    span = rows * (TX // EDGE)
    blocks = span * (TY // EDGE) // strips
    halos = (layers, EDGE, 2)
    borders = halos + (2,)
    dma = pltpu.SemaphoreType.DMA
    return pl.pallas_call(
        functools.partial(conv_kernel, (rows, columns)),
        out_shape=jax.ShapeDtypeStruct(sums.shape, jnp.bfloat16),
        in_specs=[pl.BlockSpec(memory_space=pltpu.VMEM)] * 3,
        out_specs=pl.BlockSpec(memory_space=pltpu.VMEM),
        scratch_shapes=[
            pltpu.VMEM((rows, slots, LANES), jnp.int32),
            pltpu.VMEM((EDGE, rows, slots, width), jnp.bfloat16),
            pltpu.VMEM((layers, EDGE + 2, PAIR, PAIR + 2, blocks + 2 * span, LANES), jnp.bfloat16),
            pltpu.VMEM(borders + (span, LANES), jnp.bfloat16),
            pltpu.VMEM((layers, EDGE + 2, 2, 2, span, LANES), jnp.bfloat16),
            pltpu.VMEM((layers, 2, 3, 2, 2 * LANES, 2 * LANES), jnp.bfloat16),
            pltpu.VMEM((layers, 2, 3, 2, LANES, 2 * LANES), jnp.bfloat16),
            pltpu.VMEM((EDGE, PAIR * blocks, 2 * LANES), jnp.float32),
            pltpu.VMEM((blocks, rows * slots), jnp.bfloat16),
            pltpu.VMEM((Z * slots, strips * blocks), jnp.bfloat16),
            pltpu.VMEM((EDGE, strips, blocks, width), jnp.bfloat16),
            pltpu.VMEM((EDGE, Z, slots, width), jnp.bfloat16),
            dma((rows,)),
            dma((rows,)),
            dma((EDGE, Z)),
            dma((EDGE, Z)),
            dma((EDGE, Z, strips)),
            dma((EDGE, Z, strips)),
            dma(halos),
            dma(halos),
            dma(borders),
            dma(borders),
            dma((EDGE, strips)),
            dma((EDGE, strips)),
            dma((EDGE, Z)),
            dma((EDGE, Z)),
        ],
        compiler_params=pltpu.CompilerParams(collective_id=0, has_side_effects=True),
    )(ids, sums, w_conv.reshape(layers * 27, channels, channels))


def per_device(
    features, w_in, w_mid, w_conv, point_frac, point_base, slot_dest, slot_tile_block, slot_count
):
    span = lax.axis_size("grid") * (TX // EDGE)
    sums, hidden, ids = splat(
        features, w_in, w_mid, point_frac, point_base, slot_dest, slot_tile_block, slot_count, span
    )
    cells = exchange_and_convolve(ids, sums, w_conv)
    return interpolate(cells, hidden, point_frac, point_base, slot_count)


def solution(mesh):
    return jax.shard_map(
        per_device,
        mesh=mesh,
        in_specs=(
            P(None, ("pts", "grid")),
            P(),
            P(),
            P(),
            P(None, ("pts", "grid")),
            P(None, ("pts", "grid")),
            P(("pts", "grid")),
            P(("pts", "grid")),
            P(("pts", "grid")),
        ),
        out_specs=P(None, ("pts", "grid")),
        check_vma=False,
    )
```

```python
import functools

import jax
import jax.numpy as jnp
from jax import lax
from jax.experimental import pallas as pl
from jax.experimental.pallas import tpu as pltpu
from jax.sharding import PartitionSpec as P

GZ = 8
EDGE = 4
TX = 32
TY = 32
LANES = 128
PAIR = 2
Z = GZ // PAIR
GROUP = 16
MESH = pl.DeviceIdType.MESH
LEVELS = ((1, 2), (0, 3))
ORDER = (3, 0, 1, 2)
OUT_ORDER = (0, 3, 1, 2)


def silu(total):
    return (total / (1.0 + jnp.exp(-total))).astype(jnp.bfloat16)


def point_layer(weight, inputs):
    return silu(
        lax.dot_general(
            weight, inputs, (((0,), (0,)), ((), ())), preferred_element_type=jnp.float32
        )
    )


def slot_weights(offsets, corners, count):
    width = offsets.shape[1]
    ranks = lax.broadcasted_iota(jnp.int32, (GZ, width), 0)
    live = lax.broadcasted_iota(jnp.int32, (GZ, width), 1) < count

    def axis(position, offset, corner):
        below_part = jnp.where(position == corner, 1.0 - offset, 0.0)
        above_part = jnp.where(position == corner + 1, offset, 0.0)
        return below_part + above_part

    first = ranks < EDGE
    along_xy = axis(
        lax.rem(ranks, EDGE),
        jnp.where(first, offsets[0:1], offsets[1:2]),
        jnp.where(first, corners[0:1], corners[1:2]),
    )
    along_z = jnp.where(live, axis(ranks, offsets[2:3], corners[2:3]), 0.0)
    rows = []
    for parity in range(PAIR):
        for i in range(EDGE):
            for jp in range(EDGE // PAIR):
                j = EDGE + jp * PAIR + parity
                rows.append(along_xy[i : i + 1] * along_xy[j : j + 1] * along_z)
    return jnp.concatenate(rows, axis=0).astype(jnp.bfloat16)


def splat_slots(count_ref, features_ref, w_in_ref, w_mid_ref, frac_ref, base_ref, hidden_ref, swap_ref):
    slots = count_ref.shape[0]
    width = hidden_ref.shape[1] // slots
    half = EDGE * EDGE // PAIR * GZ

    def one(g, carry):
        first = g * GROUP
        points = pl.ds(pl.multiple_of(first * width, GROUP * width), GROUP * width)
        hidden_one = point_layer(w_in_ref[...], features_ref[:, points])
        hidden_two = point_layer(w_mid_ref[...], hidden_one)
        hidden_ref[:, points] = hidden_two
        offsets, corners = frac_ref[:, points], base_ref[:, points]
        for s in range(GROUP):
            part = slice(s * width, (s + 1) * width)
            weights = slot_weights(offsets[:, part], corners[:, part], count_ref[first + s])
            sums = lax.dot_general(
                weights,
                hidden_two[:, part],
                (((1,), (1,)), ((), ())),
                preferred_element_type=jnp.float32,
            )
            rows = pl.ds(pl.multiple_of((first + s) * half, half), half)
            swap_ref[rows] = jnp.concatenate([sums[:half], sums[half:]], axis=1)
        return carry

    lax.fori_loop(0, slots // GROUP, one, 0)


def swap_phase(i, swap_ref, sums_ref):
    slots = sums_ref.shape[3]
    half = EDGE * EDGE // PAIR * GZ
    for jp in range(PAIR):
        for z in range(GZ):
            row = (i * PAIR + jp) * GZ + z
            low = z % PAIR * LANES
            sums_ref[z // PAIR, i, jp, :, low : low + LANES] = swap_ref[
                pl.ds(row, slots, stride=half)
            ].astype(jnp.bfloat16)


def interpolate_kernel(count_ref, cells_ref, hidden_ref, frac_ref, base_ref, out_ref, swap_ref):
    group = cells_ref.shape[3]
    width = hidden_ref.shape[1] // group
    channels = hidden_ref.shape[0]
    half = EDGE * EDGE // PAIR * GZ
    start = pl.program_id(0) * group
    for i in range(EDGE):
        for jp in range(EDGE // PAIR):
            for z in range(GZ):
                row = (i * (EDGE // PAIR) + jp) * GZ + z
                low = z % PAIR * LANES
                swap_ref[row * group : (row + 1) * group] = cells_ref[
                    z // PAIR, i, jp, :, low : low + LANES
                ].astype(jnp.float32)
    for s in range(group):
        points = slice(s * width, (s + 1) * width)
        weights = slot_weights(frac_ref[:, points], base_ref[:, points], count_ref[start + s])
        cells = swap_ref[pl.ds(s, half, stride=group)].T
        cells = jnp.concatenate([cells[:channels], cells[channels:]], axis=1).astype(jnp.bfloat16)
        interp = jnp.dot(cells, weights, preferred_element_type=jnp.float32).astype(jnp.bfloat16)
        out_ref[:, points] = (
            hidden_ref[:, points].astype(jnp.float32) + interp.astype(jnp.float32)
        ).astype(jnp.bfloat16)


def grouped(extent, dimension, groups):
    block = tuple(n // groups if d == dimension else n for d, n in enumerate(extent))
    return pl.BlockSpec(block, lambda g: tuple(g if d == dimension else 0 for d in range(len(extent))))


def interpolate(cells, hidden, frac, base, count):
    slots, channels = count.shape[0], hidden.shape[0]
    groups = max(1, slots // GROUP)
    half = EDGE * EDGE // PAIR * GZ
    return pl.pallas_call(
        interpolate_kernel,
        grid=(groups,),
        out_shape=jax.ShapeDtypeStruct(hidden.shape, jnp.bfloat16),
        in_specs=[
            pl.BlockSpec(memory_space=pltpu.SMEM),
            grouped(cells.shape, 3, groups),
            grouped(hidden.shape, 1, groups),
            grouped(frac.shape, 1, groups),
            grouped(base.shape, 1, groups),
        ],
        out_specs=grouped(hidden.shape, 1, groups),
        scratch_shapes=[pltpu.VMEM((slots // groups * half, PAIR * channels), jnp.float32)],
    )(count, cells, hidden, frac, base)


def build_band(w_ref, band_ref, side_ref):
    channels = w_ref.shape[1]
    width = PAIR * channels

    def one(n, carry):
        layer, a = lax.div(n, 3), lax.rem(n, 3)
        band_ref[layer, :, a] = jnp.zeros(band_ref.shape[1:2] + band_ref.shape[3:], band_ref.dtype)
        side_ref[layer, :, a] = jnp.zeros(side_ref.shape[1:2] + side_ref.shape[3:], side_ref.dtype)
        for part, levels in enumerate(LEVELS):
            for slot, zl in enumerate(levels):
                for zz in range(PAIR):
                    e = zl - zz
                    if not 0 <= e <= 2:
                        continue
                    for source, row in ((0, 0), (1, 1), (2, 2), (-1, 3)):
                        for target in range(PAIR):
                            b = source - target + 1
                            if not 0 <= b <= 2:
                                continue
                            rows = slice(row * channels, (row + 1) * channels)
                            lanes = zz * width + target * channels
                            lanes = slice(lanes, lanes + channels)
                            block = w_ref[n * 9 + b * 3 + e]
                            band_ref[layer, part, a, slot, rows, lanes] = block
                            if source in (-1, 2):
                                rows = slice(slot * channels, (slot + 1) * channels)
                                side_ref[layer, max(source, 0) // 2, a, part, rows, lanes] = block
        return carry

    lax.fori_loop(0, band_ref.shape[0] * 3, one, 0)


def conv_kernel(
    sizes,
    count_ref,
    dest_ref,
    block_ref,
    features_ref,
    w_in_ref,
    w_mid_ref,
    frac_ref,
    base_ref,
    w_hbm,
    out_ref,
    hidden_out,
    w_ref,
    hidden_ref,
    swap_ref,
    sums_ref,
    own_ids,
    ids,
    arrived,
    field,
    edge_out,
    edge_in,
    band_ref,
    side_ref,
    totals,
    sum_picks,
    out_picks,
    dense,
    values,
    id_send,
    id_recv,
    z_send,
    z_recv,
    x_send,
    x_recv,
    halo_send,
    halo_recv,
    edge_send,
    edge_recv,
    rx_send,
    rx_recv,
    rz_send,
    rz_recv,
    local_sem,
):
    rows, columns = sizes
    strips = rows // Z
    blocks = dense.shape[3]
    slots = sums_ref.shape[3]
    span = (field.shape[4] - blocks) // 2
    layers = field.shape[0]
    me_row, me_column = lax.axis_index("grid"), lax.axis_index("pts")
    me_z, me_x = lax.div(me_row, strips), lax.rem(me_row, strips)
    inner = pl.ds(span, blocks)

    def snake(column, x):
        return x + lax.rem(column, 2) * (strips - 1 - 2 * x)

    me_strip = snake(me_column, me_x)

    def beside(ds):
        strip = me_column * strips + me_strip + ds
        present = (strip >= 0) & (strip < columns * strips)
        column = lax.div(strip + strips, strips) - 1
        x = snake(column + 2, lax.rem(strip + strips, strips))
        return present, column, me_z * strips + x

    def above(dz):
        return (me_z + dz >= 0) & (me_z + dz < Z)

    def tell(t):
        return pltpu.make_async_remote_copy(
            src_ref=own_ids,
            dst_ref=ids.at[me_row],
            send_sem=id_send.at[t],
            recv_sem=id_recv.at[t],
            device_id=(me_column, lax.rem(me_row + t, rows)),
            device_id_type=MESH,
        )

    def along_z(i, jp, t):
        z = lax.rem(me_z + t, Z)
        return pltpu.make_async_remote_copy(
            src_ref=sums_ref.at[z, i, jp],
            dst_ref=arrived.at[i, jp, me_row],
            send_sem=z_send.at[i, jp, t],
            recv_sem=z_recv.at[i, jp, t],
            device_id=(me_column, z * strips + me_x),
            device_id_type=MESH,
        )

    def along_x(i, jp, t, u):
        origin = lax.rem(me_z - t + Z, Z) * strips + me_x
        return pltpu.make_async_remote_copy(
            src_ref=sums_ref.at[me_z, i, jp] if t == 0 else arrived.at[i, jp, origin],
            dst_ref=arrived.at[i, jp, origin],
            send_sem=x_send.at[i, jp, t, u],
            recv_sem=x_recv.at[i, jp, t, u],
            device_id=(me_column, me_z * strips + lax.rem(me_x + u, strips)),
            device_id_type=MESH,
        )

    def halo(layer, i, k):
        dz = (1, -1)[k]
        return pltpu.make_async_remote_copy(
            src_ref=field.at[layer, i + 1, :, 2 - k, inner],
            dst_ref=field.at[layer, i + 1, :, 3 * k, inner],
            send_sem=halo_send.at[layer, i, k],
            recv_sem=halo_recv.at[layer, i, k],
            device_id=(me_column, (me_z + dz) * strips + me_x),
            device_id_type=MESH,
        )

    def border(layer, i, part, side):
        _, column, row = beside((1, -1)[side])
        return pltpu.make_async_remote_copy(
            src_ref=edge_out.at[layer, i, side, part],
            dst_ref=edge_in.at[layer, i + 1, side, part],
            send_sem=edge_send.at[layer, i, part, side],
            recv_sem=edge_recv.at[layer, i, part, side],
            device_id=(column, row),
            device_id_type=MESH,
        )

    def back_x(i, jp, u):
        return pltpu.make_async_remote_copy(
            src_ref=dense.at[i, jp, me_strip],
            dst_ref=dense.at[i, jp, me_strip],
            send_sem=rx_send.at[i, jp, u],
            recv_sem=rx_recv.at[i, jp, u],
            device_id=(me_column, me_z * strips + lax.rem(me_x + u, strips)),
            device_id_type=MESH,
        )

    def back_z(i, jp, t):
        z = lax.rem(me_z + t, Z)
        return pltpu.make_async_remote_copy(
            src_ref=values.at[i, jp, z],
            dst_ref=out_ref.at[me_z, i, jp],
            send_sem=rz_send.at[i, jp, t],
            recv_sem=rz_recv.at[i, jp, t],
            device_id=(me_column, z * strips + me_x),
            device_id_type=MESH,
        )

    low_half = lax.broadcasted_iota(jnp.int32, (blocks, LANES), 1) < LANES // PAIR

    def send_border(layer, i, part):
        first, second = LEVELS[part]
        for side in range(2):
            rows = slice(blocks, blocks + span) if side == 0 else slice(span, 2 * span)
            view = field.at[layer, i + 1, 1 - side]
            tiles = [view[first, rows], view[second, rows]]
            tiles[side] = pltpu.roll(tiles[side].astype(jnp.float32), LANES // PAIR, 1).astype(
                jnp.bfloat16
            )
            edge_out[layer, i, side, part] = jnp.where(low_half[:span], tiles[0], tiles[1])

            @pl.when(beside((1, -1)[side])[0])
            def _():
                border(layer, i, part, side).start()

    def wait_border(layer, i):
        for side in range(2):

            @pl.when(beside((-1, 1)[side])[0])
            def _():
                for part in range(2):
                    border(layer, i, part, side).wait_recv()

    barrier = pltpu.get_barrier_semaphore()
    for t in range(1, rows):
        pl.semaphore_signal(
            barrier,
            inc=1,
            device_id=(me_column, lax.rem(me_row + t, rows)),
            device_id_type=MESH,
        )
    expected = rows - 1
    for ds in (-1, 1):
        present, column, row = beside(ds)
        other = present & (column != me_column)
        expected = expected + other.astype(jnp.int32)

        @pl.when(other)
        def _():
            pl.semaphore_signal(barrier, inc=1, device_id=(column, row), device_id_type=MESH)

    load = pltpu.make_async_copy(w_hbm, w_ref, local_sem.at[0])
    load.start()
    splat_slots(
        count_ref, features_ref, w_in_ref, w_mid_ref, frac_ref, base_ref, hidden_ref, swap_ref
    )
    keep = pltpu.make_async_copy(hidden_ref, hidden_out, local_sem.at[1])
    keep.start()
    block = block_ref[...]
    along, across = TX // EDGE, TY // EDGE
    number = lax.rem(block, across) * span + dest_ref[...] * along + lax.div(block, across)
    own_ids[...] = jnp.broadcast_to(number, own_ids.shape)
    pl.semaphore_wait(barrier, expected)

    for t in range(1, rows):
        tell(t).start()
    for i in ORDER:
        swap_phase(i, swap_ref, sums_ref)
        for jp in range(PAIR):
            for t in (2, 1, 3):
                along_z(i, jp, t).start()
            for u in range(1, strips):
                along_x(i, jp, 0, u).start()
    for i in ORDER:
        for jp in range(PAIR):
            arrived[i, jp, me_row] = sums_ref[me_z, i, jp]
    ids[me_row] = own_ids[...]
    for k in range(2):

        @pl.when(jnp.logical_not(above((-1, 1)[k])))
        def _():
            view = field.at[:, 1 : EDGE + 1, :, 3 * k, inner]
            view[...] = jnp.zeros(view.shape, field.dtype)

        @pl.when(jnp.logical_not(beside((-1, 1)[k])[0]))
        def _():
            view = edge_in.at[:, 1 : EDGE + 1, k]
            view[...] = jnp.zeros(view.shape, edge_in.dtype)

    for jp, rows_out in ((0, slice(span + blocks, 2 * span + blocks)), (1, slice(0, span))):
        view = field.at[:, :, jp, :, rows_out]
        view[...] = jnp.zeros(view.shape, field.dtype)
    def picks(r, first, size):
        named = jnp.broadcast_to(ids[r, 0:1, :slots], (size, slots))
        place_of = lax.broadcasted_iota(jnp.int32, (size, slots), 0) + first
        return jnp.where(named == place_of, 1.0, 0.0)

    def build_picks():
        for t in range(1, rows):
            tell(t).wait_recv()
        for r in range(rows):
            sum_picks[:, r * slots : (r + 1) * slots] = picks(
                r, me_strip * blocks, blocks
            ).astype(jnp.bfloat16)
        for z in range(Z):
            out_picks[z * slots : (z + 1) * slots] = picks(
                z * strips + me_x, 0, strips * blocks
            ).T.astype(jnp.bfloat16)

    def forward(i):
        for jp in range(PAIR):
            for t in (1, 2, 3):
                along_z(i, jp, t).wait_recv()
                for u in range(1, strips):
                    along_x(i, jp, t, u).start()

    def spread(layer, i, tiles):
        for jp in range(PAIR):
            for zz in range(PAIR):
                field[layer, i + 1, jp, 1 + zz, inner] = tiles(jp, zz)
        for k in range(2):

            @pl.when(above((1, -1)[k]))
            def _():
                halo(layer, i, k).start()

        send_border(layer, i, 0)

    def gather(i):
        summed = []
        for jp in range(PAIR):
            for t in range(Z):
                for u in range(1, strips):
                    along_x(i, jp, t, u).wait_recv()
            summed.append(
                jnp.dot(
                    sum_picks[...],
                    arrived[i, jp].reshape(rows * slots, arrived.shape[4]),
                    preferred_element_type=jnp.float32,
                ).astype(jnp.bfloat16)
            )
        spread(0, i, lambda jp, zz: summed[jp][:, zz * LANES : (zz + 1) * LANES])

    def shifted(tile, down):
        size = tile.shape[0]
        ranks = lax.broadcasted_iota(jnp.int32, tile.shape, 0)
        keep = lax.rem(ranks, span) != (0 if down else span - 1)
        moved = pltpu.roll(tile.astype(jnp.float32), 1 if down else size - 1, 0)
        return jnp.where(keep, moved, 0.0).astype(jnp.bfloat16)

    def shift(layer, i, levels):
        for down, phase, target in ((True, EDGE - 1, 0), (False, 0, EDGE + 1)):
            if phase == i:
                for jp in range(PAIR):
                    for zl in levels:
                        view = field.at[layer, :, jp, zl]
                        view[target, inner] = shifted(view[i + 1, inner], down)

    def shift_edges(layer, i):
        for down, phase, target in ((True, EDGE - 1, 0), (False, 0, EDGE + 1)):
            if phase == i:
                for side in range(2):
                    for part in range(2):
                        view = edge_in.at[layer, :, side, part]
                        view[target] = shifted(view[i + 1], down)

    def windows(layer, i, jp, levels):
        parts = []
        for a in range(3):
            for zl in levels:
                here = field.at[layer, i + a, :, zl]
                parts.append(here[jp, inner])
                if jp == 0:
                    up, down = here[1, inner], here[1, 0:blocks]
                else:
                    up, down = here[0, 2 * span : 2 * span + blocks], here[0, inner]
                parts.append(jnp.where(low_half, up, down))
        return jnp.concatenate(parts, axis=1)

    def conv_terms(layer, i, part):
        weight = band_ref[layer, part].reshape(-1, band_ref.shape[5])
        lhs = jnp.concatenate(
            [windows(layer, i, jp, LEVELS[part]) for jp in range(PAIR)], axis=0
        )
        return jnp.dot(lhs, weight, preferred_element_type=jnp.float32)

    def own_terms(layer, i):
        totals[i] = conv_terms(layer, i, 0)

    def edge_terms(layer, i):
        for side in range(2):
            lhs = jnp.concatenate(
                [edge_in[layer, i + a, side, part] for a in range(3) for part in range(2)], axis=1
            )
            weight = side_ref[layer, side].reshape(-1, side_ref.shape[5])
            rows_in = slice(0, span) if side == 0 else slice(2 * blocks - span, 2 * blocks)
            totals[i, rows_in] += jnp.dot(lhs, weight, preferred_element_type=jnp.float32)

    def finish(layer, i):
        total = totals[i]
        activated = silu(total)

        def tiles(jp, zz):
            return activated[jp * blocks : (jp + 1) * blocks, zz * LANES : (zz + 1) * LANES]

        if layer < layers - 1:
            spread(layer + 1, i, tiles)
            shift(layer + 1, i, LEVELS[0])
        else:
            for jp in range(PAIR):
                dense[i, jp, me_strip] = activated[jp * blocks : (jp + 1) * blocks]
                for u in range(1, strips):
                    back_x(i, jp, u).start()

    def ready(i, done):
        return {(i - 1) % EDGE, i, (i + 1) % EDGE} <= set(done)

    for n, i in enumerate(ORDER):
        forward(i)
        if n == 0:
            build_picks()
            load.wait()
            build_band(w_ref, band_ref, side_ref)
        if n > 0:
            gather(ORDER[n - 1])
            shift(0, ORDER[n - 1], LEVELS[0])
    for i in OUT_ORDER:
        if ready(i, ORDER[:-1]):
            own_terms(0, i)
    gather(ORDER[-1])
    shift(0, ORDER[-1], LEVELS[0])
    for i in OUT_ORDER:
        if not ready(i, ORDER[:-1]):
            own_terms(0, i)

    for layer in range(layers):
        before = ORDER if layer == 0 else OUT_ORDER
        if layer > 0:
            for i in OUT_ORDER:
                own_terms(layer, i)
        reached, bordered = [], []

        def reach(i):
            for phase in before:
                if phase in {(i - 1) % EDGE, i, (i + 1) % EDGE} and phase not in reached:
                    for k in range(2):

                        @pl.when(above((-1, 1)[k]))
                        def _():
                            halo(layer, phase, k).wait_recv()

                    send_border(layer, phase, 1)
                    shift(layer, phase, LEVELS[1])
                    reached.append(phase)

        def close(i):
            for phase in before:
                if phase in {(i - 1) % EDGE, i, (i + 1) % EDGE} and phase not in bordered:
                    wait_border(layer, phase)
                    shift_edges(layer, phase)
                    bordered.append(phase)
            edge_terms(layer, i)
            finish(layer, i)

        for n, i in enumerate(OUT_ORDER):
            reach(i)
            totals[i] += conv_terms(layer, i, 1)
            if n > 0:
                close(OUT_ORDER[n - 1])
        close(OUT_ORDER[-1])

    for i in OUT_ORDER:
        for jp in range(PAIR):
            for u in range(1, strips):
                back_x(i, jp, u).wait_recv()
            picked = jnp.dot(
                out_picks[...],
                dense[i, jp].reshape(strips * blocks, dense.shape[4]),
                preferred_element_type=jnp.float32,
            ).astype(jnp.bfloat16)
            values[i, jp] = picked.reshape(values.shape[2:])
            for t in (2, 1, 3):
                back_z(i, jp, t).start()
            out_ref[me_z, i, jp] = values[i, jp, me_z]

    keep.wait()
    for t in range(1, rows):
        tell(t).wait_send()
    for i in range(EDGE):
        for jp in range(PAIR):
            for t in (1, 2, 3):
                back_z(i, jp, t).wait_recv()
                back_z(i, jp, t).wait_send()
                along_z(i, jp, t).wait_send()
            for u in range(1, strips):
                back_x(i, jp, u).wait_send()
                for t in range(Z):
                    along_x(i, jp, t, u).wait_send()
        for layer in range(layers):
            for k in range(2):

                @pl.when(above((1, -1)[k]))
                def _():
                    halo(layer, i, k).wait_send()

                @pl.when(beside((1, -1)[k])[0])
                def _():
                    for part in range(2):
                        border(layer, i, part, k).wait_send()


def exchange_and_convolve(
    features, w_in, w_mid, w_conv, frac, base, slot_dest, slot_tile_block, slot_count
):
    rows, columns = lax.axis_size("grid"), lax.axis_size("pts")
    strips = rows // Z
    slots = slot_count.shape[0]
    layers, channels = w_conv.shape[0], w_conv.shape[4]
    width = PAIR * PAIR * channels
    span = rows * (TX // EDGE)
    blocks = span * (TY // EDGE) // strips
    half = EDGE * EDGE // PAIR * GZ
    hidden = (channels, features.shape[1])
    cells = (Z, EDGE, PAIR, slots, width)
    weights = (layers * 27, channels, channels)
    halos = (layers, EDGE, 2)
    borders = halos + (2,)
    dma = pltpu.SemaphoreType.DMA
    vmem = pl.BlockSpec(memory_space=pltpu.VMEM)
    return pl.pallas_call(
        functools.partial(conv_kernel, (rows, columns)),
        out_shape=(
            jax.ShapeDtypeStruct(cells, jnp.bfloat16),
            jax.ShapeDtypeStruct(hidden, jnp.bfloat16),
        ),
        in_specs=[pl.BlockSpec(memory_space=pltpu.SMEM)]
        + [vmem] * 7
        + [pl.BlockSpec(memory_space=pl.ANY)],
        out_specs=(vmem, pl.BlockSpec(memory_space=pl.ANY)),
        scratch_shapes=[
            pltpu.VMEM(weights, jnp.bfloat16),
            pltpu.VMEM(hidden, jnp.bfloat16),
            pltpu.VMEM((slots * half, LANES), jnp.float32),
            pltpu.VMEM(cells, jnp.bfloat16),
            pltpu.VMEM((8, slots), jnp.int32),
            pltpu.VMEM((rows, 8, slots), jnp.int32),
            pltpu.VMEM((EDGE, PAIR, rows, slots, width), jnp.bfloat16),
            pltpu.VMEM((layers, EDGE + 2, PAIR, PAIR + 2, blocks + 2 * span, LANES), jnp.bfloat16),
            pltpu.VMEM(borders + (span, LANES), jnp.bfloat16),
            pltpu.VMEM((layers, EDGE + 2, 2, 2, span, LANES), jnp.bfloat16),
            pltpu.VMEM((layers, 2, 3, 2, 2 * LANES, 2 * LANES), jnp.bfloat16),
            pltpu.VMEM((layers, 2, 3, 2, LANES, 2 * LANES), jnp.bfloat16),
            pltpu.VMEM((EDGE, PAIR * blocks, 2 * LANES), jnp.float32),
            pltpu.VMEM((blocks, rows * slots), jnp.bfloat16),
            pltpu.VMEM((Z * slots, strips * blocks), jnp.bfloat16),
            pltpu.VMEM((EDGE, PAIR, strips, blocks, width), jnp.bfloat16),
            pltpu.VMEM((EDGE, PAIR, Z, slots, width), jnp.bfloat16),
            dma((rows,)),
            dma((rows,)),
            dma((EDGE, PAIR, Z)),
            dma((EDGE, PAIR, Z)),
            dma((EDGE, PAIR, Z, strips)),
            dma((EDGE, PAIR, Z, strips)),
            dma(halos),
            dma(halos),
            dma(borders),
            dma(borders),
            dma((EDGE, PAIR, strips)),
            dma((EDGE, PAIR, strips)),
            dma((EDGE, PAIR, Z)),
            dma((EDGE, PAIR, Z)),
            dma((2,)),
        ],
        compiler_params=pltpu.CompilerParams(collective_id=0, has_side_effects=True),
    )(
        slot_count,
        slot_dest.reshape(1, slots),
        slot_tile_block.reshape(1, slots),
        features,
        w_in,
        w_mid,
        frac,
        base,
        w_conv.reshape(weights),
    )


def per_device(
    features, w_in, w_mid, w_conv, point_frac, point_base, slot_dest, slot_tile_block, slot_count
):
    cells, hidden = exchange_and_convolve(
        features, w_in, w_mid, w_conv, point_frac, point_base, slot_dest, slot_tile_block, slot_count
    )
    return interpolate(cells, hidden, point_frac, point_base, slot_count)


def solution(mesh):
    return jax.shard_map(
        per_device,
        mesh=mesh,
        in_specs=(
            P(None, ("pts", "grid")),
            P(),
            P(),
            P(),
            P(None, ("pts", "grid")),
            P(None, ("pts", "grid")),
            P(("pts", "grid")),
            P(("pts", "grid")),
            P(("pts", "grid")),
        ),
        out_specs=P(None, ("pts", "grid")),
        check_vma=False,
    )
```

```python
import functools

import jax
import jax.numpy as jnp
from jax import lax
from jax.experimental import pallas as pl
from jax.experimental.pallas import tpu as pltpu
from jax.sharding import PartitionSpec as P

GZ = 8
EDGE = 4
TX = 32
TY = 32
LANES = 128
PAIR = 2
Z = GZ // PAIR
GROUP = 16
HALVES = 2
MESH = pl.DeviceIdType.MESH
LEVELS = ((1, 2), (0, 3))
ORDER = (3, 0, 1, 2)
OUT_ORDER = (0, 3, 1, 2)


def silu(total):
    return (total / (1.0 + jnp.exp(-total))).astype(jnp.bfloat16)


def point_layer(weight, inputs):
    return silu(
        lax.dot_general(
            weight, inputs, (((0,), (0,)), ((), ())), preferred_element_type=jnp.float32
        )
    )


def slot_weights(offsets, corners, count):
    width = offsets.shape[1]
    ranks = lax.broadcasted_iota(jnp.int32, (GZ, width), 0)
    live = lax.broadcasted_iota(jnp.int32, (GZ, width), 1) < count

    def axis(position, offset, corner):
        below_part = jnp.where(position == corner, 1.0 - offset, 0.0)
        above_part = jnp.where(position == corner + 1, offset, 0.0)
        return below_part + above_part

    first = ranks < EDGE
    along_xy = axis(
        lax.rem(ranks, EDGE),
        jnp.where(first, offsets[0:1], offsets[1:2]),
        jnp.where(first, corners[0:1], corners[1:2]),
    )
    along_z = jnp.where(live, axis(ranks, offsets[2:3], corners[2:3]), 0.0)
    rows = []
    for parity in range(PAIR):
        for i in range(EDGE):
            for jp in range(EDGE // PAIR):
                j = EDGE + jp * PAIR + parity
                rows.append(along_xy[i : i + 1] * along_xy[j : j + 1] * along_z)
    return jnp.concatenate(rows, axis=0).astype(jnp.bfloat16)


def splat_slots(
    part, count_ref, features_ref, w_in_ref, w_mid_ref, frac_ref, base_ref, hidden_ref, swap_ref
):
    slots = count_ref.shape[0]
    width = hidden_ref.shape[1] // slots
    half = EDGE * EDGE // PAIR * GZ

    def one(g, carry):
        first = g * GROUP
        points = pl.ds(pl.multiple_of(first * width, GROUP * width), GROUP * width)
        hidden_one = point_layer(w_in_ref[...], features_ref[:, points])
        hidden_two = point_layer(w_mid_ref[...], hidden_one)
        hidden_ref[:, points] = hidden_two
        offsets, corners = frac_ref[:, points], base_ref[:, points]
        for s in range(GROUP):
            part = slice(s * width, (s + 1) * width)
            weights = slot_weights(offsets[:, part], corners[:, part], count_ref[first + s])
            sums = lax.dot_general(
                weights,
                hidden_two[:, part],
                (((1,), (1,)), ((), ())),
                preferred_element_type=jnp.float32,
            )
            rows = pl.ds(pl.multiple_of((first + s) * half, half), half)
            swap_ref[rows] = jnp.concatenate([sums[:half], sums[half:]], axis=1)
        return carry

    steps = slots // (GROUP * HALVES)
    lax.fori_loop(part * steps, (part + 1) * steps, one, 0)


def swap_phase(i, part, swap_ref, sums_ref):
    slots = sums_ref.shape[3]
    half = EDGE * EDGE // PAIR * GZ
    for jp in range(PAIR):
        for z in range(GZ):
            row = (i * PAIR + jp) * GZ + z
            low = (jp * PAIR + z % PAIR) * LANES
            sums_ref[z // PAIR, i, part, :, low : low + LANES] = swap_ref[
                pl.ds(part * slots * half + row, slots, stride=half)
            ].astype(jnp.bfloat16)


def interpolate_kernel(count_ref, cells_ref, hidden_ref, frac_ref, base_ref, out_ref, swap_ref):
    group = cells_ref.shape[3]
    width = hidden_ref.shape[1] // group
    channels = hidden_ref.shape[0]
    half = EDGE * EDGE // PAIR * GZ
    start = pl.program_id(0) * group
    for i in range(EDGE):
        for jp in range(EDGE // PAIR):
            for z in range(GZ):
                row = (i * (EDGE // PAIR) + jp) * GZ + z
                low = z % PAIR * LANES
                swap_ref[row * group : (row + 1) * group] = cells_ref[
                    z // PAIR, i, jp, :, low : low + LANES
                ].astype(jnp.float32)
    for s in range(group):
        points = slice(s * width, (s + 1) * width)
        weights = slot_weights(frac_ref[:, points], base_ref[:, points], count_ref[start + s])
        cells = swap_ref[pl.ds(s, half, stride=group)].T
        cells = jnp.concatenate([cells[:channels], cells[channels:]], axis=1).astype(jnp.bfloat16)
        interp = jnp.dot(cells, weights, preferred_element_type=jnp.float32).astype(jnp.bfloat16)
        out_ref[:, points] = (
            hidden_ref[:, points].astype(jnp.float32) + interp.astype(jnp.float32)
        ).astype(jnp.bfloat16)


def grouped(extent, dimension, groups):
    block = tuple(n // groups if d == dimension else n for d, n in enumerate(extent))
    return pl.BlockSpec(block, lambda g: tuple(g if d == dimension else 0 for d in range(len(extent))))


def interpolate(cells, hidden, frac, base, count):
    slots, channels = count.shape[0], hidden.shape[0]
    groups = max(1, slots // GROUP)
    half = EDGE * EDGE // PAIR * GZ
    return pl.pallas_call(
        interpolate_kernel,
        grid=(groups,),
        out_shape=jax.ShapeDtypeStruct(hidden.shape, jnp.bfloat16),
        in_specs=[
            pl.BlockSpec(memory_space=pltpu.SMEM),
            grouped(cells.shape, 3, groups),
            grouped(hidden.shape, 1, groups),
            grouped(frac.shape, 1, groups),
            grouped(base.shape, 1, groups),
        ],
        out_specs=grouped(hidden.shape, 1, groups),
        scratch_shapes=[pltpu.VMEM((slots // groups * half, PAIR * channels), jnp.float32)],
    )(count, cells, hidden, frac, base)


def build_band(w_ref, band_ref, side_ref):
    channels = w_ref.shape[1]
    width = PAIR * channels

    def one(n, carry):
        layer, a = lax.div(n, 3), lax.rem(n, 3)
        band_ref[layer, :, a] = jnp.zeros(band_ref.shape[1:2] + band_ref.shape[3:], band_ref.dtype)
        side_ref[layer, :, a] = jnp.zeros(side_ref.shape[1:2] + side_ref.shape[3:], side_ref.dtype)
        for part, levels in enumerate(LEVELS):
            for slot, zl in enumerate(levels):
                for zz in range(PAIR):
                    e = zl - zz
                    if not 0 <= e <= 2:
                        continue
                    for source, row in ((0, 0), (1, 1), (2, 2), (-1, 3)):
                        for target in range(PAIR):
                            b = source - target + 1
                            if not 0 <= b <= 2:
                                continue
                            rows = slice(row * channels, (row + 1) * channels)
                            lanes = zz * width + target * channels
                            lanes = slice(lanes, lanes + channels)
                            block = w_ref[n * 9 + b * 3 + e]
                            band_ref[layer, part, a, slot, rows, lanes] = block
                            if source in (-1, 2):
                                rows = slice(slot * channels, (slot + 1) * channels)
                                side_ref[layer, max(source, 0) // 2, a, part, rows, lanes] = block
        return carry

    lax.fori_loop(0, band_ref.shape[0] * 3, one, 0)


def conv_kernel(
    sizes,
    count_ref,
    dest_ref,
    block_ref,
    features_ref,
    w_in_ref,
    w_mid_ref,
    frac_ref,
    base_ref,
    w_hbm,
    out_ref,
    hidden_out,
    w_ref,
    hidden_ref,
    swap_ref,
    sums_ref,
    own_ids,
    ids,
    arrived,
    field,
    edge_out,
    edge_in,
    band_ref,
    side_ref,
    totals,
    sum_picks,
    out_picks,
    dense,
    values,
    id_send,
    id_recv,
    z_send,
    z_recv,
    x_send,
    x_recv,
    halo_send,
    halo_recv,
    edge_send,
    edge_recv,
    rx_send,
    rx_recv,
    rz_send,
    rz_recv,
    local_sem,
):
    rows, columns = sizes
    strips = rows // Z
    blocks = dense.shape[3]
    slots = values.shape[3]
    share = sums_ref.shape[3]
    span = (field.shape[4] - blocks) // 2
    layers = field.shape[0]
    me_row, me_column = lax.axis_index("grid"), lax.axis_index("pts")
    me_z, me_x = lax.div(me_row, strips), lax.rem(me_row, strips)
    inner = pl.ds(span, blocks)

    def snake(column, x):
        return x + lax.rem(column, 2) * (strips - 1 - 2 * x)

    me_strip = snake(me_column, me_x)

    def beside(ds):
        strip = me_column * strips + me_strip + ds
        present = (strip >= 0) & (strip < columns * strips)
        column = lax.div(strip + strips, strips) - 1
        x = snake(column + 2, lax.rem(strip + strips, strips))
        return present, column, me_z * strips + x

    def above(dz):
        return (me_z + dz >= 0) & (me_z + dz < Z)

    def tell(t):
        return pltpu.make_async_remote_copy(
            src_ref=own_ids,
            dst_ref=ids.at[me_row],
            send_sem=id_send.at[t],
            recv_sem=id_recv.at[t],
            device_id=(me_column, lax.rem(me_row + t, rows)),
            device_id_type=MESH,
        )

    def along_z(i, h, t):
        z = lax.rem(me_z + t, Z)
        return pltpu.make_async_remote_copy(
            src_ref=sums_ref.at[z, i, h],
            dst_ref=arrived.at[i, h, me_row],
            send_sem=z_send.at[i, h, t],
            recv_sem=z_recv.at[i, h, t],
            device_id=(me_column, z * strips + me_x),
            device_id_type=MESH,
        )

    def along_x(i, h, t, u):
        origin = lax.rem(me_z - t + Z, Z) * strips + me_x
        return pltpu.make_async_remote_copy(
            src_ref=sums_ref.at[me_z, i, h] if t == 0 else arrived.at[i, h, origin],
            dst_ref=arrived.at[i, h, origin],
            send_sem=x_send.at[i, h, t, u],
            recv_sem=x_recv.at[i, h, t, u],
            device_id=(me_column, me_z * strips + lax.rem(me_x + u, strips)),
            device_id_type=MESH,
        )

    def halo(layer, i, k):
        dz = (1, -1)[k]
        return pltpu.make_async_remote_copy(
            src_ref=field.at[layer, i + 1, :, 2 - k, inner],
            dst_ref=field.at[layer, i + 1, :, 3 * k, inner],
            send_sem=halo_send.at[layer, i, k],
            recv_sem=halo_recv.at[layer, i, k],
            device_id=(me_column, (me_z + dz) * strips + me_x),
            device_id_type=MESH,
        )

    def border(layer, i, part, side):
        _, column, row = beside((1, -1)[side])
        return pltpu.make_async_remote_copy(
            src_ref=edge_out.at[layer, i, side, part],
            dst_ref=edge_in.at[layer, i + 1, side, part],
            send_sem=edge_send.at[layer, i, part, side],
            recv_sem=edge_recv.at[layer, i, part, side],
            device_id=(column, row),
            device_id_type=MESH,
        )

    def back_x(i, jp, u):
        return pltpu.make_async_remote_copy(
            src_ref=dense.at[i, jp, me_strip],
            dst_ref=dense.at[i, jp, me_strip],
            send_sem=rx_send.at[i, jp, u],
            recv_sem=rx_recv.at[i, jp, u],
            device_id=(me_column, me_z * strips + lax.rem(me_x + u, strips)),
            device_id_type=MESH,
        )

    def back_z(i, jp, t):
        z = lax.rem(me_z + t, Z)
        return pltpu.make_async_remote_copy(
            src_ref=values.at[i, jp, z],
            dst_ref=out_ref.at[me_z, i, jp],
            send_sem=rz_send.at[i, jp, t],
            recv_sem=rz_recv.at[i, jp, t],
            device_id=(me_column, z * strips + me_x),
            device_id_type=MESH,
        )

    low_half = lax.broadcasted_iota(jnp.int32, (blocks, LANES), 1) < LANES // PAIR

    def send_border(layer, i, part):
        first, second = LEVELS[part]
        for side in range(2):
            rows = slice(blocks, blocks + span) if side == 0 else slice(span, 2 * span)
            view = field.at[layer, i + 1, 1 - side]
            tiles = [view[first, rows], view[second, rows]]
            tiles[side] = pltpu.roll(tiles[side].astype(jnp.float32), LANES // PAIR, 1).astype(
                jnp.bfloat16
            )
            edge_out[layer, i, side, part] = jnp.where(low_half[:span], tiles[0], tiles[1])

            @pl.when(beside((1, -1)[side])[0])
            def _():
                border(layer, i, part, side).start()

    def wait_border(layer, i):
        for side in range(2):

            @pl.when(beside((-1, 1)[side])[0])
            def _():
                for part in range(2):
                    border(layer, i, part, side).wait_recv()

    barrier = pltpu.get_barrier_semaphore()
    for t in range(1, rows):
        pl.semaphore_signal(
            barrier,
            inc=1,
            device_id=(me_column, lax.rem(me_row + t, rows)),
            device_id_type=MESH,
        )
    expected = rows - 1
    for ds in (-1, 1):
        present, column, row = beside(ds)
        other = present & (column != me_column)
        expected = expected + other.astype(jnp.int32)

        @pl.when(other)
        def _():
            pl.semaphore_signal(barrier, inc=1, device_id=(column, row), device_id_type=MESH)

    load = pltpu.make_async_copy(w_hbm, w_ref, local_sem.at[0])
    load.start()
    block = block_ref[...]
    along, across = TX // EDGE, TY // EDGE
    number = lax.rem(block, across) * span + dest_ref[...] * along + lax.div(block, across)
    own_ids[...] = jnp.broadcast_to(number, own_ids.shape)
    ids[me_row] = own_ids[...]
    keep = pltpu.make_async_copy(hidden_ref, hidden_out, local_sem.at[1])
    for h in range(HALVES):
        splat_slots(
            h, count_ref, features_ref, w_in_ref, w_mid_ref, frac_ref, base_ref, hidden_ref, swap_ref
        )
        if h == 0:
            pl.semaphore_wait(barrier, expected)
            for t in range(1, rows):
                tell(t).start()
        for i in ORDER:
            swap_phase(i, h, swap_ref, sums_ref)
            for t in (2, 1, 3):
                along_z(i, h, t).start()
            for u in range(1, strips):
                along_x(i, h, 0, u).start()
            arrived[i, h, me_row] = sums_ref[me_z, i, h]
    keep.start()
    for k in range(2):

        @pl.when(jnp.logical_not(above((-1, 1)[k])))
        def _():
            view = field.at[:, 1 : EDGE + 1, :, 3 * k, inner]
            view[...] = jnp.zeros(view.shape, field.dtype)

        @pl.when(jnp.logical_not(beside((-1, 1)[k])[0]))
        def _():
            view = edge_in.at[:, 1 : EDGE + 1, k]
            view[...] = jnp.zeros(view.shape, edge_in.dtype)

    for jp, rows_out in ((0, slice(span + blocks, 2 * span + blocks)), (1, slice(0, span))):
        view = field.at[:, :, jp, :, rows_out]
        view[...] = jnp.zeros(view.shape, field.dtype)
    def picks(r, first, size):
        named = jnp.broadcast_to(ids[r, 0:1, :slots], (size, slots))
        place_of = lax.broadcasted_iota(jnp.int32, (size, slots), 0) + first
        return jnp.where(named == place_of, 1.0, 0.0)

    def build_picks():
        for t in range(1, rows):
            tell(t).wait_recv()
        for r in range(rows):
            one_hot = picks(r, me_strip * blocks, blocks).astype(jnp.bfloat16)
            for h in range(HALVES):
                low = (h * rows + r) * share
                sum_picks[:, low : low + share] = one_hot[:, h * share : (h + 1) * share]
        for z in range(Z):
            out_picks[z * slots : (z + 1) * slots] = picks(
                z * strips + me_x, 0, strips * blocks
            ).T.astype(jnp.bfloat16)

    def forward(i, h):
        for t in (1, 2, 3):
            along_z(i, h, t).wait_recv()
            for u in range(1, strips):
                along_x(i, h, t, u).start()

    def spread(layer, i, tiles):
        for jp in range(PAIR):
            for zz in range(PAIR):
                field[layer, i + 1, jp, 1 + zz, inner] = tiles(jp, zz)
        for k in range(2):

            @pl.when(above((1, -1)[k]))
            def _():
                halo(layer, i, k).start()

        send_border(layer, i, 0)

    def gather(i):
        for h in range(HALVES):
            for t in range(Z):
                for u in range(1, strips):
                    along_x(i, h, t, u).wait_recv()
        summed = jnp.dot(
            sum_picks[...],
            arrived[i].reshape(rows * slots, arrived.shape[4]),
            preferred_element_type=jnp.float32,
        ).astype(jnp.bfloat16)

        def tiles(jp, zz):
            low = (jp * PAIR + zz) * LANES
            return summed[:, low : low + LANES]

        spread(0, i, tiles)

    def shifted(tile, down):
        size = tile.shape[0]
        ranks = lax.broadcasted_iota(jnp.int32, tile.shape, 0)
        keep = lax.rem(ranks, span) != (0 if down else span - 1)
        moved = pltpu.roll(tile.astype(jnp.float32), 1 if down else size - 1, 0)
        return jnp.where(keep, moved, 0.0).astype(jnp.bfloat16)

    def shift(layer, i, levels):
        for down, phase, target in ((True, EDGE - 1, 0), (False, 0, EDGE + 1)):
            if phase == i:
                for jp in range(PAIR):
                    for zl in levels:
                        view = field.at[layer, :, jp, zl]
                        view[target, inner] = shifted(view[i + 1, inner], down)

    def shift_edges(layer, i):
        for down, phase, target in ((True, EDGE - 1, 0), (False, 0, EDGE + 1)):
            if phase == i:
                for side in range(2):
                    for part in range(2):
                        view = edge_in.at[layer, :, side, part]
                        view[target] = shifted(view[i + 1], down)

    def windows(layer, i, jp, levels, taps):
        parts = []
        for a in taps:
            for zl in levels:
                here = field.at[layer, i + a, :, zl]
                parts.append(here[jp, inner])
                if jp == 0:
                    up, down = here[1, inner], here[1, 0:blocks]
                else:
                    up, down = here[0, 2 * span : 2 * span + blocks], here[0, inner]
                parts.append(jnp.where(low_half, up, down))
        return jnp.concatenate(parts, axis=1)

    def conv_terms(layer, i, part, taps):
        depth = band_ref.shape[5]
        weight = jnp.concatenate(
            [band_ref[layer, part, a].reshape(-1, depth) for a in taps], axis=0
        )
        lhs = jnp.concatenate(
            [windows(layer, i, jp, LEVELS[part], taps) for jp in range(PAIR)], axis=0
        )
        return jnp.dot(lhs, weight, preferred_element_type=jnp.float32)

    def own_terms(layer, i):
        totals[i] = conv_terms(layer, i, 0, range(3))

    def edge_terms(layer, i):
        for side in range(2):
            lhs = jnp.concatenate(
                [edge_in[layer, i + a, side, part] for a in range(3) for part in range(2)], axis=1
            )
            weight = side_ref[layer, side].reshape(-1, side_ref.shape[5])
            rows_in = slice(0, span) if side == 0 else slice(2 * blocks - span, 2 * blocks)
            totals[i, rows_in] += jnp.dot(lhs, weight, preferred_element_type=jnp.float32)

    def finish(layer, i):
        total = totals[i]
        activated = silu(total)

        def tiles(jp, zz):
            return activated[jp * blocks : (jp + 1) * blocks, zz * LANES : (zz + 1) * LANES]

        if layer < layers - 1:
            spread(layer + 1, i, tiles)
            shift(layer + 1, i, LEVELS[0])
        else:
            for jp in range(PAIR):
                dense[i, jp, me_strip] = activated[jp * blocks : (jp + 1) * blocks]
                for u in range(1, strips):
                    back_x(i, jp, u).start()

    def near(i):
        return ((i - 1) % EDGE, i, (i + 1) % EDGE)

    for h in range(HALVES):
        for n, i in enumerate(ORDER):
            forward(i, h)
            if h == 0 and n == 0:
                build_picks()
            if h == 0 and n == 1:
                load.wait()
                build_band(w_ref, band_ref, side_ref)
            if h == HALVES - 1 and n > 0:
                gather(ORDER[n - 1])
                shift(0, ORDER[n - 1], LEVELS[0])
    for i in OUT_ORDER:
        if ORDER[-1] not in near(i):
            own_terms(0, i)
    gather(ORDER[-1])
    shift(0, ORDER[-1], LEVELS[0])
    for i in OUT_ORDER:
        if ORDER[-1] in near(i):
            own_terms(0, i)

    for layer in range(layers):
        before = ORDER if layer == 0 else OUT_ORDER
        if layer > 0:
            for i in OUT_ORDER:
                own_terms(layer, i)
        bordered = []

        def reach(phase):
            for k in range(2):

                @pl.when(above((-1, 1)[k]))
                def _():
                    halo(layer, phase, k).wait_recv()

            send_border(layer, phase, 1)
            shift(layer, phase, LEVELS[1])

        def add_terms(i, phases):
            taps = [a for a in range(3) if near(i)[a] in phases]
            totals[i] += conv_terms(layer, i, 1, taps)

        def close(i):
            for phase in before:
                if phase in near(i) and phase not in bordered:
                    wait_border(layer, phase)
                    shift_edges(layer, phase)
                    bordered.append(phase)
            edge_terms(layer, i)
            finish(layer, i)

        reached = []
        for n, i in enumerate(OUT_ORDER):
            for phase in before:
                if phase in near(i) and phase not in reached:
                    reach(phase)
                    reached.append(phase)
            add_terms(i, before)
            if n > 0:
                close(OUT_ORDER[n - 1])
        close(OUT_ORDER[-1])

    for i in OUT_ORDER:
        for jp in range(PAIR):
            for u in range(1, strips):
                back_x(i, jp, u).wait_recv()
            picked = jnp.dot(
                out_picks[...],
                dense[i, jp].reshape(strips * blocks, dense.shape[4]),
                preferred_element_type=jnp.float32,
            ).astype(jnp.bfloat16)
            values[i, jp] = picked.reshape(values.shape[2:])
            for t in (2, 1, 3):
                back_z(i, jp, t).start()
            out_ref[me_z, i, jp] = values[i, jp, me_z]

    keep.wait()
    for t in range(1, rows):
        tell(t).wait_send()
    for i in range(EDGE):
        for jp in range(PAIR):
            for t in (1, 2, 3):
                back_z(i, jp, t).wait_recv()
                back_z(i, jp, t).wait_send()
            for u in range(1, strips):
                back_x(i, jp, u).wait_send()
        for h in range(HALVES):
            for t in (1, 2, 3):
                along_z(i, h, t).wait_send()
            for u in range(1, strips):
                for t in range(Z):
                    along_x(i, h, t, u).wait_send()
        for layer in range(layers):
            for k in range(2):

                @pl.when(above((1, -1)[k]))
                def _():
                    halo(layer, i, k).wait_send()

                @pl.when(beside((1, -1)[k])[0])
                def _():
                    for part in range(2):
                        border(layer, i, part, k).wait_send()


def exchange_and_convolve(
    features, w_in, w_mid, w_conv, frac, base, slot_dest, slot_tile_block, slot_count
):
    rows, columns = lax.axis_size("grid"), lax.axis_size("pts")
    strips = rows // Z
    slots = slot_count.shape[0]
    layers, channels = w_conv.shape[0], w_conv.shape[4]
    width = PAIR * PAIR * channels
    span = rows * (TX // EDGE)
    blocks = span * (TY // EDGE) // strips
    half = EDGE * EDGE // PAIR * GZ
    hidden = (channels, features.shape[1])
    cells = (Z, EDGE, PAIR, slots, width)
    weights = (layers * 27, channels, channels)
    share = (HALVES, slots // HALVES, PAIR * width)
    halos = (layers, EDGE, 2)
    borders = halos + (2,)
    dma = pltpu.SemaphoreType.DMA
    vmem = pl.BlockSpec(memory_space=pltpu.VMEM)
    return pl.pallas_call(
        functools.partial(conv_kernel, (rows, columns)),
        out_shape=(
            jax.ShapeDtypeStruct(cells, jnp.bfloat16),
            jax.ShapeDtypeStruct(hidden, jnp.bfloat16),
        ),
        in_specs=[pl.BlockSpec(memory_space=pltpu.SMEM)]
        + [vmem] * 7
        + [pl.BlockSpec(memory_space=pl.ANY)],
        out_specs=(vmem, pl.BlockSpec(memory_space=pl.ANY)),
        scratch_shapes=[
            pltpu.VMEM(weights, jnp.bfloat16),
            pltpu.VMEM(hidden, jnp.bfloat16),
            pltpu.VMEM((slots * half, LANES), jnp.float32),
            pltpu.VMEM((Z, EDGE) + share, jnp.bfloat16),
            pltpu.VMEM((8, slots), jnp.int32),
            pltpu.VMEM((rows, 8, slots), jnp.int32),
            pltpu.VMEM((EDGE, HALVES, rows) + share[1:], jnp.bfloat16),
            pltpu.VMEM((layers, EDGE + 2, PAIR, PAIR + 2, blocks + 2 * span, LANES), jnp.bfloat16),
            pltpu.VMEM(borders + (span, LANES), jnp.bfloat16),
            pltpu.VMEM((layers, EDGE + 2, 2, 2, span, LANES), jnp.bfloat16),
            pltpu.VMEM((layers, 2, 3, 2, 2 * LANES, 2 * LANES), jnp.bfloat16),
            pltpu.VMEM((layers, 2, 3, 2, LANES, 2 * LANES), jnp.bfloat16),
            pltpu.VMEM((EDGE, PAIR * blocks, 2 * LANES), jnp.float32),
            pltpu.VMEM((blocks, rows * slots), jnp.bfloat16),
            pltpu.VMEM((Z * slots, strips * blocks), jnp.bfloat16),
            pltpu.VMEM((EDGE, PAIR, strips, blocks, width), jnp.bfloat16),
            pltpu.VMEM((EDGE, PAIR, Z, slots, width), jnp.bfloat16),
            dma((rows,)),
            dma((rows,)),
            dma((EDGE, HALVES, Z)),
            dma((EDGE, HALVES, Z)),
            dma((EDGE, HALVES, Z, strips)),
            dma((EDGE, HALVES, Z, strips)),
            dma(halos),
            dma(halos),
            dma(borders),
            dma(borders),
            dma((EDGE, PAIR, strips)),
            dma((EDGE, PAIR, strips)),
            dma((EDGE, PAIR, Z)),
            dma((EDGE, PAIR, Z)),
            dma((2,)),
        ],
        compiler_params=pltpu.CompilerParams(collective_id=0, has_side_effects=True),
    )(
        slot_count,
        slot_dest.reshape(1, slots),
        slot_tile_block.reshape(1, slots),
        features,
        w_in,
        w_mid,
        frac,
        base,
        w_conv.reshape(weights),
    )


def per_device(
    features, w_in, w_mid, w_conv, point_frac, point_base, slot_dest, slot_tile_block, slot_count
):
    cells, hidden = exchange_and_convolve(
        features, w_in, w_mid, w_conv, point_frac, point_base, slot_dest, slot_tile_block, slot_count
    )
    return interpolate(cells, hidden, point_frac, point_base, slot_count)


def solution(mesh):
    return jax.shard_map(
        per_device,
        mesh=mesh,
        in_specs=(
            P(None, ("pts", "grid")),
            P(),
            P(),
            P(),
            P(None, ("pts", "grid")),
            P(None, ("pts", "grid")),
            P(("pts", "grid")),
            P(("pts", "grid")),
            P(("pts", "grid")),
        ),
        out_specs=P(None, ("pts", "grid")),
        check_vma=False,
    )
```

```python
import functools

import jax
import jax.numpy as jnp
from jax import lax
from jax.experimental import pallas as pl
from jax.experimental.pallas import tpu as pltpu
from jax.sharding import PartitionSpec as P

GZ = 8
EDGE = 4
TX = 32
TY = 32
LANES = 128
PAIR = 2
Z = GZ // PAIR
GROUP = 16
HALVES = 2
MESH = pl.DeviceIdType.MESH
LEVELS = ((1, 2), (0, 3))
ORDER = (3, 0, 1, 2)
OUT_ORDER = (0, 3, 1, 2)


def silu(total):
    return (total / (1.0 + jnp.exp(-total))).astype(jnp.bfloat16)


def point_layer(weight, inputs):
    return silu(
        lax.dot_general(
            weight, inputs, (((0,), (0,)), ((), ())), preferred_element_type=jnp.float32
        )
    )


def slot_weights(offsets, corners, count):
    width = offsets.shape[1]
    ranks = lax.broadcasted_iota(jnp.int32, (GZ, width), 0)
    live = lax.broadcasted_iota(jnp.int32, (GZ, width), 1) < count

    def axis(position, offset, corner):
        below_part = jnp.where(position == corner, 1.0 - offset, 0.0)
        above_part = jnp.where(position == corner + 1, offset, 0.0)
        return below_part + above_part

    first = ranks < EDGE
    along_xy = axis(
        lax.rem(ranks, EDGE),
        jnp.where(first, offsets[0:1], offsets[1:2]),
        jnp.where(first, corners[0:1], corners[1:2]),
    )
    along_z = jnp.where(live, axis(ranks, offsets[2:3], corners[2:3]), 0.0)
    rows = []
    for parity in range(PAIR):
        for i in range(EDGE):
            for jp in range(EDGE // PAIR):
                j = EDGE + jp * PAIR + parity
                rows.append(along_xy[i : i + 1] * along_xy[j : j + 1] * along_z)
    return jnp.concatenate(rows, axis=0).astype(jnp.bfloat16)


def splat_slots(
    part,
    count_ref,
    features_ref,
    w_in_ref,
    w_mid_ref,
    frac_ref,
    base_ref,
    hidden_ref,
    weight_ref,
    swap_ref,
):
    slots = count_ref.shape[0]
    width = hidden_ref.shape[1] // slots
    half = EDGE * EDGE // PAIR * GZ

    def one(g, carry):
        first = g * GROUP
        points = pl.ds(pl.multiple_of(first * width, GROUP * width), GROUP * width)
        hidden_one = point_layer(w_in_ref[...], features_ref[:, points])
        hidden_two = point_layer(w_mid_ref[...], hidden_one)
        hidden_ref[:, points] = hidden_two
        offsets, corners = frac_ref[:, points], base_ref[:, points]
        for s in range(GROUP):
            part = slice(s * width, (s + 1) * width)
            weights = slot_weights(offsets[:, part], corners[:, part], count_ref[first + s])
            weight_ref[first + s] = weights
            sums = lax.dot_general(
                weights,
                hidden_two[:, part],
                (((1,), (1,)), ((), ())),
                preferred_element_type=jnp.float32,
            )
            rows = pl.ds(pl.multiple_of((first + s) * half, half), half)
            swap_ref[rows] = jnp.concatenate([sums[:half], sums[half:]], axis=1)
        return carry

    steps = slots // (GROUP * HALVES)
    lax.fori_loop(part * steps, (part + 1) * steps, one, 0)


def swap_phase(i, part, swap_ref, sums_ref):
    slots = sums_ref.shape[3]
    half = EDGE * EDGE // PAIR * GZ
    for jp in range(PAIR):
        for z in range(GZ):
            row = (i * PAIR + jp) * GZ + z
            low = (jp * PAIR + z % PAIR) * LANES
            sums_ref[z // PAIR, i, part, :, low : low + LANES] = swap_ref[
                pl.ds(part * slots * half + row, slots, stride=half)
            ].astype(jnp.bfloat16)


def unswap_piece(i, jp, cells_ref, swap_ref):
    slots = cells_ref.shape[3]
    for z in range(GZ):
        row = (i * PAIR + jp) * GZ + z
        low = z % PAIR * LANES
        swap_ref[row * slots : (row + 1) * slots] = cells_ref[
            z // PAIR, i, jp, :, low : low + LANES
        ].astype(jnp.float32)


def interpolate_slot(s, slots, swap_ref, weight_ref, hidden_ref):
    width = hidden_ref.shape[1] // slots
    channels = hidden_ref.shape[0]
    half = EDGE * EDGE // PAIR * GZ
    points = slice(s * width, (s + 1) * width)
    cells = swap_ref[pl.ds(s, half, stride=slots)].T
    cells = jnp.concatenate([cells[:channels], cells[channels:]], axis=1).astype(jnp.bfloat16)
    interp = jnp.dot(cells, weight_ref[s], preferred_element_type=jnp.float32).astype(jnp.bfloat16)
    hidden_ref[:, points] = (
        hidden_ref[:, points].astype(jnp.float32) + interp.astype(jnp.float32)
    ).astype(jnp.bfloat16)


def build_band(w_ref, band_ref, side_ref):
    channels = w_ref.shape[1]
    width = PAIR * channels

    def one(n, carry):
        layer, a = lax.div(n, 3), lax.rem(n, 3)
        band_ref[layer, :, a] = jnp.zeros(band_ref.shape[1:2] + band_ref.shape[3:], band_ref.dtype)
        side_ref[layer, :, a] = jnp.zeros(side_ref.shape[1:2] + side_ref.shape[3:], side_ref.dtype)
        for part, levels in enumerate(LEVELS):
            for slot, zl in enumerate(levels):
                for zz in range(PAIR):
                    e = zl - zz
                    if not 0 <= e <= 2:
                        continue
                    for source, row in ((0, 0), (1, 1), (2, 2), (-1, 3)):
                        for target in range(PAIR):
                            b = source - target + 1
                            if not 0 <= b <= 2:
                                continue
                            rows = slice(row * channels, (row + 1) * channels)
                            lanes = zz * width + target * channels
                            lanes = slice(lanes, lanes + channels)
                            block = w_ref[n * 9 + b * 3 + e]
                            band_ref[layer, part, a, slot, rows, lanes] = block
                            if source in (-1, 2):
                                rows = slice(slot * channels, (slot + 1) * channels)
                                side_ref[layer, max(source, 0) // 2, a, part, rows, lanes] = block
        return carry

    lax.fori_loop(0, band_ref.shape[0] * 3, one, 0)


def conv_kernel(
    sizes,
    count_ref,
    dest_ref,
    block_ref,
    features_ref,
    w_in_ref,
    w_mid_ref,
    frac_ref,
    base_ref,
    w_hbm,
    out_hbm,
    w_ref,
    hidden_ref,
    weight_ref,
    swap_ref,
    out_ref,
    sums_ref,
    own_ids,
    ids,
    arrived,
    field,
    edge_out,
    edge_in,
    band_ref,
    side_ref,
    totals,
    sum_picks,
    out_picks,
    dense,
    values,
    id_send,
    id_recv,
    z_send,
    z_recv,
    x_send,
    x_recv,
    halo_send,
    halo_recv,
    edge_send,
    edge_recv,
    rx_send,
    rx_recv,
    rz_send,
    rz_recv,
    local_sem,
):
    rows, columns = sizes
    strips = rows // Z
    blocks = dense.shape[3]
    slots = values.shape[3]
    share = sums_ref.shape[3]
    span = (field.shape[4] - blocks) // 2
    layers = field.shape[0]
    me_row, me_column = lax.axis_index("grid"), lax.axis_index("pts")
    me_z, me_x = lax.div(me_row, strips), lax.rem(me_row, strips)
    inner = pl.ds(span, blocks)

    def snake(column, x):
        return x + lax.rem(column, 2) * (strips - 1 - 2 * x)

    me_strip = snake(me_column, me_x)

    def beside(ds):
        strip = me_column * strips + me_strip + ds
        present = (strip >= 0) & (strip < columns * strips)
        column = lax.div(strip + strips, strips) - 1
        x = snake(column + 2, lax.rem(strip + strips, strips))
        return present, column, me_z * strips + x

    def above(dz):
        return (me_z + dz >= 0) & (me_z + dz < Z)

    def tell(t):
        return pltpu.make_async_remote_copy(
            src_ref=own_ids,
            dst_ref=ids.at[me_row],
            send_sem=id_send.at[t],
            recv_sem=id_recv.at[t],
            device_id=(me_column, lax.rem(me_row + t, rows)),
            device_id_type=MESH,
        )

    def along_z(i, h, t):
        z = lax.rem(me_z + t, Z)
        return pltpu.make_async_remote_copy(
            src_ref=sums_ref.at[z, i, h],
            dst_ref=arrived.at[i, h, me_row],
            send_sem=z_send.at[i, h, t],
            recv_sem=z_recv.at[i, h, t],
            device_id=(me_column, z * strips + me_x),
            device_id_type=MESH,
        )

    def along_x(i, h, t, u):
        origin = lax.rem(me_z - t + Z, Z) * strips + me_x
        return pltpu.make_async_remote_copy(
            src_ref=sums_ref.at[me_z, i, h] if t == 0 else arrived.at[i, h, origin],
            dst_ref=arrived.at[i, h, origin],
            send_sem=x_send.at[i, h, t, u],
            recv_sem=x_recv.at[i, h, t, u],
            device_id=(me_column, me_z * strips + lax.rem(me_x + u, strips)),
            device_id_type=MESH,
        )

    def halo(layer, i, k):
        dz = (1, -1)[k]
        return pltpu.make_async_remote_copy(
            src_ref=field.at[layer, i + 1, :, 2 - k, inner],
            dst_ref=field.at[layer, i + 1, :, 3 * k, inner],
            send_sem=halo_send.at[layer, i, k],
            recv_sem=halo_recv.at[layer, i, k],
            device_id=(me_column, (me_z + dz) * strips + me_x),
            device_id_type=MESH,
        )

    def border(layer, i, part, side):
        _, column, row = beside((1, -1)[side])
        return pltpu.make_async_remote_copy(
            src_ref=edge_out.at[layer, i, side, part],
            dst_ref=edge_in.at[layer, i + 1, side, part],
            send_sem=edge_send.at[layer, i, part, side],
            recv_sem=edge_recv.at[layer, i, part, side],
            device_id=(column, row),
            device_id_type=MESH,
        )

    def back_x(i, jp, u):
        return pltpu.make_async_remote_copy(
            src_ref=dense.at[i, jp, me_strip],
            dst_ref=dense.at[i, jp, me_strip],
            send_sem=rx_send.at[i, jp, u],
            recv_sem=rx_recv.at[i, jp, u],
            device_id=(me_column, me_z * strips + lax.rem(me_x + u, strips)),
            device_id_type=MESH,
        )

    def back_z(i, jp, t):
        z = lax.rem(me_z + t, Z)
        return pltpu.make_async_remote_copy(
            src_ref=values.at[i, jp, z],
            dst_ref=out_ref.at[me_z, i, jp],
            send_sem=rz_send.at[i, jp, t],
            recv_sem=rz_recv.at[i, jp, t],
            device_id=(me_column, z * strips + me_x),
            device_id_type=MESH,
        )

    low_half = lax.broadcasted_iota(jnp.int32, (blocks, LANES), 1) < LANES // PAIR

    def send_border(layer, i, part):
        first, second = LEVELS[part]
        for side in range(2):
            rows = slice(blocks, blocks + span) if side == 0 else slice(span, 2 * span)
            view = field.at[layer, i + 1, 1 - side]
            tiles = [view[first, rows], view[second, rows]]
            tiles[side] = pltpu.roll(tiles[side].astype(jnp.float32), LANES // PAIR, 1).astype(
                jnp.bfloat16
            )
            edge_out[layer, i, side, part] = jnp.where(low_half[:span], tiles[0], tiles[1])

            @pl.when(beside((1, -1)[side])[0])
            def _():
                border(layer, i, part, side).start()

    def wait_border(layer, i):
        for side in range(2):

            @pl.when(beside((-1, 1)[side])[0])
            def _():
                for part in range(2):
                    border(layer, i, part, side).wait_recv()

    barrier = pltpu.get_barrier_semaphore()
    for t in range(1, rows):
        pl.semaphore_signal(
            barrier,
            inc=1,
            device_id=(me_column, lax.rem(me_row + t, rows)),
            device_id_type=MESH,
        )
    expected = rows - 1
    for ds in (-1, 1):
        present, column, row = beside(ds)
        other = present & (column != me_column)
        expected = expected + other.astype(jnp.int32)

        @pl.when(other)
        def _():
            pl.semaphore_signal(barrier, inc=1, device_id=(column, row), device_id_type=MESH)

    load = pltpu.make_async_copy(w_hbm, w_ref, local_sem.at[0])
    load.start()
    block = block_ref[...]
    along, across = TX // EDGE, TY // EDGE
    number = lax.rem(block, across) * span + dest_ref[...] * along + lax.div(block, across)
    own_ids[...] = jnp.broadcast_to(number, own_ids.shape)
    ids[me_row] = own_ids[...]
    for h in range(HALVES):
        splat_slots(
            h,
            count_ref,
            features_ref,
            w_in_ref,
            w_mid_ref,
            frac_ref,
            base_ref,
            hidden_ref,
            weight_ref,
            swap_ref,
        )
        if h == 0:
            pl.semaphore_wait(barrier, expected)
            for t in range(1, rows):
                tell(t).start()
        for i in ORDER:
            swap_phase(i, h, swap_ref, sums_ref)
            for t in (2, 1, 3):
                along_z(i, h, t).start()
            for u in range(1, strips):
                along_x(i, h, 0, u).start()
            arrived[i, h, me_row] = sums_ref[me_z, i, h]
    for k in range(2):

        @pl.when(jnp.logical_not(above((-1, 1)[k])))
        def _():
            view = field.at[:, 1 : EDGE + 1, :, 3 * k, inner]
            view[...] = jnp.zeros(view.shape, field.dtype)

        @pl.when(jnp.logical_not(beside((-1, 1)[k])[0]))
        def _():
            view = edge_in.at[:, 1 : EDGE + 1, k]
            view[...] = jnp.zeros(view.shape, edge_in.dtype)

    for jp, rows_out in ((0, slice(span + blocks, 2 * span + blocks)), (1, slice(0, span))):
        view = field.at[:, :, jp, :, rows_out]
        view[...] = jnp.zeros(view.shape, field.dtype)
    def picks(r, first, size):
        named = jnp.broadcast_to(ids[r, 0:1, :slots], (size, slots))
        place_of = lax.broadcasted_iota(jnp.int32, (size, slots), 0) + first
        return jnp.where(named == place_of, 1.0, 0.0)

    def build_picks():
        for t in range(1, rows):
            tell(t).wait_recv()
        for r in range(rows):
            one_hot = picks(r, me_strip * blocks, blocks).astype(jnp.bfloat16)
            for h in range(HALVES):
                low = (h * rows + r) * share
                sum_picks[:, low : low + share] = one_hot[:, h * share : (h + 1) * share]
        for z in range(Z):
            out_picks[z * slots : (z + 1) * slots] = picks(
                z * strips + me_x, 0, strips * blocks
            ).T.astype(jnp.bfloat16)

    def forward(i, h):
        for t in (1, 2, 3):
            along_z(i, h, t).wait_recv()
            for u in range(1, strips):
                along_x(i, h, t, u).start()

    def spread(layer, i, tiles):
        for jp in range(PAIR):
            for zz in range(PAIR):
                field[layer, i + 1, jp, 1 + zz, inner] = tiles(jp, zz)
        for k in range(2):

            @pl.when(above((1, -1)[k]))
            def _():
                halo(layer, i, k).start()

        send_border(layer, i, 0)

    def gather(i):
        for h in range(HALVES):
            for t in range(Z):
                for u in range(1, strips):
                    along_x(i, h, t, u).wait_recv()
        summed = jnp.dot(
            sum_picks[...],
            arrived[i].reshape(rows * slots, arrived.shape[4]),
            preferred_element_type=jnp.float32,
        ).astype(jnp.bfloat16)

        def tiles(jp, zz):
            low = (jp * PAIR + zz) * LANES
            return summed[:, low : low + LANES]

        spread(0, i, tiles)

    def shifted(tile, down):
        size = tile.shape[0]
        ranks = lax.broadcasted_iota(jnp.int32, tile.shape, 0)
        keep = lax.rem(ranks, span) != (0 if down else span - 1)
        moved = pltpu.roll(tile.astype(jnp.float32), 1 if down else size - 1, 0)
        return jnp.where(keep, moved, 0.0).astype(jnp.bfloat16)

    def shift(layer, i, levels):
        for down, phase, target in ((True, EDGE - 1, 0), (False, 0, EDGE + 1)):
            if phase == i:
                for jp in range(PAIR):
                    for zl in levels:
                        view = field.at[layer, :, jp, zl]
                        view[target, inner] = shifted(view[i + 1, inner], down)

    def shift_edges(layer, i):
        for down, phase, target in ((True, EDGE - 1, 0), (False, 0, EDGE + 1)):
            if phase == i:
                for side in range(2):
                    for part in range(2):
                        view = edge_in.at[layer, :, side, part]
                        view[target] = shifted(view[i + 1], down)

    def windows(layer, i, jp, levels, taps):
        parts = []
        for a in taps:
            for zl in levels:
                here = field.at[layer, i + a, :, zl]
                parts.append(here[jp, inner])
                if jp == 0:
                    up, down = here[1, inner], here[1, 0:blocks]
                else:
                    up, down = here[0, 2 * span : 2 * span + blocks], here[0, inner]
                parts.append(jnp.where(low_half, up, down))
        return jnp.concatenate(parts, axis=1)

    def conv_terms(layer, i, part, taps):
        depth = band_ref.shape[5]
        weight = jnp.concatenate(
            [band_ref[layer, part, a].reshape(-1, depth) for a in taps], axis=0
        )
        lhs = jnp.concatenate(
            [windows(layer, i, jp, LEVELS[part], taps) for jp in range(PAIR)], axis=0
        )
        return jnp.dot(lhs, weight, preferred_element_type=jnp.float32)

    def own_terms(layer, i):
        totals[i] = conv_terms(layer, i, 0, range(3))

    def edge_terms(layer, i):
        for side in range(2):
            lhs = jnp.concatenate(
                [edge_in[layer, i + a, side, part] for a in range(3) for part in range(2)], axis=1
            )
            weight = side_ref[layer, side].reshape(-1, side_ref.shape[5])
            rows_in = slice(0, span) if side == 0 else slice(2 * blocks - span, 2 * blocks)
            totals[i, rows_in] += jnp.dot(lhs, weight, preferred_element_type=jnp.float32)

    def finish(layer, i):
        total = totals[i]
        activated = silu(total)

        def tiles(jp, zz):
            return activated[jp * blocks : (jp + 1) * blocks, zz * LANES : (zz + 1) * LANES]

        if layer < layers - 1:
            spread(layer + 1, i, tiles)
            shift(layer + 1, i, LEVELS[0])
        else:
            for jp in range(PAIR):
                dense[i, jp, me_strip] = activated[jp * blocks : (jp + 1) * blocks]
                for u in range(1, strips):
                    back_x(i, jp, u).start()

    def near(i):
        return ((i - 1) % EDGE, i, (i + 1) % EDGE)

    for h in range(HALVES):
        for n, i in enumerate(ORDER):
            forward(i, h)
            if h == 0 and n == 0:
                build_picks()
            if h == 0 and n == 1:
                load.wait()
                build_band(w_ref, band_ref, side_ref)
            if h == HALVES - 1 and n > 0:
                gather(ORDER[n - 1])
                shift(0, ORDER[n - 1], LEVELS[0])
    for i in OUT_ORDER:
        if ORDER[-1] not in near(i):
            own_terms(0, i)
    gather(ORDER[-1])
    shift(0, ORDER[-1], LEVELS[0])
    for i in OUT_ORDER:
        if ORDER[-1] in near(i):
            own_terms(0, i)

    for layer in range(layers):
        before = ORDER if layer == 0 else OUT_ORDER
        if layer > 0:
            for i in OUT_ORDER:
                own_terms(layer, i)
        bordered = []

        def reach(phase):
            for k in range(2):

                @pl.when(above((-1, 1)[k]))
                def _():
                    halo(layer, phase, k).wait_recv()

            send_border(layer, phase, 1)
            shift(layer, phase, LEVELS[1])

        def add_terms(i, phases):
            taps = [a for a in range(3) if near(i)[a] in phases]
            totals[i] += conv_terms(layer, i, 1, taps)

        def close(i):
            for phase in before:
                if phase in near(i) and phase not in bordered:
                    wait_border(layer, phase)
                    shift_edges(layer, phase)
                    bordered.append(phase)
            edge_terms(layer, i)
            finish(layer, i)

        reached = []
        for n, i in enumerate(OUT_ORDER):
            for phase in before:
                if phase in near(i) and phase not in reached:
                    reach(phase)
                    reached.append(phase)
            add_terms(i, before)
            if n > 0:
                close(OUT_ORDER[n - 1])
        close(OUT_ORDER[-1])

    for i in OUT_ORDER:
        for jp in range(PAIR):
            for u in range(1, strips):
                back_x(i, jp, u).wait_recv()
            picked = jnp.dot(
                out_picks[...],
                dense[i, jp].reshape(strips * blocks, dense.shape[4]),
                preferred_element_type=jnp.float32,
            ).astype(jnp.bfloat16)
            values[i, jp] = picked.reshape(values.shape[2:])
            for t in (2, 1, 3):
                back_z(i, jp, t).start()
            out_ref[me_z, i, jp] = values[i, jp, me_z]

    for i in OUT_ORDER:
        for jp in range(PAIR):
            for t in (1, 2, 3):
                back_z(i, jp, t).wait_recv()
            unswap_piece(i, jp, out_ref, swap_ref)

    def keep(g):
        width = hidden_ref.shape[1] * GROUP // slots
        points = slice(g * width, (g + 1) * width)
        return pltpu.make_async_copy(
            hidden_ref.at[:, points], out_hbm.at[:, points], local_sem.at[1 + g]
        )

    for g in range(slots // GROUP):
        for s in range(g * GROUP, (g + 1) * GROUP):
            interpolate_slot(s, slots, swap_ref, weight_ref, hidden_ref)
        keep(g).start()
    for g in range(slots // GROUP):
        keep(g).wait()
    for t in range(1, rows):
        tell(t).wait_send()
    for i in range(EDGE):
        for jp in range(PAIR):
            for t in (1, 2, 3):
                back_z(i, jp, t).wait_send()
            for u in range(1, strips):
                back_x(i, jp, u).wait_send()
        for h in range(HALVES):
            for t in (1, 2, 3):
                along_z(i, h, t).wait_send()
            for u in range(1, strips):
                for t in range(Z):
                    along_x(i, h, t, u).wait_send()
        for layer in range(layers):
            for k in range(2):

                @pl.when(above((1, -1)[k]))
                def _():
                    halo(layer, i, k).wait_send()

                @pl.when(beside((1, -1)[k])[0])
                def _():
                    for part in range(2):
                        border(layer, i, part, k).wait_send()


def exchange_and_convolve(
    features, w_in, w_mid, w_conv, frac, base, slot_dest, slot_tile_block, slot_count
):
    rows, columns = lax.axis_size("grid"), lax.axis_size("pts")
    strips = rows // Z
    slots = slot_count.shape[0]
    layers, channels = w_conv.shape[0], w_conv.shape[4]
    width = PAIR * PAIR * channels
    span = rows * (TX // EDGE)
    blocks = span * (TY // EDGE) // strips
    half = EDGE * EDGE // PAIR * GZ
    hidden = (channels, features.shape[1])
    cells = (Z, EDGE, PAIR, slots, width)
    weights = (layers * 27, channels, channels)
    share = (HALVES, slots // HALVES, PAIR * width)
    halos = (layers, EDGE, 2)
    borders = halos + (2,)
    dma = pltpu.SemaphoreType.DMA
    vmem = pl.BlockSpec(memory_space=pltpu.VMEM)
    return pl.pallas_call(
        functools.partial(conv_kernel, (rows, columns)),
        out_shape=jax.ShapeDtypeStruct(hidden, jnp.bfloat16),
        in_specs=[pl.BlockSpec(memory_space=pltpu.SMEM)]
        + [vmem] * 7
        + [pl.BlockSpec(memory_space=pl.ANY)],
        out_specs=pl.BlockSpec(memory_space=pl.ANY),
        scratch_shapes=[
            pltpu.VMEM(weights, jnp.bfloat16),
            pltpu.VMEM(hidden, jnp.bfloat16),
            pltpu.VMEM((slots, PAIR * half, hidden[1] // slots), jnp.bfloat16),
            pltpu.VMEM((slots * half, LANES), jnp.float32),
            pltpu.VMEM(cells, jnp.bfloat16),
            pltpu.VMEM((Z, EDGE) + share, jnp.bfloat16),
            pltpu.VMEM((8, slots), jnp.int32),
            pltpu.VMEM((rows, 8, slots), jnp.int32),
            pltpu.VMEM((EDGE, HALVES, rows) + share[1:], jnp.bfloat16),
            pltpu.VMEM((layers, EDGE + 2, PAIR, PAIR + 2, blocks + 2 * span, LANES), jnp.bfloat16),
            pltpu.VMEM(borders + (span, LANES), jnp.bfloat16),
            pltpu.VMEM((layers, EDGE + 2, 2, 2, span, LANES), jnp.bfloat16),
            pltpu.VMEM((layers, 2, 3, 2, 2 * LANES, 2 * LANES), jnp.bfloat16),
            pltpu.VMEM((layers, 2, 3, 2, LANES, 2 * LANES), jnp.bfloat16),
            pltpu.VMEM((EDGE, PAIR * blocks, 2 * LANES), jnp.float32),
            pltpu.VMEM((blocks, rows * slots), jnp.bfloat16),
            pltpu.VMEM((Z * slots, strips * blocks), jnp.bfloat16),
            pltpu.VMEM((EDGE, PAIR, strips, blocks, width), jnp.bfloat16),
            pltpu.VMEM((EDGE, PAIR, Z, slots, width), jnp.bfloat16),
            dma((rows,)),
            dma((rows,)),
            dma((EDGE, HALVES, Z)),
            dma((EDGE, HALVES, Z)),
            dma((EDGE, HALVES, Z, strips)),
            dma((EDGE, HALVES, Z, strips)),
            dma(halos),
            dma(halos),
            dma(borders),
            dma(borders),
            dma((EDGE, PAIR, strips)),
            dma((EDGE, PAIR, strips)),
            dma((EDGE, PAIR, Z)),
            dma((EDGE, PAIR, Z)),
            dma((1 + slots // GROUP,)),
        ],
        compiler_params=pltpu.CompilerParams(
            collective_id=0, has_side_effects=True, vmem_limit_bytes=52 << 20
        ),
    )(
        *(
            pltpu.with_memory_space_constraint(operand, pltpu.HBM)
            for operand in (
                slot_count,
                slot_dest.reshape(1, slots),
                slot_tile_block.reshape(1, slots),
                features,
                w_in,
                w_mid,
                frac,
                base,
                w_conv.reshape(weights),
            )
        )
    )


def solution(mesh):
    return jax.shard_map(
        exchange_and_convolve,
        mesh=mesh,
        in_specs=(
            P(None, ("pts", "grid")),
            P(),
            P(),
            P(),
            P(None, ("pts", "grid")),
            P(None, ("pts", "grid")),
            P(("pts", "grid")),
            P(("pts", "grid")),
            P(("pts", "grid")),
        ),
        out_specs=P(None, ("pts", "grid")),
        check_vma=False,
    )
```

```python
import functools

import jax
import jax.numpy as jnp
from jax import lax
from jax.experimental import pallas as pl
from jax.experimental.pallas import tpu as pltpu
from jax.sharding import PartitionSpec as P

GZ = 8
EDGE = 4
TX = 32
TY = 32
LANES = 128
PAIR = 2
Z = GZ // PAIR
GROUP = 16
HALVES = 2
MESH = pl.DeviceIdType.MESH
LEVELS = ((1, 2), (0, 3))
ORDER = (3, 0, 1, 2)
OUT_ORDER = (0, 3, 1, 2)


def silu(total):
    return (total / (1.0 + jnp.exp(-total))).astype(jnp.bfloat16)


def point_layer(weight, inputs):
    return silu(
        lax.dot_general(
            weight, inputs, (((0,), (0,)), ((), ())), preferred_element_type=jnp.float32
        )
    )


def slot_weights(offsets, corners, count):
    width = offsets.shape[1]
    ranks = lax.broadcasted_iota(jnp.int32, (GZ, width), 0)
    live = lax.broadcasted_iota(jnp.int32, (GZ, width), 1) < count

    def axis(position, offset, corner):
        below_part = jnp.where(position == corner, 1.0 - offset, 0.0)
        above_part = jnp.where(position == corner + 1, offset, 0.0)
        return below_part + above_part

    first = ranks < EDGE
    along_xy = axis(
        lax.rem(ranks, EDGE),
        jnp.where(first, offsets[0:1], offsets[1:2]),
        jnp.where(first, corners[0:1], corners[1:2]),
    )
    along_z = jnp.where(live, axis(ranks, offsets[2:3], corners[2:3]), 0.0)
    rows = []
    for parity in range(PAIR):
        for i in range(EDGE):
            for jp in range(EDGE // PAIR):
                j = EDGE + jp * PAIR + parity
                rows.append(along_xy[i : i + 1] * along_xy[j : j + 1] * along_z)
    return jnp.concatenate(rows, axis=0).astype(jnp.bfloat16)


def splat_slots(
    part,
    count_ref,
    features_ref,
    w_in_ref,
    w_mid_ref,
    frac_ref,
    base_ref,
    hidden_ref,
    weight_ref,
    swap_ref,
):
    slots = count_ref.shape[0]
    width = hidden_ref.shape[1] // slots
    half = EDGE * EDGE // PAIR * GZ

    def one(g, carry):
        first = g * GROUP
        points = pl.ds(pl.multiple_of(first * width, GROUP * width), GROUP * width)
        hidden_one = point_layer(w_in_ref[...], features_ref[:, points])
        hidden_two = point_layer(w_mid_ref[...], hidden_one)
        hidden_ref[:, points] = hidden_two
        offsets, corners = frac_ref[:, points], base_ref[:, points]
        for s in range(GROUP):
            part = slice(s * width, (s + 1) * width)
            weights = slot_weights(offsets[:, part], corners[:, part], count_ref[first + s])
            weight_ref[first + s] = weights
            sums = lax.dot_general(
                weights,
                hidden_two[:, part],
                (((1,), (1,)), ((), ())),
                preferred_element_type=jnp.float32,
            )
            rows = pl.ds(pl.multiple_of((first + s) * half, half), half)
            swap_ref[rows] = jnp.concatenate([sums[:half], sums[half:]], axis=1)
        return carry

    steps = slots // (GROUP * HALVES)
    lax.fori_loop(part * steps, (part + 1) * steps, one, 0)


def swap_phase(i, part, swap_ref, sums_ref):
    slots = sums_ref.shape[3]
    half = EDGE * EDGE // PAIR * GZ
    for jp in range(PAIR):
        for z in range(GZ):
            row = (i * PAIR + jp) * GZ + z
            low = (jp * PAIR + z % PAIR) * LANES
            sums_ref[z // PAIR, i, part, :, low : low + LANES] = swap_ref[
                pl.ds(part * slots * half + row, slots, stride=half)
            ].astype(jnp.bfloat16)


def unswap_piece(i, jp, cells_ref, swap_ref):
    slots = cells_ref.shape[3]
    for z in range(GZ):
        row = (i * PAIR + jp) * GZ + z
        low = z % PAIR * LANES
        swap_ref[row * slots : (row + 1) * slots] = cells_ref[
            z // PAIR, i, jp, :, low : low + LANES
        ].astype(jnp.float32)


def interpolate_slot(s, slots, swap_ref, weight_ref, hidden_ref):
    width = hidden_ref.shape[1] // slots
    channels = hidden_ref.shape[0]
    half = EDGE * EDGE // PAIR * GZ
    points = slice(s * width, (s + 1) * width)
    cells = swap_ref[pl.ds(s, half, stride=slots)].T
    cells = jnp.concatenate([cells[:channels], cells[channels:]], axis=1).astype(jnp.bfloat16)
    interp = jnp.dot(cells, weight_ref[s], preferred_element_type=jnp.float32).astype(jnp.bfloat16)
    hidden_ref[:, points] = (
        hidden_ref[:, points].astype(jnp.float32) + interp.astype(jnp.float32)
    ).astype(jnp.bfloat16)


def build_band(w_ref, band_ref, side_ref):
    channels = w_ref.shape[1]
    width = PAIR * channels

    def one(n, carry):
        layer, a = lax.div(n, 3), lax.rem(n, 3)
        band_ref[layer, :, a] = jnp.zeros(band_ref.shape[1:2] + band_ref.shape[3:], band_ref.dtype)
        side_ref[layer, :, a] = jnp.zeros(side_ref.shape[1:2] + side_ref.shape[3:], side_ref.dtype)
        for part, levels in enumerate(LEVELS):
            for slot, zl in enumerate(levels):
                for zz in range(PAIR):
                    e = zl - zz
                    if not 0 <= e <= 2:
                        continue
                    for source, row in ((0, 0), (1, 1), (2, 2), (-1, 3)):
                        for target in range(PAIR):
                            b = source - target + 1
                            if not 0 <= b <= 2:
                                continue
                            rows = slice(row * channels, (row + 1) * channels)
                            lanes = zz * width + target * channels
                            lanes = slice(lanes, lanes + channels)
                            block = w_ref[n * 9 + b * 3 + e]
                            band_ref[layer, part, a, slot, rows, lanes] = block
                            if source in (-1, 2):
                                rows = slice(slot * channels, (slot + 1) * channels)
                                side_ref[layer, max(source, 0) // 2, a, part, rows, lanes] = block
        return carry

    lax.fori_loop(0, band_ref.shape[0] * 3, one, 0)


def conv_kernel(
    sizes,
    count_ref,
    dest_ref,
    block_ref,
    features_ref,
    w_in_ref,
    w_mid_ref,
    frac_ref,
    base_ref,
    w_hbm,
    out_hbm,
    w_ref,
    hidden_ref,
    weight_ref,
    swap_ref,
    out_ref,
    sums_ref,
    own_ids,
    ids,
    arrived,
    field,
    edge_out,
    edge_in,
    band_ref,
    side_ref,
    totals,
    sum_picks,
    out_picks,
    dense,
    values,
    id_send,
    id_recv,
    z_send,
    z_recv,
    x_send,
    x_recv,
    halo_send,
    halo_recv,
    edge_send,
    edge_recv,
    rx_send,
    rx_recv,
    rz_send,
    rz_recv,
    local_sem,
):
    rows, columns = sizes
    strips = rows // Z
    blocks = dense.shape[3]
    slots = values.shape[3]
    share = sums_ref.shape[3]
    span = (field.shape[4] - blocks) // 2
    layers = field.shape[0]
    me_row, me_column = lax.axis_index("grid"), lax.axis_index("pts")
    me_z, me_x = lax.div(me_row, strips), lax.rem(me_row, strips)
    inner = pl.ds(span, blocks)

    def snake(column, x):
        return x + lax.rem(column, 2) * (strips - 1 - 2 * x)

    me_strip = snake(me_column, me_x)

    def beside(ds):
        strip = me_column * strips + me_strip + ds
        present = (strip >= 0) & (strip < columns * strips)
        column = lax.div(strip + strips, strips) - 1
        x = snake(column + 2, lax.rem(strip + strips, strips))
        return present, column, me_z * strips + x

    def above(dz):
        return (me_z + dz >= 0) & (me_z + dz < Z)

    def tell(t):
        return pltpu.make_async_remote_copy(
            src_ref=own_ids,
            dst_ref=ids.at[me_row],
            send_sem=id_send.at[t],
            recv_sem=id_recv.at[t],
            device_id=(me_column, lax.rem(me_row + t, rows)),
            device_id_type=MESH,
        )

    def along_z(i, h, t):
        z = lax.rem(me_z + t, Z)
        return pltpu.make_async_remote_copy(
            src_ref=sums_ref.at[z, i, h],
            dst_ref=arrived.at[i, h, me_row],
            send_sem=z_send.at[i, h, t],
            recv_sem=z_recv.at[i, h, t],
            device_id=(me_column, z * strips + me_x),
            device_id_type=MESH,
        )

    def along_x(i, h, t, u):
        origin = lax.rem(me_z - t + Z, Z) * strips + me_x
        return pltpu.make_async_remote_copy(
            src_ref=sums_ref.at[me_z, i, h] if t == 0 else arrived.at[i, h, origin],
            dst_ref=arrived.at[i, h, origin],
            send_sem=x_send.at[i, h, t, u],
            recv_sem=x_recv.at[i, h, t, u],
            device_id=(me_column, me_z * strips + lax.rem(me_x + u, strips)),
            device_id_type=MESH,
        )

    def halo(layer, i, k):
        dz = (1, -1)[k]
        return pltpu.make_async_remote_copy(
            src_ref=field.at[layer, i + 1, :, 2 - k, inner],
            dst_ref=field.at[layer, i + 1, :, 3 * k, inner],
            send_sem=halo_send.at[layer, i, k],
            recv_sem=halo_recv.at[layer, i, k],
            device_id=(me_column, (me_z + dz) * strips + me_x),
            device_id_type=MESH,
        )

    def border(layer, i, part, side):
        _, column, row = beside((1, -1)[side])
        return pltpu.make_async_remote_copy(
            src_ref=edge_out.at[layer, i, side, part],
            dst_ref=edge_in.at[layer, i + 1, side, part],
            send_sem=edge_send.at[layer, i, part, side],
            recv_sem=edge_recv.at[layer, i, part, side],
            device_id=(column, row),
            device_id_type=MESH,
        )

    def back_x(i, jp, u):
        return pltpu.make_async_remote_copy(
            src_ref=dense.at[i, jp, me_strip],
            dst_ref=dense.at[i, jp, me_strip],
            send_sem=rx_send.at[i, jp, u],
            recv_sem=rx_recv.at[i, jp, u],
            device_id=(me_column, me_z * strips + lax.rem(me_x + u, strips)),
            device_id_type=MESH,
        )

    def back_z(i, jp, t):
        z = lax.rem(me_z + t, Z)
        return pltpu.make_async_remote_copy(
            src_ref=values.at[i, jp, z],
            dst_ref=out_ref.at[me_z, i, jp],
            send_sem=rz_send.at[i, jp, t],
            recv_sem=rz_recv.at[i, jp, t],
            device_id=(me_column, z * strips + me_x),
            device_id_type=MESH,
        )

    low_half = lax.broadcasted_iota(jnp.int32, (blocks, LANES), 1) < LANES // PAIR

    def send_border(layer, i, part):
        first, second = LEVELS[part]
        for side in range(2):
            rows = slice(blocks, blocks + span) if side == 0 else slice(span, 2 * span)
            view = field.at[layer, i + 1, 1 - side]
            tiles = [view[first, rows], view[second, rows]]
            tiles[side] = pltpu.roll(tiles[side].astype(jnp.float32), LANES // PAIR, 1).astype(
                jnp.bfloat16
            )
            edge_out[layer, i, side, part] = jnp.where(low_half[:span], tiles[0], tiles[1])

            @pl.when(beside((1, -1)[side])[0])
            def _():
                border(layer, i, part, side).start()

    def wait_border(layer, i):
        for side in range(2):

            @pl.when(beside((-1, 1)[side])[0])
            def _():
                for part in range(2):
                    border(layer, i, part, side).wait_recv()

    barrier = pltpu.get_barrier_semaphore()
    for t in range(1, rows):
        pl.semaphore_signal(
            barrier,
            inc=1,
            device_id=(me_column, lax.rem(me_row + t, rows)),
            device_id_type=MESH,
        )
    expected = rows - 1
    for ds in (-1, 1):
        present, column, row = beside(ds)
        other = present & (column != me_column)
        expected = expected + other.astype(jnp.int32)

        @pl.when(other)
        def _():
            pl.semaphore_signal(barrier, inc=1, device_id=(column, row), device_id_type=MESH)

    load = pltpu.make_async_copy(w_hbm, w_ref, local_sem.at[0])
    load.start()
    block = block_ref[...]
    along, across = TX // EDGE, TY // EDGE
    number = lax.rem(block, across) * span + dest_ref[...] * along + lax.div(block, across)
    own_ids[...] = jnp.broadcast_to(number, own_ids.shape)
    ids[me_row] = own_ids[...]
    for h in range(HALVES):
        splat_slots(
            h,
            count_ref,
            features_ref,
            w_in_ref,
            w_mid_ref,
            frac_ref,
            base_ref,
            hidden_ref,
            weight_ref,
            swap_ref,
        )
        if h == 0:
            pl.semaphore_wait(barrier, expected)
            for t in range(1, rows):
                tell(t).start()
        for i in ORDER:
            swap_phase(i, h, swap_ref, sums_ref)
            for t in (2, 1, 3):
                along_z(i, h, t).start()
            for u in range(1, strips):
                along_x(i, h, 0, u).start()
            arrived[i, h, me_row] = sums_ref[me_z, i, h]
    for k in range(2):

        @pl.when(jnp.logical_not(above((-1, 1)[k])))
        def _():
            view = field.at[:, 1 : EDGE + 1, :, 3 * k, inner]
            view[...] = jnp.zeros(view.shape, field.dtype)

        @pl.when(jnp.logical_not(beside((-1, 1)[k])[0]))
        def _():
            view = edge_in.at[:, 1 : EDGE + 1, k]
            view[...] = jnp.zeros(view.shape, edge_in.dtype)

    for jp, rows_out in ((0, slice(span + blocks, 2 * span + blocks)), (1, slice(0, span))):
        view = field.at[:, :, jp, :, rows_out]
        view[...] = jnp.zeros(view.shape, field.dtype)
    def picks(r, first, size):
        named = jnp.broadcast_to(ids[r, 0:1, :slots], (size, slots))
        place_of = lax.broadcasted_iota(jnp.int32, (size, slots), 0) + first
        return jnp.where(named == place_of, 1.0, 0.0)

    def build_picks():
        for t in range(1, rows):
            tell(t).wait_recv()
        for r in range(rows):
            one_hot = picks(r, me_strip * blocks, blocks).astype(jnp.bfloat16)
            for h in range(HALVES):
                low = (h * rows + r) * share
                sum_picks[:, low : low + share] = one_hot[:, h * share : (h + 1) * share]
        for z in range(Z):
            out_picks[z * slots : (z + 1) * slots] = picks(
                z * strips + me_x, 0, strips * blocks
            ).T.astype(jnp.bfloat16)

    def forward(i, h):
        for t in (1, 2, 3):
            along_z(i, h, t).wait_recv()
            for u in range(1, strips):
                along_x(i, h, t, u).start()

    def spread(layer, i, tiles):
        for jp in range(PAIR):
            for zz in range(PAIR):
                field[layer, i + 1, jp, 1 + zz, inner] = tiles(jp, zz)
        for k in range(2):

            @pl.when(above((1, -1)[k]))
            def _():
                halo(layer, i, k).start()

        send_border(layer, i, 0)

    def gather(i):
        for h in range(HALVES):
            for t in range(Z):
                for u in range(1, strips):
                    along_x(i, h, t, u).wait_recv()
        summed = jnp.dot(
            sum_picks[...],
            arrived[i].reshape(rows * slots, arrived.shape[4]),
            preferred_element_type=jnp.float32,
        ).astype(jnp.bfloat16)

        def tiles(jp, zz):
            low = (jp * PAIR + zz) * LANES
            return summed[:, low : low + LANES]

        spread(0, i, tiles)

    def shifted(tile, down):
        size = tile.shape[0]
        ranks = lax.broadcasted_iota(jnp.int32, tile.shape, 0)
        keep = lax.rem(ranks, span) != (0 if down else span - 1)
        moved = pltpu.roll(tile.astype(jnp.float32), 1 if down else size - 1, 0)
        return jnp.where(keep, moved, 0.0).astype(jnp.bfloat16)

    def shift(layer, i, levels):
        for down, phase, target in ((True, EDGE - 1, 0), (False, 0, EDGE + 1)):
            if phase == i:
                for jp in range(PAIR):
                    for zl in levels:
                        view = field.at[layer, :, jp, zl]
                        view[target, inner] = shifted(view[i + 1, inner], down)

    def shift_edges(layer, i):
        for down, phase, target in ((True, EDGE - 1, 0), (False, 0, EDGE + 1)):
            if phase == i:
                for side in range(2):
                    for part in range(2):
                        view = edge_in.at[layer, :, side, part]
                        view[target] = shifted(view[i + 1], down)

    def windows(layer, i, jp, levels, taps):
        parts = []
        for a in taps:
            for zl in levels:
                here = field.at[layer, i + a, :, zl]
                parts.append(here[jp, inner])
                if jp == 0:
                    up, down = here[1, inner], here[1, 0:blocks]
                else:
                    up, down = here[0, 2 * span : 2 * span + blocks], here[0, inner]
                parts.append(jnp.where(low_half, up, down))
        return jnp.concatenate(parts, axis=1)

    def conv_terms(layer, i, part, taps):
        depth = band_ref.shape[5]
        weight = jnp.concatenate(
            [band_ref[layer, part, a].reshape(-1, depth) for a in taps], axis=0
        )
        lhs = jnp.concatenate(
            [windows(layer, i, jp, LEVELS[part], taps) for jp in range(PAIR)], axis=0
        )
        return jnp.dot(lhs, weight, preferred_element_type=jnp.float32)

    def own_terms(layer, i):
        totals[i] = conv_terms(layer, i, 0, range(3))

    def edge_terms(layer, i):
        for side in range(2):
            lhs = jnp.concatenate(
                [edge_in[layer, i + a, side, part] for a in range(3) for part in range(2)], axis=1
            )
            weight = side_ref[layer, side].reshape(-1, side_ref.shape[5])
            rows_in = slice(0, span) if side == 0 else slice(2 * blocks - span, 2 * blocks)
            totals[i, rows_in] += jnp.dot(lhs, weight, preferred_element_type=jnp.float32)

    def finish(layer, i):
        total = totals[i]
        activated = silu(total)

        def tiles(jp, zz):
            return activated[jp * blocks : (jp + 1) * blocks, zz * LANES : (zz + 1) * LANES]

        if layer < layers - 1:
            spread(layer + 1, i, tiles)
            shift(layer + 1, i, LEVELS[0])
        else:
            for jp in range(PAIR):
                dense[i, jp, me_strip] = activated[jp * blocks : (jp + 1) * blocks]
                for u in range(1, strips):
                    back_x(i, jp, u).start()

    def near(i):
        return ((i - 1) % EDGE, i, (i + 1) % EDGE)

    for h in range(HALVES):
        for n, i in enumerate(ORDER):
            forward(i, h)
            if h == 0 and n == 0:
                build_picks()
            if h == 0 and n == 1:
                load.wait()
                build_band(w_ref, band_ref, side_ref)
            if h == HALVES - 1 and n > 0:
                gather(ORDER[n - 1])
                shift(0, ORDER[n - 1], LEVELS[0])
    for i in OUT_ORDER:
        if ORDER[-1] not in near(i):
            own_terms(0, i)
    gather(ORDER[-1])
    shift(0, ORDER[-1], LEVELS[0])
    for i in OUT_ORDER:
        if ORDER[-1] in near(i):
            own_terms(0, i)

    for layer in range(layers):
        before = ORDER if layer == 0 else OUT_ORDER
        if layer > 0:
            for i in OUT_ORDER:
                own_terms(layer, i)
        bordered = []

        def reach(phase):
            for k in range(2):

                @pl.when(above((-1, 1)[k]))
                def _():
                    halo(layer, phase, k).wait_recv()

            send_border(layer, phase, 1)
            shift(layer, phase, LEVELS[1])

        def add_terms(i, phases):
            taps = [a for a in range(3) if near(i)[a] in phases]
            totals[i] += conv_terms(layer, i, 1, taps)

        def close(i):
            for phase in before:
                if phase in near(i) and phase not in bordered:
                    wait_border(layer, phase)
                    shift_edges(layer, phase)
                    bordered.append(phase)
            edge_terms(layer, i)
            finish(layer, i)

        reached = []
        for n, i in enumerate(OUT_ORDER):
            for phase in before:
                if phase in near(i) and phase not in reached:
                    reach(phase)
                    reached.append(phase)
            add_terms(i, before)
            if n > 0:
                close(OUT_ORDER[n - 1])
        close(OUT_ORDER[-1])

    for i in OUT_ORDER:
        for jp in range(PAIR):
            for u in range(1, strips):
                back_x(i, jp, u).wait_recv()
            picked = jnp.dot(
                out_picks[...],
                dense[i, jp].reshape(strips * blocks, dense.shape[4]),
                preferred_element_type=jnp.float32,
            ).astype(jnp.bfloat16)
            values[i, jp] = picked.reshape(values.shape[2:])
            for t in (2, 1, 3):
                back_z(i, jp, t).start()
            out_ref[me_z, i, jp] = values[i, jp, me_z]

    for i in OUT_ORDER:
        for jp in range(PAIR):
            for t in (1, 2, 3):
                back_z(i, jp, t).wait_recv()
            unswap_piece(i, jp, out_ref, swap_ref)

    def keep(g):
        width = hidden_ref.shape[1] * GROUP // slots
        points = slice(g * width, (g + 1) * width)
        return pltpu.make_async_copy(
            hidden_ref.at[:, points], out_hbm.at[:, points], local_sem.at[1 + g]
        )

    for g in range(slots // GROUP):
        for s in range(g * GROUP, (g + 1) * GROUP):
            interpolate_slot(s, slots, swap_ref, weight_ref, hidden_ref)
        keep(g).start()
    for g in range(slots // GROUP):
        keep(g).wait()
    for t in range(1, rows):
        tell(t).wait_send()
    for i in range(EDGE):
        for jp in range(PAIR):
            for t in (1, 2, 3):
                back_z(i, jp, t).wait_send()
            for u in range(1, strips):
                back_x(i, jp, u).wait_send()
        for h in range(HALVES):
            for t in (1, 2, 3):
                along_z(i, h, t).wait_send()
            for u in range(1, strips):
                for t in range(Z):
                    along_x(i, h, t, u).wait_send()
        for layer in range(layers):
            for k in range(2):

                @pl.when(above((1, -1)[k]))
                def _():
                    halo(layer, i, k).wait_send()

                @pl.when(beside((1, -1)[k])[0])
                def _():
                    for part in range(2):
                        border(layer, i, part, k).wait_send()


def exchange_and_convolve(
    features, w_in, w_mid, w_conv, frac, base, slot_dest, slot_tile_block, slot_count
):
    rows, columns = lax.axis_size("grid"), lax.axis_size("pts")
    strips = rows // Z
    slots = slot_count.shape[0]
    layers, channels = w_conv.shape[0], w_conv.shape[4]
    width = PAIR * PAIR * channels
    span = rows * (TX // EDGE)
    blocks = span * (TY // EDGE) // strips
    half = EDGE * EDGE // PAIR * GZ
    hidden = (channels, features.shape[1])
    cells = (Z, EDGE, PAIR, slots, width)
    weights = (layers * 27, channels, channels)
    share = (HALVES, slots // HALVES, PAIR * width)
    halos = (layers, EDGE, 2)
    borders = halos + (2,)
    dma = pltpu.SemaphoreType.DMA
    vmem = pl.BlockSpec(memory_space=pltpu.VMEM)
    return pl.pallas_call(
        functools.partial(conv_kernel, (rows, columns)),
        out_shape=jax.ShapeDtypeStruct(hidden, jnp.bfloat16),
        in_specs=[pl.BlockSpec(memory_space=pltpu.SMEM)]
        + [vmem] * 7
        + [pl.BlockSpec(memory_space=pl.ANY)],
        out_specs=pl.BlockSpec(memory_space=pl.ANY),
        scratch_shapes=[
            pltpu.VMEM(weights, jnp.bfloat16),
            pltpu.VMEM(hidden, jnp.bfloat16),
            pltpu.VMEM((slots, PAIR * half, hidden[1] // slots), jnp.bfloat16),
            pltpu.VMEM((slots * half, LANES), jnp.float32),
            pltpu.VMEM(cells, jnp.bfloat16),
            pltpu.VMEM((Z, EDGE) + share, jnp.bfloat16),
            pltpu.VMEM((8, slots), jnp.int32),
            pltpu.VMEM((rows, 8, slots), jnp.int32),
            pltpu.VMEM((EDGE, HALVES, rows) + share[1:], jnp.bfloat16),
            pltpu.VMEM((layers, EDGE + 2, PAIR, PAIR + 2, blocks + 2 * span, LANES), jnp.bfloat16),
            pltpu.VMEM(borders + (span, LANES), jnp.bfloat16),
            pltpu.VMEM((layers, EDGE + 2, 2, 2, span, LANES), jnp.bfloat16),
            pltpu.VMEM((layers, 2, 3, 2, 2 * LANES, 2 * LANES), jnp.bfloat16),
            pltpu.VMEM((layers, 2, 3, 2, LANES, 2 * LANES), jnp.bfloat16),
            pltpu.VMEM((EDGE, PAIR * blocks, 2 * LANES), jnp.float32),
            pltpu.VMEM((blocks, rows * slots), jnp.bfloat16),
            pltpu.VMEM((Z * slots, strips * blocks), jnp.bfloat16),
            pltpu.VMEM((EDGE, PAIR, strips, blocks, width), jnp.bfloat16),
            pltpu.VMEM((EDGE, PAIR, Z, slots, width), jnp.bfloat16),
            dma((rows,)),
            dma((rows,)),
            dma((EDGE, HALVES, Z)),
            dma((EDGE, HALVES, Z)),
            dma((EDGE, HALVES, Z, strips)),
            dma((EDGE, HALVES, Z, strips)),
            dma(halos),
            dma(halos),
            dma(borders),
            dma(borders),
            dma((EDGE, PAIR, strips)),
            dma((EDGE, PAIR, strips)),
            dma((EDGE, PAIR, Z)),
            dma((EDGE, PAIR, Z)),
            dma((1 + slots // GROUP,)),
        ],
        compiler_params=pltpu.CompilerParams(
            collective_id=0, has_side_effects=True, vmem_limit_bytes=46 << 20
        ),
    )(
        *(
            pltpu.with_memory_space_constraint(operand, pltpu.HBM)
            for operand in (
                slot_count,
                slot_dest.reshape(1, slots),
                slot_tile_block.reshape(1, slots),
                features,
                w_in,
                w_mid,
                frac,
                base,
                w_conv.reshape(weights),
            )
        )
    )


def solution(mesh):
    return jax.shard_map(
        exchange_and_convolve,
        mesh=mesh,
        in_specs=(
            P(None, ("pts", "grid")),
            P(),
            P(),
            P(),
            P(None, ("pts", "grid")),
            P(None, ("pts", "grid")),
            P(("pts", "grid")),
            P(("pts", "grid")),
            P(("pts", "grid")),
        ),
        out_specs=P(None, ("pts", "grid")),
        check_vma=False,
    )
```

```python
import functools

import jax
import jax.numpy as jnp
from jax import lax
from jax.experimental import pallas as pl
from jax.experimental.pallas import tpu as pltpu
from jax.sharding import PartitionSpec as P

GZ = 8
EDGE = 4
TX = 32
TY = 32
LANES = 128
PAIR = 2
Z = GZ // PAIR
GROUP = 16
HALVES = 2
MESH = pl.DeviceIdType.MESH
LEVELS = ((1, 2), (0, 3))
ORDER = (3, 0, 1, 2)
OUT_ORDER = (0, 3, 1, 2)


def silu(total):
    return (total / (1.0 + jnp.exp(-total))).astype(jnp.bfloat16)


def point_layer(weight, inputs):
    return silu(
        lax.dot_general(
            weight, inputs, (((0,), (0,)), ((), ())), preferred_element_type=jnp.float32
        )
    )


def slot_weights(offsets, corners, count):
    width = offsets.shape[1]
    ranks = lax.broadcasted_iota(jnp.int32, (GZ, width), 0)
    live = lax.broadcasted_iota(jnp.int32, (GZ, width), 1) < count

    def axis(position, offset, corner):
        below_part = jnp.where(position == corner, 1.0 - offset, 0.0)
        above_part = jnp.where(position == corner + 1, offset, 0.0)
        return below_part + above_part

    first = ranks < EDGE
    along_xy = axis(
        lax.rem(ranks, EDGE),
        jnp.where(first, offsets[0:1], offsets[1:2]),
        jnp.where(first, corners[0:1], corners[1:2]),
    )
    along_z = jnp.where(live, axis(ranks, offsets[2:3], corners[2:3]), 0.0)
    rows = []
    for parity in range(PAIR):
        for i in range(EDGE):
            for jp in range(EDGE // PAIR):
                j = EDGE + jp * PAIR + parity
                rows.append(along_xy[i : i + 1] * along_xy[j : j + 1] * along_z)
    return jnp.concatenate(rows, axis=0).astype(jnp.bfloat16)


def splat_slots(
    part,
    count_ref,
    features_ref,
    w_in_ref,
    w_mid_ref,
    frac_ref,
    base_ref,
    hidden_ref,
    weight_ref,
    swap_ref,
):
    slots = count_ref.shape[0]
    width = hidden_ref.shape[1] // slots
    half = EDGE * EDGE // PAIR * GZ

    def one(g, carry):
        first = g * GROUP
        points = pl.ds(pl.multiple_of(first * width, GROUP * width), GROUP * width)
        hidden_one = point_layer(w_in_ref[...], features_ref[:, points])
        hidden_two = point_layer(w_mid_ref[...], hidden_one)
        hidden_ref[:, points] = hidden_two
        offsets, corners = frac_ref[:, points], base_ref[:, points]
        for s in range(GROUP):
            part = slice(s * width, (s + 1) * width)
            weights = slot_weights(offsets[:, part], corners[:, part], count_ref[first + s])
            weight_ref[first + s] = weights
            sums = lax.dot_general(
                weights,
                hidden_two[:, part],
                (((1,), (1,)), ((), ())),
                preferred_element_type=jnp.float32,
            )
            rows = pl.ds(pl.multiple_of((first + s) * half, half), half)
            swap_ref[rows] = jnp.concatenate([sums[:half], sums[half:]], axis=1)
        return carry

    steps = slots // (GROUP * HALVES)
    lax.fori_loop(part * steps, (part + 1) * steps, one, 0)


def swap_phase(i, part, swap_ref, sums_ref):
    slots = sums_ref.shape[3]
    half = EDGE * EDGE // PAIR * GZ
    for jp in range(PAIR):
        for z in range(GZ):
            row = (i * PAIR + jp) * GZ + z
            low = (jp * PAIR + z % PAIR) * LANES
            sums_ref[z // PAIR, i, part, :, low : low + LANES] = swap_ref[
                pl.ds(part * slots * half + row, slots, stride=half)
            ].astype(jnp.bfloat16)


def unswap_piece(i, jp, cells_ref, swap_ref):
    slots = cells_ref.shape[3]
    for z in range(GZ):
        row = (i * PAIR + jp) * GZ + z
        low = z % PAIR * LANES
        swap_ref[row * slots : (row + 1) * slots] = cells_ref[
            z // PAIR, i, jp, :, low : low + LANES
        ].astype(jnp.float32)


def interpolate_slot(s, slots, swap_ref, weight_ref, hidden_ref):
    width = hidden_ref.shape[1] // slots
    channels = hidden_ref.shape[0]
    half = EDGE * EDGE // PAIR * GZ
    points = slice(s * width, (s + 1) * width)
    cells = swap_ref[pl.ds(s, half, stride=slots)].T
    cells = jnp.concatenate([cells[:channels], cells[channels:]], axis=1).astype(jnp.bfloat16)
    interp = jnp.dot(cells, weight_ref[s], preferred_element_type=jnp.float32).astype(jnp.bfloat16)
    hidden_ref[:, points] = (
        hidden_ref[:, points].astype(jnp.float32) + interp.astype(jnp.float32)
    ).astype(jnp.bfloat16)


def build_band(w_ref, band_ref, side_ref):
    channels = w_ref.shape[1]
    width = PAIR * channels

    def one(n, carry):
        layer, a = lax.div(n, 3), lax.rem(n, 3)
        band_ref[layer, :, a] = jnp.zeros(band_ref.shape[1:2] + band_ref.shape[3:], band_ref.dtype)
        side_ref[layer, :, a] = jnp.zeros(side_ref.shape[1:2] + side_ref.shape[3:], side_ref.dtype)
        for part, levels in enumerate(LEVELS):
            for slot, zl in enumerate(levels):
                for zz in range(PAIR):
                    e = zl - zz
                    if not 0 <= e <= 2:
                        continue
                    for source, row in ((0, 0), (1, 1), (2, 2), (-1, 3)):
                        for target in range(PAIR):
                            b = source - target + 1
                            if not 0 <= b <= 2:
                                continue
                            rows = slice(row * channels, (row + 1) * channels)
                            lanes = zz * width + target * channels
                            lanes = slice(lanes, lanes + channels)
                            block = w_ref[n * 9 + b * 3 + e]
                            band_ref[layer, part, a, slot, rows, lanes] = block
                            if source in (-1, 2):
                                rows = slice(slot * channels, (slot + 1) * channels)
                                side_ref[layer, max(source, 0) // 2, a, part, rows, lanes] = block
        return carry

    lax.fori_loop(0, band_ref.shape[0] * 3, one, 0)


def conv_kernel(
    sizes,
    count_ref,
    dest_ref,
    block_ref,
    features_ref,
    w_in_ref,
    w_mid_ref,
    frac_ref,
    base_ref,
    w_hbm,
    out_hbm,
    w_ref,
    hidden_ref,
    weight_ref,
    swap_ref,
    out_ref,
    sums_ref,
    own_ids,
    ids,
    arrived,
    field,
    edge_out,
    edge_in,
    band_ref,
    side_ref,
    totals,
    sum_picks,
    out_picks,
    dense,
    values,
    id_send,
    id_recv,
    z_send,
    z_recv,
    x_send,
    x_recv,
    halo_send,
    halo_recv,
    edge_send,
    edge_recv,
    rx_send,
    rx_recv,
    rz_send,
    rz_recv,
    local_sem,
):
    rows, columns = sizes
    strips = rows // Z
    blocks = dense.shape[3]
    slots = values.shape[3]
    share = sums_ref.shape[3]
    span = (field.shape[4] - blocks) // 2
    layers = field.shape[0]
    me_row, me_column = lax.axis_index("grid"), lax.axis_index("pts")
    me_z, me_x = lax.div(me_row, strips), lax.rem(me_row, strips)
    inner = pl.ds(span, blocks)

    def snake(column, x):
        return x + lax.rem(column, 2) * (strips - 1 - 2 * x)

    me_strip = snake(me_column, me_x)

    def beside(ds):
        strip = me_column * strips + me_strip + ds
        present = (strip >= 0) & (strip < columns * strips)
        column = lax.div(strip + strips, strips) - 1
        x = snake(column + 2, lax.rem(strip + strips, strips))
        return present, column, me_z * strips + x

    def above(dz):
        return (me_z + dz >= 0) & (me_z + dz < Z)

    def tell(t):
        return pltpu.make_async_remote_copy(
            src_ref=own_ids,
            dst_ref=ids.at[me_row],
            send_sem=id_send.at[t],
            recv_sem=id_recv.at[t],
            device_id=(me_column, lax.rem(me_row + t, rows)),
            device_id_type=MESH,
        )

    def along_z(i, h, t):
        z = lax.rem(me_z + t, Z)
        return pltpu.make_async_remote_copy(
            src_ref=sums_ref.at[z, i, h],
            dst_ref=arrived.at[i, h, me_row],
            send_sem=z_send.at[i, h, t],
            recv_sem=z_recv.at[i, h, t],
            device_id=(me_column, z * strips + me_x),
            device_id_type=MESH,
        )

    def along_x(i, h, t, u):
        origin = lax.rem(me_z - t + Z, Z) * strips + me_x
        return pltpu.make_async_remote_copy(
            src_ref=sums_ref.at[me_z, i, h] if t == 0 else arrived.at[i, h, origin],
            dst_ref=arrived.at[i, h, origin],
            send_sem=x_send.at[i, h, t, u],
            recv_sem=x_recv.at[i, h, t, u],
            device_id=(me_column, me_z * strips + lax.rem(me_x + u, strips)),
            device_id_type=MESH,
        )

    def halo(layer, i, k):
        dz = (1, -1)[k]
        return pltpu.make_async_remote_copy(
            src_ref=field.at[layer, i + 1, :, 2 - k, inner],
            dst_ref=field.at[layer, i + 1, :, 3 * k, inner],
            send_sem=halo_send.at[layer, i, k],
            recv_sem=halo_recv.at[layer, i, k],
            device_id=(me_column, (me_z + dz) * strips + me_x),
            device_id_type=MESH,
        )

    def border(layer, i, part, side):
        _, column, row = beside((1, -1)[side])
        return pltpu.make_async_remote_copy(
            src_ref=edge_out.at[layer, i, side, part],
            dst_ref=edge_in.at[layer, i + 1, side, part],
            send_sem=edge_send.at[layer, i, part, side],
            recv_sem=edge_recv.at[layer, i, part, side],
            device_id=(column, row),
            device_id_type=MESH,
        )

    def back_x(i, jp, u):
        return pltpu.make_async_remote_copy(
            src_ref=dense.at[i, jp, me_strip],
            dst_ref=dense.at[i, jp, me_strip],
            send_sem=rx_send.at[i, jp, u],
            recv_sem=rx_recv.at[i, jp, u],
            device_id=(me_column, me_z * strips + lax.rem(me_x + u, strips)),
            device_id_type=MESH,
        )

    def back_z(i, jp, t):
        z = lax.rem(me_z + t, Z)
        return pltpu.make_async_remote_copy(
            src_ref=values.at[i, jp, z],
            dst_ref=out_ref.at[me_z, i, jp],
            send_sem=rz_send.at[i, jp, t],
            recv_sem=rz_recv.at[i, jp, t],
            device_id=(me_column, z * strips + me_x),
            device_id_type=MESH,
        )

    low_half = lax.broadcasted_iota(jnp.int32, (blocks, LANES), 1) < LANES // PAIR

    def send_border(layer, i, part):
        first, second = LEVELS[part]
        for side in range(2):
            rows = slice(blocks, blocks + span) if side == 0 else slice(span, 2 * span)
            view = field.at[layer, i + 1, 1 - side]
            tiles = [view[first, rows], view[second, rows]]
            tiles[side] = pltpu.roll(tiles[side].astype(jnp.float32), LANES // PAIR, 1).astype(
                jnp.bfloat16
            )
            edge_out[layer, i, side, part] = jnp.where(low_half[:span], tiles[0], tiles[1])

            @pl.when(beside((1, -1)[side])[0])
            def _():
                border(layer, i, part, side).start()

    def wait_border(layer, i):
        for side in range(2):

            @pl.when(beside((-1, 1)[side])[0])
            def _():
                for part in range(2):
                    border(layer, i, part, side).wait_recv()

    barrier = pltpu.get_barrier_semaphore()
    for t in range(1, rows):
        pl.semaphore_signal(
            barrier,
            inc=1,
            device_id=(me_column, lax.rem(me_row + t, rows)),
            device_id_type=MESH,
        )
    expected = rows - 1
    for ds in (-1, 1):
        present, column, row = beside(ds)
        other = present & (column != me_column)
        expected = expected + other.astype(jnp.int32)

        @pl.when(other)
        def _():
            pl.semaphore_signal(barrier, inc=1, device_id=(column, row), device_id_type=MESH)

    load = pltpu.make_async_copy(w_hbm, w_ref, local_sem.at[0])
    load.start()
    block = block_ref[...]
    along, across = TX // EDGE, TY // EDGE
    number = lax.rem(block, across) * span + dest_ref[...] * along + lax.div(block, across)
    own_ids[...] = jnp.broadcast_to(number, own_ids.shape)
    ids[me_row] = own_ids[...]
    for h in range(HALVES):
        splat_slots(
            h,
            count_ref,
            features_ref,
            w_in_ref,
            w_mid_ref,
            frac_ref,
            base_ref,
            hidden_ref,
            weight_ref,
            swap_ref,
        )
        if h == 0:
            for i in ORDER:
                swap_phase(i, h, swap_ref, sums_ref)
            pl.semaphore_wait(barrier, expected)
            for t in range(1, rows):
                tell(t).start()
        for i in ORDER:
            if h > 0:
                swap_phase(i, h, swap_ref, sums_ref)
            for t in (2, 1, 3):
                along_z(i, h, t).start()
            for u in range(1, strips):
                along_x(i, h, 0, u).start()
            arrived[i, h, me_row] = sums_ref[me_z, i, h]
    for k in range(2):

        @pl.when(jnp.logical_not(above((-1, 1)[k])))
        def _():
            view = field.at[:, 1 : EDGE + 1, :, 3 * k, inner]
            view[...] = jnp.zeros(view.shape, field.dtype)

        @pl.when(jnp.logical_not(beside((-1, 1)[k])[0]))
        def _():
            view = edge_in.at[:, 1 : EDGE + 1, k]
            view[...] = jnp.zeros(view.shape, edge_in.dtype)

    for jp, rows_out in ((0, slice(span + blocks, 2 * span + blocks)), (1, slice(0, span))):
        view = field.at[:, :, jp, :, rows_out]
        view[...] = jnp.zeros(view.shape, field.dtype)
    def picks(r, first, size):
        named = jnp.broadcast_to(ids[r, 0:1, :slots], (size, slots))
        place_of = lax.broadcasted_iota(jnp.int32, (size, slots), 0) + first
        return jnp.where(named == place_of, 1.0, 0.0)

    def build_picks():
        for t in range(1, rows):
            tell(t).wait_recv()
        for r in range(rows):
            one_hot = picks(r, me_strip * blocks, blocks).astype(jnp.bfloat16)
            for h in range(HALVES):
                low = (h * rows + r) * share
                sum_picks[:, low : low + share] = one_hot[:, h * share : (h + 1) * share]
        for z in range(Z):
            out_picks[z * slots : (z + 1) * slots] = picks(
                z * strips + me_x, 0, strips * blocks
            ).T.astype(jnp.bfloat16)

    def forward(i, h):
        for t in (2, 1, 3):
            along_z(i, h, t).wait_recv()
            for u in range(1, strips):
                along_x(i, h, t, u).start()

    def spread(layer, i, tiles):
        for jp in range(PAIR):
            for zz in range(PAIR):
                field[layer, i + 1, jp, 1 + zz, inner] = tiles(jp, zz)
        for k in range(2):

            @pl.when(above((1, -1)[k]))
            def _():
                halo(layer, i, k).start()

        send_border(layer, i, 0)

    def gather(i):
        for h in range(HALVES):
            for t in range(Z):
                for u in range(1, strips):
                    along_x(i, h, t, u).wait_recv()
        summed = jnp.dot(
            sum_picks[...],
            arrived[i].reshape(rows * slots, arrived.shape[4]),
            preferred_element_type=jnp.float32,
        ).astype(jnp.bfloat16)

        def tiles(jp, zz):
            low = (jp * PAIR + zz) * LANES
            return summed[:, low : low + LANES]

        spread(0, i, tiles)

    def shifted(tile, down):
        size = tile.shape[0]
        ranks = lax.broadcasted_iota(jnp.int32, tile.shape, 0)
        keep = lax.rem(ranks, span) != (0 if down else span - 1)
        moved = pltpu.roll(tile.astype(jnp.float32), 1 if down else size - 1, 0)
        return jnp.where(keep, moved, 0.0).astype(jnp.bfloat16)

    def shift(layer, i, levels):
        for down, phase, target in ((True, EDGE - 1, 0), (False, 0, EDGE + 1)):
            if phase == i:
                for jp in range(PAIR):
                    for zl in levels:
                        view = field.at[layer, :, jp, zl]
                        view[target, inner] = shifted(view[i + 1, inner], down)

    def shift_edges(layer, i):
        for down, phase, target in ((True, EDGE - 1, 0), (False, 0, EDGE + 1)):
            if phase == i:
                for side in range(2):
                    for part in range(2):
                        view = edge_in.at[layer, :, side, part]
                        view[target] = shifted(view[i + 1], down)

    def windows(layer, i, jp, levels, taps):
        parts = []
        for a in taps:
            for zl in levels:
                here = field.at[layer, i + a, :, zl]
                parts.append(here[jp, inner])
                if jp == 0:
                    up, down = here[1, inner], here[1, 0:blocks]
                else:
                    up, down = here[0, 2 * span : 2 * span + blocks], here[0, inner]
                parts.append(jnp.where(low_half, up, down))
        return jnp.concatenate(parts, axis=1)

    def conv_terms(layer, i, part, taps):
        depth = band_ref.shape[5]
        weight = jnp.concatenate(
            [band_ref[layer, part, a].reshape(-1, depth) for a in taps], axis=0
        )
        lhs = jnp.concatenate(
            [windows(layer, i, jp, LEVELS[part], taps) for jp in range(PAIR)], axis=0
        )
        return jnp.dot(lhs, weight, preferred_element_type=jnp.float32)

    def own_terms(layer, i):
        totals[i] = conv_terms(layer, i, 0, range(3))

    def edge_terms(layer, i):
        for side in range(2):
            lhs = jnp.concatenate(
                [edge_in[layer, i + a, side, part] for a in range(3) for part in range(2)], axis=1
            )
            weight = side_ref[layer, side].reshape(-1, side_ref.shape[5])
            rows_in = slice(0, span) if side == 0 else slice(2 * blocks - span, 2 * blocks)
            totals[i, rows_in] += jnp.dot(lhs, weight, preferred_element_type=jnp.float32)

    def finish(layer, i):
        total = totals[i]
        activated = silu(total)

        def tiles(jp, zz):
            return activated[jp * blocks : (jp + 1) * blocks, zz * LANES : (zz + 1) * LANES]

        if layer < layers - 1:
            spread(layer + 1, i, tiles)
            shift(layer + 1, i, LEVELS[0])
        else:
            for jp in range(PAIR):
                dense[i, jp, me_strip] = activated[jp * blocks : (jp + 1) * blocks]
                for u in range(1, strips):
                    back_x(i, jp, u).start()

    def near(i):
        return ((i - 1) % EDGE, i, (i + 1) % EDGE)

    for h in range(HALVES):
        for n, i in enumerate(ORDER):
            forward(i, h)
            if h == 0 and n == 0:
                build_picks()
            if h == 0 and n == 1:
                load.wait()
                build_band(w_ref, band_ref, side_ref)
            if h == HALVES - 1 and n > 0:
                gather(ORDER[n - 1])
                shift(0, ORDER[n - 1], LEVELS[0])
    for i in OUT_ORDER:
        if ORDER[-1] not in near(i):
            own_terms(0, i)
    gather(ORDER[-1])
    shift(0, ORDER[-1], LEVELS[0])
    for i in OUT_ORDER:
        if ORDER[-1] in near(i):
            own_terms(0, i)

    for layer in range(layers):
        before = ORDER if layer == 0 else OUT_ORDER
        if layer > 0:
            for i in OUT_ORDER:
                own_terms(layer, i)
        bordered = []

        def reach(phase):
            for k in range(2):

                @pl.when(above((-1, 1)[k]))
                def _():
                    halo(layer, phase, k).wait_recv()

            send_border(layer, phase, 1)
            shift(layer, phase, LEVELS[1])

        def add_terms(i, phases):
            taps = [a for a in range(3) if near(i)[a] in phases]
            totals[i] += conv_terms(layer, i, 1, taps)

        def close(i):
            for phase in before:
                if phase in near(i) and phase not in bordered:
                    wait_border(layer, phase)
                    shift_edges(layer, phase)
                    bordered.append(phase)
            edge_terms(layer, i)
            finish(layer, i)

        reached = []
        for n, i in enumerate(OUT_ORDER):
            for phase in before:
                if phase in near(i) and phase not in reached:
                    reach(phase)
                    reached.append(phase)
            add_terms(i, before)
            if n > 0:
                close(OUT_ORDER[n - 1])
        close(OUT_ORDER[-1])

    for i in OUT_ORDER:
        for jp in range(PAIR):
            for u in range(1, strips):
                back_x(i, jp, u).wait_recv()
            picked = jnp.dot(
                out_picks[...],
                dense[i, jp].reshape(strips * blocks, dense.shape[4]),
                preferred_element_type=jnp.float32,
            ).astype(jnp.bfloat16)
            values[i, jp] = picked.reshape(values.shape[2:])
            for t in (2, 1, 3):
                back_z(i, jp, t).start()
            out_ref[me_z, i, jp] = values[i, jp, me_z]

    for i in OUT_ORDER:
        for jp in range(PAIR):
            for t in (1, 2, 3):
                back_z(i, jp, t).wait_recv()
            unswap_piece(i, jp, out_ref, swap_ref)

    def keep(g):
        width = hidden_ref.shape[1] * GROUP // slots
        points = slice(g * width, (g + 1) * width)
        return pltpu.make_async_copy(
            hidden_ref.at[:, points], out_hbm.at[:, points], local_sem.at[1 + g]
        )

    for g in range(slots // GROUP):
        for s in range(g * GROUP, (g + 1) * GROUP):
            interpolate_slot(s, slots, swap_ref, weight_ref, hidden_ref)
        keep(g).start()
    for g in range(slots // GROUP):
        keep(g).wait()
    for t in range(1, rows):
        tell(t).wait_send()
    for i in range(EDGE):
        for jp in range(PAIR):
            for t in (1, 2, 3):
                back_z(i, jp, t).wait_send()
            for u in range(1, strips):
                back_x(i, jp, u).wait_send()
        for h in range(HALVES):
            for t in (1, 2, 3):
                along_z(i, h, t).wait_send()
            for u in range(1, strips):
                for t in range(Z):
                    along_x(i, h, t, u).wait_send()
        for layer in range(layers):
            for k in range(2):

                @pl.when(above((1, -1)[k]))
                def _():
                    halo(layer, i, k).wait_send()

                @pl.when(beside((1, -1)[k])[0])
                def _():
                    for part in range(2):
                        border(layer, i, part, k).wait_send()


def exchange_and_convolve(
    features, w_in, w_mid, w_conv, frac, base, slot_dest, slot_tile_block, slot_count
):
    rows, columns = lax.axis_size("grid"), lax.axis_size("pts")
    strips = rows // Z
    slots = slot_count.shape[0]
    layers, channels = w_conv.shape[0], w_conv.shape[4]
    width = PAIR * PAIR * channels
    span = rows * (TX // EDGE)
    blocks = span * (TY // EDGE) // strips
    half = EDGE * EDGE // PAIR * GZ
    hidden = (channels, features.shape[1])
    cells = (Z, EDGE, PAIR, slots, width)
    weights = (layers * 27, channels, channels)
    share = (HALVES, slots // HALVES, PAIR * width)
    halos = (layers, EDGE, 2)
    borders = halos + (2,)
    dma = pltpu.SemaphoreType.DMA
    vmem = pl.BlockSpec(memory_space=pltpu.VMEM)
    return pl.pallas_call(
        functools.partial(conv_kernel, (rows, columns)),
        out_shape=jax.ShapeDtypeStruct(hidden, jnp.bfloat16),
        in_specs=[pl.BlockSpec(memory_space=pltpu.SMEM)]
        + [vmem] * 7
        + [pl.BlockSpec(memory_space=pl.ANY)],
        out_specs=pl.BlockSpec(memory_space=pl.ANY),
        scratch_shapes=[
            pltpu.VMEM(weights, jnp.bfloat16),
            pltpu.VMEM(hidden, jnp.bfloat16),
            pltpu.VMEM((slots, PAIR * half, hidden[1] // slots), jnp.bfloat16),
            pltpu.VMEM((slots * half, LANES), jnp.float32),
            pltpu.VMEM(cells, jnp.bfloat16),
            pltpu.VMEM((Z, EDGE) + share, jnp.bfloat16),
            pltpu.VMEM((8, slots), jnp.int32),
            pltpu.VMEM((rows, 8, slots), jnp.int32),
            pltpu.VMEM((EDGE, HALVES, rows) + share[1:], jnp.bfloat16),
            pltpu.VMEM((layers, EDGE + 2, PAIR, PAIR + 2, blocks + 2 * span, LANES), jnp.bfloat16),
            pltpu.VMEM(borders + (span, LANES), jnp.bfloat16),
            pltpu.VMEM((layers, EDGE + 2, 2, 2, span, LANES), jnp.bfloat16),
            pltpu.VMEM((layers, 2, 3, 2, 2 * LANES, 2 * LANES), jnp.bfloat16),
            pltpu.VMEM((layers, 2, 3, 2, LANES, 2 * LANES), jnp.bfloat16),
            pltpu.VMEM((EDGE, PAIR * blocks, 2 * LANES), jnp.float32),
            pltpu.VMEM((blocks, rows * slots), jnp.bfloat16),
            pltpu.VMEM((Z * slots, strips * blocks), jnp.bfloat16),
            pltpu.VMEM((EDGE, PAIR, strips, blocks, width), jnp.bfloat16),
            pltpu.VMEM((EDGE, PAIR, Z, slots, width), jnp.bfloat16),
            dma((rows,)),
            dma((rows,)),
            dma((EDGE, HALVES, Z)),
            dma((EDGE, HALVES, Z)),
            dma((EDGE, HALVES, Z, strips)),
            dma((EDGE, HALVES, Z, strips)),
            dma(halos),
            dma(halos),
            dma(borders),
            dma(borders),
            dma((EDGE, PAIR, strips)),
            dma((EDGE, PAIR, strips)),
            dma((EDGE, PAIR, Z)),
            dma((EDGE, PAIR, Z)),
            dma((1 + slots // GROUP,)),
        ],
        compiler_params=pltpu.CompilerParams(
            collective_id=0, has_side_effects=True, vmem_limit_bytes=46 << 20
        ),
    )(
        *(
            pltpu.with_memory_space_constraint(operand, pltpu.HBM)
            for operand in (
                slot_count,
                slot_dest.reshape(1, slots),
                slot_tile_block.reshape(1, slots),
                features,
                w_in,
                w_mid,
                frac,
                base,
                w_conv.reshape(weights),
            )
        )
    )


def solution(mesh):
    return jax.shard_map(
        exchange_and_convolve,
        mesh=mesh,
        in_specs=(
            P(None, ("pts", "grid")),
            P(),
            P(),
            P(),
            P(None, ("pts", "grid")),
            P(None, ("pts", "grid")),
            P(("pts", "grid")),
            P(("pts", "grid")),
            P(("pts", "grid")),
        ),
        out_specs=P(None, ("pts", "grid")),
        check_vma=False,
    )
```
